32 devices in a mesh: row: 4 (over y, core), col: 8 (over z, x).
Axes of the slice: x: 2, y: 2, z: 4, core: 2. Of those that a mesh axis runs over, the one named last changes fastest.
Arguments:
- state: bfloat16 [128, 768, 128], P('row', 'col'), may hold values from -0.94921875 to 0.94921875
- grad: bfloat16 [128, 768, 128], P('row', 'col'), may hold values from -6 to 6
- kernel: bfloat16 [3, 3, 128, 128], replicated, may hold values from -0.1875 to 0.1875
- ray_matrix: bfloat16 [8, 4, 64, 1024], replicated, may hold values from -0.1875 to 0.1875
- ray_weight: float32 [256, 64, 128], P(('row', 'col')), may hold values from 0.2 to 2
- hits: int32 [4, 24, 16], replicated, may hold values from 0 to 255, as said below
- offsets: int32 [4, 24, 16], P('row', 'col'), may hold values from 0 to 3
- block_slot: int32 [256], replicated, may hold values from 0 to 255, as said below
- angle_count: int32 [8], replicated, may hold values from 16 to 32
Outputs:
- adjoint: float32 [128, 768, 128], P('row', 'col')
The draws below stay inside these ranges and needn't reach their ends.
Inputs may be any that keep to these rules, and one draw needn't show every extreme that they name: `hits`: of the listed pairs of the tiles of one device, at most 3 name blocks whose owner slots lie in one device's range [d * 8, (d + 1) * 8), and exactly 3 do so for some owner d of each device. Devices are numbered row * 8 + col, in the order of the mesh, row first. `block_slot`: A permutation of the ray blocks' slots.
All inputs are finite; a program needn't handle non-finite values.
Results may differ from the reference program's by a relative error of at most 0.0049.
Values may be sent and summed in bfloat16 or wider, within the bound.
No kernel may reach another device: no remote copies, remote signals or barrier semaphores. Data moves between devices by JAX's collectives and lax.ppermute only.
A program may use at most 128 MiB of HBM per device.

```python
import math
import jax
import jax.numpy as jnp
from jax import lax

PIX = 32
C = 128
BINS = 64
TPIX = 1024
ANGLES = 8
OFFSETS = 4
HITS = 16
ITERS = 2
TR = 1
TC = 3
BLK_DEV = 8
TILE_ROWS = 4
TILE_COLS = 24
NR = 128
NC = 768
BLOCKS = 256
BLK_ANG = 32
CAP = 3
N_ROW = 4
N_COL = 8
DEVICES = 32


def make_routes(key):
    base = jax.random.fold_in(key, 7)
    key_perm, key_count, key_dest, key_local, key_shuffle = jax.random.split(base, 5)
    slots = jax.random.permutation(key_perm, BLOCKS).astype(jnp.int32)
    inverse = jnp.zeros((BLOCKS,), jnp.int32).at[slots].set(jnp.arange(BLOCKS, dtype=jnp.int32))
    pairs = TR * TC * HITS
    counts = jax.random.randint(key_count, (DEVICES, DEVICES), CAP - 1, CAP + 1)
    counts = counts.at[:, 0].set(CAP)
    ends = jnp.cumsum(counts, axis=1)
    positions = jnp.arange(pairs, dtype=jnp.int32)
    ranking = jnp.sum((ends[:, None, :] <= positions[None, :, None]).astype(jnp.int32), axis=2)
    orders = jax.vmap(lambda sub: jax.random.permutation(sub, DEVICES))(jax.random.split(key_dest, DEVICES))
    target = jnp.take_along_axis(orders.astype(jnp.int32), ranking, axis=1)
    local_slot = jax.random.randint(key_local, (DEVICES, pairs), 0, BLK_DEV)
    shuffle = jax.vmap(lambda sub: jax.random.permutation(sub, pairs))(jax.random.split(key_shuffle, DEVICES))
    target = jnp.take_along_axis(target, shuffle.astype(jnp.int32), axis=1)
    local_slot = jnp.take_along_axis(local_slot, shuffle.astype(jnp.int32), axis=1)
    block_ids = inverse[target * BLK_DEV + local_slot]
    shaped = block_ids.reshape(N_ROW, N_COL, TR, TC, HITS).transpose(0, 2, 1, 3, 4)
    return (slots, shaped.reshape(TR * N_ROW, TC * N_COL, HITS).astype(jnp.int32))


def draw_hits(key, part):
    return make_routes(key)[1]


def draw_block_slot(key, part):
    return make_routes(key)[0]


def place_ends(array, rng, least, high):
    longest = array.shape.index(max(array.shape))
    spots = []
    for shift in (0, 1):
        where = [jax.random.randint(jax.random.fold_in(rng, axis), (), 0, length) for axis, length in enumerate(array.shape)]
        where[longest] = (where[longest] + shift) % array.shape[longest]
        spots.append(tuple(where))
    return array.at[spots[0]].set(least).at[spots[1]].set(high)


def steps_of(stream_key, shape, cuts, low, high):
    gain, own = 1.0, jax.random.fold_in(stream_key, 6)
    for dim, parts in cuts:
        steps = jnp.exp(jax.random.uniform(jax.random.fold_in(own, dim), (parts,), jnp.float32, low / len(cuts), high / len(cuts)))
        gain = gain * jnp.repeat(steps, shape[dim] // parts).reshape([-1 if axis == dim else 1 for axis in range(len(shape))])
    return gain


def noise(stream_key, dims, width, limit, cuts=(), kind=jnp.bfloat16):
    drawn = jax.random.normal(stream_key, dims, jnp.float32) * width
    if len(cuts) > 0:
        drawn = steps_of(stream_key, dims, cuts, -0.22, 0.18) * drawn
    return jnp.clip(drawn, min=-limit, max=limit).astype(kind)


def setup_inputs(seed: int = 0) -> dict:
    arg_keys = jax.random.split(jax.random.key(seed), 10)
    state = jnp.clip(jax.random.uniform(arg_keys[0], (NR, NC, C), jnp.float32, -0.94921875, 0.94921875) * steps_of(arg_keys[0], (NR, NC, C), ((0, 4), (1, 8)), -0.4, 0.0), -0.94921875, 0.94921875).astype(jnp.bfloat16)
    grad = noise(arg_keys[1], (NR, NC, C), 1.0, 6.0, ((0, 4), (1, 8)))
    kernel = noise(arg_keys[2], (3, 3, C, C), (9 * C) ** -0.5, 0.1875)
    ray_matrix = noise(arg_keys[3], (ANGLES, OFFSETS, BINS, TPIX), TPIX ** -0.5, 0.1875)
    ray_weight = jnp.clip(jnp.exp(math.log(2.0) - 2.3025851 * jax.random.uniform(arg_keys[4], (BLOCKS, BINS, C), jnp.float32) ** steps_of(arg_keys[4], (BLOCKS, BINS, C), ((0, 32),), -0.2, 0.2)), 0.2, 2.0)
    hits = draw_hits(jax.random.fold_in(arg_keys[9], 71), 0)
    offsets = place_ends(jax.random.randint(arg_keys[6], (TILE_ROWS, TILE_COLS, HITS), 0, OFFSETS), jax.random.fold_in(arg_keys[6], 1), 0, OFFSETS - 1).astype(jnp.int32)
    block_slot = draw_block_slot(jax.random.fold_in(arg_keys[9], 71), 0)
    angle_count = place_ends(jax.random.randint(arg_keys[8], (ANGLES,), BLK_ANG // 2, BLK_ANG + 1), jax.random.fold_in(arg_keys[8], 1), BLK_ANG // 2, BLK_ANG).astype(jnp.int32)
    return {"state": state, "grad": grad, "kernel": kernel, "ray_matrix": ray_matrix, "ray_weight": ray_weight, "hits": hits, "offsets": offsets, "block_slot": block_slot, "angle_count": angle_count}


relax_rate = 0.25


def to_tiles(image):
    shaped = image.reshape(TILE_ROWS, PIX, TILE_COLS, PIX, C)
    return shaped.transpose(0, 2, 1, 3, 4).reshape(TILE_ROWS, TILE_COLS, PIX * PIX, C)


def from_tiles(tiles):
    shaped = tiles.reshape(TILE_ROWS, TILE_COLS, PIX, PIX, C)
    return shaped.transpose(0, 2, 1, 3, 4).reshape(NR, NC, C)


def conv_pull(scaled, kernel):
    padded = jnp.pad(scaled, ((1, 1), (1, 1), (0, 0)))
    total = jnp.zeros((NR * NC, C), jnp.float32)
    for shift_row in range(3):
        for shift_col in range(3):
            window = padded[2 - shift_row:2 - shift_row + NR, 2 - shift_col:2 - shift_col + NC]
            total = total + jnp.dot(window.reshape(NR * NC, C), kernel[shift_row, shift_col].T,
                                    preferred_element_type=jnp.float32)
    return total.reshape(NR, NC, C)


def reference(state, grad, kernel, ray_matrix, ray_weight, hits, offsets, block_slot, angle_count):
    block_ids = jnp.arange(BLOCKS, dtype=jnp.int32)
    inuse = ((block_ids % BLK_ANG) < angle_count[block_ids // BLK_ANG]).astype(jnp.float32)
    scaling = inuse[:, None, None] * ray_weight[block_slot]
    derivative = 1.0 - jnp.square(state.astype(jnp.float32))
    cotangent = grad.astype(jnp.float32)
    adjoint = cotangent

    def matrices_of(hit_row, offset_row):
        chosen = ray_matrix[hit_row // BLK_ANG, offset_row]
        return chosen.reshape(TILE_COLS, HITS * BINS, PIX * PIX).astype(jnp.float32)

    for turn in range(ITERS):
        scaled = (derivative * adjoint).astype(jnp.bfloat16)
        pulled = conv_pull(scaled, kernel)
        pulled_tiles = to_tiles(pulled.astype(jnp.bfloat16))

        def project_row(inputs):
            tile_row, hit_row, offset_row = inputs
            chosen = matrices_of(hit_row, offset_row)
            result = jnp.einsum('tkp,tpc->tkc', chosen, tile_row.astype(jnp.float32))
            return result.reshape(TILE_COLS, HITS, BINS, C)

        partial_value = lax.map(project_row, (pulled_tiles, hits, offsets))
        sinogram = jax.ops.segment_sum(partial_value.reshape(-1, BINS, C), hits.reshape(-1), num_segments=BLOCKS)
        weighted = (scaling * sinogram).astype(jnp.bfloat16)

        def back_row(inputs):
            hit_row, offset_row = inputs
            chosen = matrices_of(hit_row, offset_row)
            picked = weighted[hit_row].reshape(TILE_COLS, HITS * BINS, C).astype(jnp.float32)
            return jnp.einsum('tkp,tkc->tpc', chosen, picked)

        backed = from_tiles(lax.map(back_row, (hits, offsets)))
        adjoint = cotangent + (pulled - relax_rate * backed)
    return adjoint
```

```python
import functools

import jax
import jax.numpy as jnp
from jax import lax
from jax.experimental import pallas as pl
from jax.experimental.pallas import tpu as pltpu
from jax.sharding import Mesh, PartitionSpec as P

PIX = 32
ANGLES = 8
HITS = 16
ITERS = 2
RING = 4

relax_rate = 0.25

COL = ("zh", "zl", "x")
GROUP = ("row", "zl", "x")


def fetch_matrices(mat_idx, ray_ref, held, sems, pairs):
    def body(q, carry):
        pltpu.make_async_copy(ray_ref.at[mat_idx[q]], held.at[q], sems.at[q]).start()
        return carry

    lax.fori_loop(0, pairs, body, 0)


def await_matrices(mat_idx, ray_ref, held, sems, first, count):
    for k in range(count):
        q = first + k
        pltpu.make_async_copy(ray_ref.at[mat_idx[q]], held.at[q], sems.at[q]).wait()


def project_kernel(
    mat_idx, send_slot, scaled, above, below, left, right, taps, ray_ref,
    pulled_out, out, held, sems, wide, cols3, *, tiles, hits, tile_cols,
):
    t = pl.program_id(0)
    rows, cols, chans = scaled.shape
    bins, tile_pix = held.shape[1:]

    @pl.when(t == 0)
    def _():
        fetch_matrices(mat_idx, ray_ref, held, sems, tiles * hits)
        f32 = jnp.float32
        wide[0, 8 : 8 + cols, :] = above[...].astype(f32)
        wide[rows + 1, 8 : 8 + cols, :] = below[...].astype(f32)
        wide[1 : rows + 1, 8 : 8 + cols, :] = scaled[...].astype(f32)
        lefts = left[...].astype(f32)
        rights = right[...].astype(f32)
        for r in range(rows + 2):
            wide[r, 7:8, :] = lefts[r : r + 1, :]
            wide[r, 8 + cols : 9 + cols, :] = rights[r : r + 1, :]
        for dc in range(3):
            cols3[:, :, dc * chans : (dc + 1) * chans] = wide[:, 7 + dc : 7 + dc + cols, :].astype(
                jnp.bfloat16
            )
        out[...] = jnp.zeros_like(out)

    r0 = (t // tile_cols) * PIX
    c0 = pl.multiple_of((t % tile_cols) * PIX, PIX)
    acc = None
    for dr in range(3):
        window = cols3[pl.ds(r0 + dr, PIX), pl.ds(c0, PIX), :].reshape(tile_pix, 3 * chans)
        term = jnp.dot(window, taps[dr], preferred_element_type=jnp.float32)
        acc = term if acc is None else acc + term
    pulled_out[0] = acc
    low = acc.astype(jnp.bfloat16)
    first = t * hits
    await_matrices(mat_idx, ray_ref, held, sems, first, hits)
    matrix = held[pl.ds(first, hits)].reshape(hits * bins, tile_pix)
    part = jnp.dot(matrix, low, preferred_element_type=jnp.float32).astype(jnp.bfloat16)
    for k in range(hits):
        out[send_slot[first + k]] = part[k * bins : (k + 1) * bins, :]


def combine_kernel(table, recv, total, low, acc):
    acc[...] = jnp.zeros_like(acc)

    def body(j, carry):
        acc[table[j]] += recv[j].astype(jnp.float32)
        return carry

    lax.fori_loop(0, recv.shape[0], body, 0, unroll=8)
    total[...] = acc[: total.shape[0]]
    low[...] = acc[: total.shape[0]].astype(jnp.bfloat16)


def reply_kernel(table, total, other, scaling, out, held):
    n = total.shape[0]
    held[:n] = (scaling[...] * (total[...] + other[...].astype(jnp.float32))).astype(jnp.bfloat16)
    held[n] = jnp.zeros(held.shape[1:], jnp.bfloat16)

    def body(j, carry):
        out[j] = held[table[j]]
        return carry

    lax.fori_loop(0, out.shape[0], body, 0, unroll=8)


def back_kernel(
    mat_idx, send_slot, returned, pulled, grad, state, ray_ref, out, held, sems, picked,
    *, tiles, hits, last,
):
    t = pl.program_id(0)
    bins, tile_pix = held.shape[1:]
    chans = returned.shape[2]

    @pl.when(t == 0)
    def _():
        fetch_matrices(mat_idx, ray_ref, held, sems, tiles * hits)

    first = t * hits
    for k in range(hits):
        picked[k * bins : (k + 1) * bins, :] = returned[send_slot[first + k]]
    await_matrices(mat_idx, ray_ref, held, sems, first, hits)
    matrix = held[pl.ds(first, hits)].reshape(hits * bins, tile_pix)
    backed = lax.dot_general(
        matrix, picked[...], (((0,), (0,)), ((), ())), preferred_element_type=jnp.float32
    )
    change = (pulled[0] - relax_rate * backed).reshape(PIX, PIX, chans)
    adjoint = grad[...].astype(jnp.float32) + change
    if last:
        out[...] = adjoint
    else:
        value = state[...].astype(jnp.float32)
        out[...] = ((1.0 - value * value) * adjoint).astype(jnp.bfloat16)


def halo_of(scaled):
    rows, cols, chans = scaled.shape
    nr = lax.axis_size("row")
    nc = lax.axis_size(COL)
    up = [(i, i + 1) for i in range(nr - 1)]
    down = [(b, a) for a, b in up]
    right = [(i, i + 1) for i in range(nc - 1)]
    left = [(b, a) for a, b in right]
    above = lax.ppermute(scaled[rows - 1], "row", up)
    below = lax.ppermute(scaled[0], "row", down)
    last = jnp.concatenate([above[cols - 1 :], scaled[:, cols - 1], below[cols - 1 :]], axis=0)
    first = jnp.concatenate([above[:1], scaled[:, 0], below[:1]], axis=0)
    lefts = lax.ppermute(last, COL, right)
    rights = lax.ppermute(first, COL, left)
    return above, below, lefts, rights


def on_device(state, grad, kernel, ray_matrix, ray_weight, hits, offsets, block_slot, angle_count):
    f32, bf16, i32 = jnp.float32, jnp.bfloat16, jnp.int32
    rows_dev, cols_dev, chans = state.shape
    angles, spots, bins, tile_pix = ray_matrix.shape
    nr = lax.axis_size("row")
    nx = lax.axis_size("x")
    nc = lax.axis_size(COL)
    devices = nr * nc
    row, zh, zl, x = (lax.axis_index(a) for a in ("row",) + COL)
    tile_rows = rows_dev // PIX
    tile_cols = cols_dev // PIX
    tiles = tile_rows * tile_cols
    pairs = tiles * HITS
    blk_dev = ray_weight.shape[0]
    blocks = blk_dev * devices
    blk_ang = blocks // ANGLES
    cap = 2 * max(2, (pairs + devices - 2) // devices + 1)
    cap = min(cap, pairs)
    peers = nr * 2 * nx
    slots = peers * cap
    dense = 2 * blk_dev

    scaled = (
        (1.0 - jnp.square(state.astype(f32))) * grad.astype(f32)
    ).astype(bf16)
    halo = halo_of(scaled)

    everyone = hits.reshape(nr, tile_rows, nc, tile_cols, HITS).transpose(0, 2, 1, 3, 4)
    everyone = everyone.reshape(nr, 2, 2, nx, pairs)
    group = lax.dynamic_index_in_dim(everyone, zh, 1, keepdims=False).reshape(peers, pairs)
    storage = jnp.sum(
        jnp.where(group[:, :, None] == jnp.arange(blocks, dtype=i32), block_slot, 0), axis=2
    )
    owner = storage // blk_dev
    local = storage % blk_dev
    owner_z = (owner % nc) // nx
    owner_zh = owner_z // 2
    owner_zl = owner_z % 2
    side = jnp.where(owner_zh == zh, owner_zl, 1 - owner_zl)
    peer = ((owner // nc) * 2 + side) * nx + owner % nx
    place = owner_zh * blk_dev + local
    earlier = jnp.arange(pairs)[None, :] < jnp.arange(pairs)[:, None]
    ranking = jnp.sum(
        ((peer[:, :, None] == peer[:, None, :]) & earlier[None]).astype(i32), axis=2
    )
    me = (row * 2 + zl) * nx + x
    my_hits = lax.dynamic_index_in_dim(group, me, 0, keepdims=False)
    send_slot = lax.dynamic_index_in_dim(peer * cap + ranking, me, 0, keepdims=False)
    matched = (peer[:, None, :] == me) & (
        ranking[:, None, :] == jnp.arange(cap, dtype=i32)[None, :, None]
    )
    table = dense + jnp.sum(jnp.where(matched, place[:, None, :] - dense, 0), axis=2)
    table = table.reshape(slots)
    mat_idx = (my_hits // blk_ang) * spots + offsets.reshape(pairs)

    own_place = (row * nc + (zh * 2 + zl) * nx + x) * blk_dev + jnp.arange(blk_dev, dtype=i32)
    number = jnp.arange(blocks, dtype=i32)
    used = (
        (number % blk_ang).reshape(ANGLES, blk_ang) < angle_count[:, None]
    ).reshape(1, blocks)
    inuse = jnp.any((block_slot[None, :] == own_place[:, None]) & used, axis=1).astype(f32)
    own_scale = inuse[:, None, None] * ray_weight
    swap = [(z, RING - 1 - z) for z in range(RING)]

    def exchange(value):
        return lax.ppermute(value, ("zh", "zl"), swap)

    other_scale = exchange(own_scale)
    scaling = jnp.concatenate(
        [jnp.where(zh == 0, own_scale, other_scale), jnp.where(zh == 0, other_scale, own_scale)]
    )
    taps = kernel[::-1, ::-1].transpose(0, 1, 3, 2).reshape(3, 3 * chans, chans)
    rays = ray_matrix.reshape(angles * spots, bins, tile_pix)

    whole = lambda shape: pl.BlockSpec(shape, lambda t, *_: (0,) * len(shape))
    hbm = pl.BlockSpec(memory_space=pl.ANY)
    by_tile = pl.BlockSpec((PIX, PIX, chans), lambda t, *_: (t // tile_cols, t % tile_cols, 0))
    by_index = pl.BlockSpec((1, tile_pix, chans), lambda t, *_: (t, 0, 0))
    matrices = [
        pltpu.VMEM((pairs, bins, tile_pix), bf16),
        pltpu.SemaphoreType.DMA((pairs,)),
    ]
    block = (bins, chans)

    project = pl.pallas_call(
        functools.partial(project_kernel, tiles=tiles, hits=HITS, tile_cols=tile_cols),
        out_shape=(
            jax.ShapeDtypeStruct((tiles, tile_pix, chans), f32),
            jax.ShapeDtypeStruct((slots,) + block, bf16),
        ),
        grid_spec=pltpu.PrefetchScalarGridSpec(
            num_scalar_prefetch=2,
            grid=(tiles,),
            in_specs=[
                whole((rows_dev, cols_dev, chans)),
                whole((cols_dev, chans)),
                whole((cols_dev, chans)),
                whole((rows_dev + 2, chans)),
                whole((rows_dev + 2, chans)),
                whole((3, 3 * chans, chans)),
                hbm,
            ],
            out_specs=(by_index, whole((slots,) + block)),
            scratch_shapes=matrices
            + [
                pltpu.VMEM((rows_dev + 2, cols_dev + 16, chans), f32),
                pltpu.VMEM((rows_dev + 2, cols_dev, 3 * chans), bf16),
            ],
        ),
        name="project",
    )
    combine = pl.pallas_call(
        combine_kernel,
        out_shape=(
            jax.ShapeDtypeStruct((dense,) + block, f32),
            jax.ShapeDtypeStruct((dense,) + block, bf16),
        ),
        grid_spec=pltpu.PrefetchScalarGridSpec(
            num_scalar_prefetch=1,
            grid=(1,),
            in_specs=[whole((slots,) + block)],
            out_specs=(whole((dense,) + block), whole((dense,) + block)),
            scratch_shapes=[pltpu.VMEM((dense + 1,) + block, f32)],
        ),
        name="combine",
    )
    reply = pl.pallas_call(
        reply_kernel,
        out_shape=jax.ShapeDtypeStruct((slots,) + block, bf16),
        grid_spec=pltpu.PrefetchScalarGridSpec(
            num_scalar_prefetch=1,
            grid=(1,),
            in_specs=[whole((dense,) + block)] * 3,
            out_specs=whole((slots,) + block),
            scratch_shapes=[pltpu.VMEM((dense + 1,) + block, bf16)],
        ),
        name="reply",
    )

    def back(last):
        return pl.pallas_call(
            functools.partial(back_kernel, tiles=tiles, hits=HITS, last=last),
            out_shape=jax.ShapeDtypeStruct(state.shape, f32 if last else bf16),
            grid_spec=pltpu.PrefetchScalarGridSpec(
                num_scalar_prefetch=2,
                grid=(tiles,),
                in_specs=[whole((slots,) + block), by_index, by_tile, by_tile, hbm],
                out_specs=by_tile,
                scratch_shapes=matrices + [pltpu.VMEM((HITS * bins, chans), bf16)],
            ),
            name="back",
        )

    def across(value):
        value = value.reshape((peers, cap) + block)
        value = lax.all_to_all(value, GROUP, split_axis=0, concat_axis=0, tiled=True)
        return value.reshape((slots,) + block)

    for turn in range(ITERS):
        if turn:
            halo = halo_of(scaled)
        pulled, outgoing = project(mat_idx, send_slot, scaled, *halo, taps, rays)
        total, low = combine(table, across(outgoing))
        replies = reply(table, total, exchange(low), scaling)
        last = turn == ITERS - 1
        scaled = back(last)(mat_idx, send_slot, across(replies), pulled, grad, state, rays)
    return scaled


def solution(mesh):
    nr, nc = mesh.devices.shape
    fine = Mesh(mesh.devices.reshape(nr, 2, RING // 2, nc // RING), ("row",) + COL)
    image = P("row", COL, None)
    placed = (
        image,
        image,
        P(),
        P(),
        P(("row",) + COL, None, None),
        P(),
        image,
        P(),
        P(),
    )
    return jax.shard_map(
        on_device, mesh=fine, in_specs=placed, out_specs=image, check_vma=False
    )
```

```python
import functools

import jax
import jax.numpy as jnp
from jax import lax
from jax.experimental import pallas as pl
from jax.experimental.pallas import tpu as pltpu
from jax.sharding import Mesh, PartitionSpec as P

PIX = 32
ANGLES = 8
HITS = 16
ITERS = 2
RING = 4

relax_rate = 0.25
LIM = dict(project=24 << 20, combine=8 << 20, reply=8 << 20, back=24 << 20)

COL = ("zh", "zl", "x")
GROUP = ("row", "zl", "x")


def fetch_matrices(mat_idx, ray_ref, held, sems, pairs):
    def body(q, carry):
        pltpu.make_async_copy(ray_ref.at[mat_idx[q]], held.at[q], sems.at[q]).start()
        return carry

    lax.fori_loop(0, pairs, body, 0)


def await_matrices(mat_idx, ray_ref, held, sems, first, count):
    for k in range(count):
        q = first + k
        pltpu.make_async_copy(ray_ref.at[mat_idx[q]], held.at[q], sems.at[q]).wait()


def project_kernel(
    mat_idx, send_slot, scaled, above, below, left, right, taps, ray_ref,
    pulled_out, out, held, sems, wide, cols3, *, tiles, hits, tile_cols,
):
    t = pl.program_id(0)
    rows, cols, chans = scaled.shape
    bins, tile_pix = held.shape[1:]

    @pl.when(t == 0)
    def _():
        fetch_matrices(mat_idx, ray_ref, held, sems, tiles * hits)
        f32 = jnp.float32
        wide[0, 8 : 8 + cols, :] = above[...].astype(f32)
        wide[rows + 1, 8 : 8 + cols, :] = below[...].astype(f32)
        wide[1 : rows + 1, 8 : 8 + cols, :] = scaled[...].astype(f32)
        lefts = left[...].astype(f32)
        rights = right[...].astype(f32)
        for r in range(rows + 2):
            wide[r, 7:8, :] = lefts[r : r + 1, :]
            wide[r, 8 + cols : 9 + cols, :] = rights[r : r + 1, :]
        for dc in range(3):
            cols3[:, :, dc * chans : (dc + 1) * chans] = wide[:, 7 + dc : 7 + dc + cols, :].astype(
                jnp.bfloat16
            )
        out[...] = jnp.zeros_like(out)

    r0 = (t // tile_cols) * PIX
    c0 = pl.multiple_of((t % tile_cols) * PIX, PIX)
    acc = None
    for dr in range(3):
        window = cols3[pl.ds(r0 + dr, PIX), pl.ds(c0, PIX), :].reshape(tile_pix, 3 * chans)
        term = jnp.dot(window, taps[dr], preferred_element_type=jnp.float32)
        acc = term if acc is None else acc + term
    pulled_out[0] = acc
    low = acc.astype(jnp.bfloat16)
    first = t * hits
    await_matrices(mat_idx, ray_ref, held, sems, first, hits)
    matrix = held[pl.ds(first, hits)].reshape(hits * bins, tile_pix)
    part = jnp.dot(matrix, low, preferred_element_type=jnp.float32).astype(jnp.bfloat16)
    for k in range(hits):
        out[send_slot[first + k]] = part[k * bins : (k + 1) * bins, :]


def combine_kernel(table, recv, total, low, acc):
    acc[...] = jnp.zeros_like(acc)

    def body(j, carry):
        acc[table[j]] += recv[j].astype(jnp.float32)
        return carry

    lax.fori_loop(0, recv.shape[0], body, 0, unroll=8)
    total[...] = acc[: total.shape[0]]
    low[...] = acc[: total.shape[0]].astype(jnp.bfloat16)


def reply_kernel(table, total, other, scaling, out, held):
    n = total.shape[0]
    held[:n] = (scaling[...] * (total[...] + other[...].astype(jnp.float32))).astype(jnp.bfloat16)
    held[n] = jnp.zeros(held.shape[1:], jnp.bfloat16)

    def body(j, carry):
        out[j] = held[table[j]]
        return carry

    lax.fori_loop(0, out.shape[0], body, 0, unroll=8)


def back_kernel(
    mat_idx, send_slot, returned, pulled, grad, state, ray_ref, out, held, sems, picked,
    *, tiles, hits, last,
):
    t = pl.program_id(0)
    bins, tile_pix = held.shape[1:]
    chans = returned.shape[2]

    @pl.when(t == 0)
    def _():
        fetch_matrices(mat_idx, ray_ref, held, sems, tiles * hits)

    first = t * hits
    for k in range(hits):
        picked[k * bins : (k + 1) * bins, :] = returned[send_slot[first + k]]
    await_matrices(mat_idx, ray_ref, held, sems, first, hits)
    matrix = held[pl.ds(first, hits)].reshape(hits * bins, tile_pix)
    backed = lax.dot_general(
        matrix, picked[...], (((0,), (0,)), ((), ())), preferred_element_type=jnp.float32
    )
    change = (pulled[0] - relax_rate * backed).reshape(PIX, PIX, chans)
    adjoint = grad[...].astype(jnp.float32) + change
    if last:
        out[...] = adjoint
    else:
        value = state[...].astype(jnp.float32)
        out[...] = ((1.0 - value * value) * adjoint).astype(jnp.bfloat16)


def halo_of(scaled):
    rows, cols, chans = scaled.shape
    nr = lax.axis_size("row")
    nc = lax.axis_size(COL)
    up = [(i, i + 1) for i in range(nr - 1)]
    down = [(b, a) for a, b in up]
    right = [(i, i + 1) for i in range(nc - 1)]
    left = [(b, a) for a, b in right]
    above = lax.ppermute(scaled[rows - 1], "row", up)
    below = lax.ppermute(scaled[0], "row", down)
    last = jnp.concatenate([above[cols - 1 :], scaled[:, cols - 1], below[cols - 1 :]], axis=0)
    first = jnp.concatenate([above[:1], scaled[:, 0], below[:1]], axis=0)
    lefts = lax.ppermute(last, COL, right)
    rights = lax.ppermute(first, COL, left)
    return above, below, lefts, rights


def on_device(state, grad, kernel, ray_matrix, ray_weight, hits, offsets, block_slot, angle_count):
    f32, bf16, i32 = jnp.float32, jnp.bfloat16, jnp.int32
    rows_dev, cols_dev, chans = state.shape
    angles, spots, bins, tile_pix = ray_matrix.shape
    nr = lax.axis_size("row")
    nx = lax.axis_size("x")
    nc = lax.axis_size(COL)
    devices = nr * nc
    row, zh, zl, x = (lax.axis_index(a) for a in ("row",) + COL)
    tile_rows = rows_dev // PIX
    tile_cols = cols_dev // PIX
    tiles = tile_rows * tile_cols
    pairs = tiles * HITS
    blk_dev = ray_weight.shape[0]
    blocks = blk_dev * devices
    blk_ang = blocks // ANGLES
    cap = 2 * max(2, (pairs + devices - 2) // devices + 1)
    cap = min(cap, pairs)
    peers = nr * 2 * nx
    slots = peers * cap
    dense = 2 * blk_dev

    scaled = (
        (1.0 - jnp.square(state.astype(f32))) * grad.astype(f32)
    ).astype(bf16)
    halo = halo_of(scaled)

    everyone = hits.reshape(nr, tile_rows, nc, tile_cols, HITS).transpose(0, 2, 1, 3, 4)
    everyone = everyone.reshape(nr, 2, 2, nx, pairs)
    group = lax.dynamic_index_in_dim(everyone, zh, 1, keepdims=False).reshape(peers, pairs)
    storage = jnp.sum(
        jnp.where(group[:, :, None] == jnp.arange(blocks, dtype=i32), block_slot, 0), axis=2
    )
    owner = storage // blk_dev
    local = storage % blk_dev
    owner_z = (owner % nc) // nx
    owner_zh = owner_z // 2
    owner_zl = owner_z % 2
    side = jnp.where(owner_zh == zh, owner_zl, 1 - owner_zl)
    peer = ((owner // nc) * 2 + side) * nx + owner % nx
    place = owner_zh * blk_dev + local
    earlier = jnp.arange(pairs)[None, :] < jnp.arange(pairs)[:, None]
    ranking = jnp.sum(
        ((peer[:, :, None] == peer[:, None, :]) & earlier[None]).astype(i32), axis=2
    )
    me = (row * 2 + zl) * nx + x
    my_hits = lax.dynamic_index_in_dim(group, me, 0, keepdims=False)
    send_slot = lax.dynamic_index_in_dim(peer * cap + ranking, me, 0, keepdims=False)
    matched = (peer[:, None, :] == me) & (
        ranking[:, None, :] == jnp.arange(cap, dtype=i32)[None, :, None]
    )
    table = dense + jnp.sum(jnp.where(matched, place[:, None, :] - dense, 0), axis=2)
    table = table.reshape(slots)
    mat_idx = (my_hits // blk_ang) * spots + offsets.reshape(pairs)

    own_place = (row * nc + (zh * 2 + zl) * nx + x) * blk_dev + jnp.arange(blk_dev, dtype=i32)
    number = jnp.arange(blocks, dtype=i32)
    used = (
        (number % blk_ang).reshape(ANGLES, blk_ang) < angle_count[:, None]
    ).reshape(1, blocks)
    inuse = jnp.any((block_slot[None, :] == own_place[:, None]) & used, axis=1).astype(f32)
    own_scale = inuse[:, None, None] * ray_weight
    swap = [(z, RING - 1 - z) for z in range(RING)]

    def exchange(value):
        return lax.ppermute(value, ("zh", "zl"), swap)

    other_scale = exchange(own_scale)
    scaling = jnp.concatenate(
        [jnp.where(zh == 0, own_scale, other_scale), jnp.where(zh == 0, other_scale, own_scale)]
    )
    taps = kernel[::-1, ::-1].transpose(0, 1, 3, 2).reshape(3, 3 * chans, chans)
    rays = ray_matrix.reshape(angles * spots, bins, tile_pix)

    whole = lambda shape: pl.BlockSpec(shape, lambda t, *_: (0,) * len(shape))
    hbm = pl.BlockSpec(memory_space=pl.ANY)
    by_tile = pl.BlockSpec((PIX, PIX, chans), lambda t, *_: (t // tile_cols, t % tile_cols, 0))
    by_index = pl.BlockSpec((1, tile_pix, chans), lambda t, *_: (t, 0, 0))
    matrices = [
        pltpu.VMEM((pairs, bins, tile_pix), bf16),
        pltpu.SemaphoreType.DMA((pairs,)),
    ]
    block = (bins, chans)

    project = pl.pallas_call(
        functools.partial(project_kernel, tiles=tiles, hits=HITS, tile_cols=tile_cols),
        out_shape=(
            jax.ShapeDtypeStruct((tiles, tile_pix, chans), f32),
            jax.ShapeDtypeStruct((slots,) + block, bf16),
        ),
        grid_spec=pltpu.PrefetchScalarGridSpec(
            num_scalar_prefetch=2,
            grid=(tiles,),
            in_specs=[
                whole((rows_dev, cols_dev, chans)),
                whole((cols_dev, chans)),
                whole((cols_dev, chans)),
                whole((rows_dev + 2, chans)),
                whole((rows_dev + 2, chans)),
                whole((3, 3 * chans, chans)),
                hbm,
            ],
            out_specs=(by_index, whole((slots,) + block)),
            scratch_shapes=matrices
            + [
                pltpu.VMEM((rows_dev + 2, cols_dev + 16, chans), f32),
                pltpu.VMEM((rows_dev + 2, cols_dev, 3 * chans), bf16),
            ],
        ),
        name="project", compiler_params=pltpu.CompilerParams(vmem_limit_bytes=LIM["project"]),
    )
    combine = pl.pallas_call(
        combine_kernel,
        out_shape=(
            jax.ShapeDtypeStruct((dense,) + block, f32),
            jax.ShapeDtypeStruct((dense,) + block, bf16),
        ),
        grid_spec=pltpu.PrefetchScalarGridSpec(
            num_scalar_prefetch=1,
            grid=(1,),
            in_specs=[whole((slots,) + block)],
            out_specs=(whole((dense,) + block), whole((dense,) + block)),
            scratch_shapes=[pltpu.VMEM((dense + 1,) + block, f32)],
        ),
        name="combine", compiler_params=pltpu.CompilerParams(vmem_limit_bytes=LIM["combine"]),
    )
    reply = pl.pallas_call(
        reply_kernel,
        out_shape=jax.ShapeDtypeStruct((slots,) + block, bf16),
        grid_spec=pltpu.PrefetchScalarGridSpec(
            num_scalar_prefetch=1,
            grid=(1,),
            in_specs=[whole((dense,) + block)] * 3,
            out_specs=whole((slots,) + block),
            scratch_shapes=[pltpu.VMEM((dense + 1,) + block, bf16)],
        ),
        name="reply", compiler_params=pltpu.CompilerParams(vmem_limit_bytes=LIM["reply"]),
    )

    def back(last):
        return pl.pallas_call(
            functools.partial(back_kernel, tiles=tiles, hits=HITS, last=last),
            out_shape=jax.ShapeDtypeStruct(state.shape, f32 if last else bf16),
            grid_spec=pltpu.PrefetchScalarGridSpec(
                num_scalar_prefetch=2,
                grid=(tiles,),
                in_specs=[whole((slots,) + block), by_index, by_tile, by_tile, hbm],
                out_specs=by_tile,
                scratch_shapes=matrices + [pltpu.VMEM((HITS * bins, chans), bf16)],
            ),
            name="back", compiler_params=pltpu.CompilerParams(vmem_limit_bytes=LIM["back"]),
        )

    def across(value):
        value = value.reshape((peers, cap) + block)
        value = lax.all_to_all(value, GROUP, split_axis=0, concat_axis=0, tiled=True)
        return value.reshape((slots,) + block)

    for turn in range(ITERS):
        if turn:
            halo = halo_of(scaled)
        pulled, outgoing = project(mat_idx, send_slot, scaled, *halo, taps, rays)
        total, low = combine(table, across(outgoing))
        replies = reply(table, total, exchange(low), scaling)
        last = turn == ITERS - 1
        scaled = back(last)(mat_idx, send_slot, across(replies), pulled, grad, state, rays)
    return scaled


def solution(mesh):
    nr, nc = mesh.devices.shape
    fine = Mesh(mesh.devices.reshape(nr, 2, RING // 2, nc // RING), ("row",) + COL)
    image = P("row", COL, None)
    placed = (
        image,
        image,
        P(),
        P(),
        P(("row",) + COL, None, None),
        P(),
        image,
        P(),
        P(),
    )
    return jax.shard_map(
        on_device, mesh=fine, in_specs=placed, out_specs=image, check_vma=False
    )
```

```python
import functools

import jax
import jax.numpy as jnp
from jax import lax
from jax.experimental import pallas as pl
from jax.experimental.pallas import tpu as pltpu
from jax.sharding import Mesh, PartitionSpec as P

PIX = 32
ANGLES = 8
HITS = 16
ITERS = 2
RING = 4
PARTS = 2

relax_rate = 0.25

COL = ("zh", "zl", "x")
GROUP = ("row", "zl", "x")

VMEM = pl.BlockSpec(memory_space=pltpu.VMEM)
SMEM = pl.BlockSpec(memory_space=pltpu.SMEM)
HBM = pl.BlockSpec(memory_space=pltpu.HBM)


def gather_kernel(mat_idx, rays, *refs):
    outs, sem = refs[:-1], refs[-1]
    part = outs[0].shape[1]

    def copy(q, h):
        source = rays.at[mat_idx[q], pl.ds(h * part, part)]
        return pltpu.make_async_copy(source, outs[h].at[q], sem.at[q, h])

    def begin(q, carry):
        for h in range(len(outs)):
            copy(q, h).start()
        return carry

    def finish(q, carry):
        for h in range(len(outs)):
            copy(q, h).wait()
        return carry

    pairs = outs[0].shape[0]
    lax.fori_loop(0, pairs, begin, 0)
    lax.fori_loop(0, pairs, finish, 0)


def project_tile(send_slot, matrices, low, out, t):
    hits = HITS
    part, tile_pix = matrices.shape[1:]
    matrix = matrices[pl.ds(t * hits, hits)].reshape(hits * part, tile_pix)
    value = jnp.dot(matrix, low, preferred_element_type=jnp.float32).astype(jnp.bfloat16)
    for k in range(hits):
        out[send_slot[t * hits + k]] = value[k * part : (k + 1) * part, :]


def conv_kernel(
    send_slot, scaled, above, below, left, right, taps, matrices,
    pulled, low, out, wide, cols3, *, tile_cols,
):
    rows, cols, chans = scaled.shape
    tile_pix = PIX * PIX
    half = PIX // 2
    f32, bf16 = jnp.float32, jnp.bfloat16
    wide[0, 8 : 8 + cols, :] = above[...].astype(f32)
    wide[rows + 1, 8 : 8 + cols, :] = below[...].astype(f32)
    wide[1 : rows + 1, 8 : 8 + cols, :] = scaled[...].astype(f32)
    lefts = left[...].astype(f32)
    rights = right[...].astype(f32)
    for r in range(rows + 2):
        wide[r, 7:8, :] = lefts[r : r + 1, :]
        wide[r, 8 + cols : 9 + cols, :] = rights[r : r + 1, :]
    for dc in range(3):
        value = wide[:, 7 + dc : 7 + dc + cols, :].astype(bf16)
        cols3[:, :, :, dc * chans : (dc + 1) * chans] = value.reshape(
            (rows + 2) // 2, 2, cols, chans
        )
    out[...] = jnp.zeros_like(out)

    def body(t, carry):
        r0 = (t // tile_cols) * half
        c0 = pl.multiple_of((t % tile_cols) * PIX, PIX)
        acc = None
        for dr in range(4):
            window = cols3[pl.ds(r0 + dr // 2, half), dr % 2, pl.ds(c0, PIX), :]
            term = jnp.dot(
                window.reshape(half * PIX, 3 * chans), taps[dr], preferred_element_type=f32
            )
            acc = term if acc is None else acc + term
        for odd in range(2):
            value = acc[:, odd * chans : (odd + 1) * chans].reshape(half, PIX, chans)
            pulled[t, :, odd] = value
            low[t, :, odd] = value.astype(bf16)
        project_tile(send_slot, matrices, low[t].reshape(tile_pix, chans), out, t)
        return carry

    lax.fori_loop(0, pulled.shape[0], body, 0)


def project_kernel(send_slot, low, matrices, out):
    tiles = low.shape[0]
    chans = low.shape[-1]
    out[...] = jnp.zeros_like(out)

    def body(t, carry):
        project_tile(send_slot, matrices, low[t].reshape(PIX * PIX, chans), out, t)
        return carry

    lax.fori_loop(0, tiles, body, 0)


def combine_kernel(table, recv, total, low, acc):
    acc[...] = jnp.zeros_like(acc)

    def body(j, carry):
        acc[table[j]] += recv[j].astype(jnp.float32)
        return carry

    lax.fori_loop(0, recv.shape[0], body, 0, unroll=8)
    total[...] = acc[: total.shape[0]]
    low[...] = acc[: total.shape[0]].astype(jnp.bfloat16)


def reply_kernel(table, total, other, scaling, out, held):
    n = total.shape[0]
    held[:n] = (scaling[...] * (total[...] + other[...].astype(jnp.float32))).astype(jnp.bfloat16)
    held[n] = jnp.zeros(held.shape[1:], jnp.bfloat16)

    def body(j, carry):
        out[j] = held[table[j]]
        return carry

    lax.fori_loop(0, out.shape[0], body, 0, unroll=8)


def back_tile(send_slot, returned, matrices, picked, t):
    part, tile_pix = matrices.shape[1:]
    for k in range(HITS):
        picked[k * part : (k + 1) * part, :] = returned[send_slot[t * HITS + k]]
    matrix = matrices[pl.ds(t * HITS, HITS)].reshape(HITS * part, tile_pix)
    return lax.dot_general(
        matrix, picked[...], (((0,), (0,)), ((), ())), preferred_element_type=jnp.float32
    )


def back_kernel(send_slot, returned, matrices, so_far, out, picked):
    tiles = so_far.shape[0]

    def body(t, carry):
        backed = back_tile(send_slot, returned, matrices, picked, t)
        out[t] = so_far[t] - relax_rate * backed.reshape(so_far.shape[1:])
        return carry

    lax.fori_loop(0, tiles, body, 0)


def finish_kernel(
    send_slot, returned, matrices, so_far, grad, state, *refs, tile_cols, last,
):
    outs, picked = refs[:-1], refs[-1]
    tiles = so_far.shape[0]
    cols, chans = grad.shape[1:]

    def body(t, carry):
        backed = back_tile(send_slot, returned, matrices, picked, t)
        change = so_far[t].reshape(backed.shape) - relax_rate * backed
        where = (
            pl.ds((t // tile_cols) * PIX, PIX),
            pl.ds(pl.multiple_of((t % tile_cols) * PIX, PIX), PIX),
        )
        adjoint = grad[where].astype(jnp.float32) + change.reshape(PIX, PIX, chans)
        if last:
            outs[0][where] = adjoint
        else:
            value = state[where].astype(jnp.float32)
            outs[0][where] = ((1.0 - value * value) * adjoint).astype(jnp.bfloat16)
        return carry

    lax.fori_loop(0, tiles, body, 0)


def halo_of(scaled):
    rows, cols, chans = scaled.shape
    nr = lax.axis_size("row")
    nc = lax.axis_size(COL)
    up = [(i, i + 1) for i in range(nr - 1)]
    down = [(b, a) for a, b in up]
    right = [(i, i + 1) for i in range(nc - 1)]
    left = [(b, a) for a, b in right]
    above = lax.ppermute(scaled[rows - 1], "row", up)
    below = lax.ppermute(scaled[0], "row", down)
    last = jnp.concatenate([above[cols - 1 :], scaled[:, cols - 1], below[cols - 1 :]], axis=0)
    first = jnp.concatenate([above[:1], scaled[:, 0], below[:1]], axis=0)
    lefts = lax.ppermute(last, COL, right)
    rights = lax.ppermute(first, COL, left)
    return above, below, lefts, rights


def on_device(state, grad, kernel, ray_matrix, ray_weight, hits, offsets, block_slot, angle_count):
    f32, bf16, i32 = jnp.float32, jnp.bfloat16, jnp.int32
    rows_dev, cols_dev, chans = state.shape
    angles, spots, bins, tile_pix = ray_matrix.shape
    nr = lax.axis_size("row")
    nx = lax.axis_size("x")
    nc = lax.axis_size(COL)
    devices = nr * nc
    row, zh, zl, x = (lax.axis_index(a) for a in ("row",) + COL)
    tile_rows = rows_dev // PIX
    tile_cols = cols_dev // PIX
    tiles = tile_rows * tile_cols
    pairs = tiles * HITS
    blk_dev = ray_weight.shape[0]
    blocks = blk_dev * devices
    blk_ang = blocks // ANGLES
    cap = 2 * max(2, (pairs + devices - 2) // devices + 1)
    cap = min(cap, pairs)
    peers = nr * 2 * nx
    slots = peers * cap
    dense = 2 * blk_dev
    part = bins // PARTS

    scaled = (
        (1.0 - jnp.square(state.astype(f32))) * grad.astype(f32)
    ).astype(bf16)
    halo = halo_of(scaled)

    everyone = hits.reshape(nr, tile_rows, nc, tile_cols, HITS).transpose(0, 2, 1, 3, 4)
    everyone = everyone.reshape(nr, 2, 2, nx, pairs)
    group = lax.dynamic_index_in_dim(everyone, zh, 1, keepdims=False).reshape(peers, pairs)
    storage = jnp.sum(
        jnp.where(group[:, :, None] == jnp.arange(blocks, dtype=i32), block_slot, 0), axis=2
    )
    owner = storage // blk_dev
    local = storage % blk_dev
    owner_z = (owner % nc) // nx
    owner_zh = owner_z // 2
    owner_zl = owner_z % 2
    side = jnp.where(owner_zh == zh, owner_zl, 1 - owner_zl)
    peer = ((owner // nc) * 2 + side) * nx + owner % nx
    place = owner_zh * blk_dev + local
    earlier = jnp.arange(pairs)[None, :] < jnp.arange(pairs)[:, None]
    ranking = jnp.sum(
        ((peer[:, :, None] == peer[:, None, :]) & earlier[None]).astype(i32), axis=2
    )
    me = (row * 2 + zl) * nx + x
    my_hits = lax.dynamic_index_in_dim(group, me, 0, keepdims=False)
    send_slot = lax.dynamic_index_in_dim(peer * cap + ranking, me, 0, keepdims=False)
    matched = (peer[:, None, :] == me) & (
        ranking[:, None, :] == jnp.arange(cap, dtype=i32)[None, :, None]
    )
    table = dense + jnp.sum(jnp.where(matched, place[:, None, :] - dense, 0), axis=2)
    table = table.reshape(slots)
    mat_idx = (my_hits // blk_ang) * spots + offsets.reshape(pairs)

    own_place = (row * nc + (zh * 2 + zl) * nx + x) * blk_dev + jnp.arange(blk_dev, dtype=i32)
    number = jnp.arange(blocks, dtype=i32)
    used = (
        (number % blk_ang).reshape(ANGLES, blk_ang) < angle_count[:, None]
    ).reshape(1, blocks)
    inuse = jnp.any((block_slot[None, :] == own_place[:, None]) & used, axis=1).astype(f32)
    own_scale = inuse[:, None, None] * ray_weight
    swap = [(z, RING - 1 - z) for z in range(RING)]

    def exchange(value):
        return lax.ppermute(value, ("zh", "zl"), swap)

    other_scale = exchange(own_scale)
    scaling = jnp.concatenate(
        [jnp.where(zh == 0, own_scale, other_scale), jnp.where(zh == 0, other_scale, own_scale)]
    )
    scalings = [scaling[:, h * part : (h + 1) * part] for h in range(PARTS)]
    taps = kernel[::-1, ::-1].transpose(0, 1, 3, 2).reshape(3, 3 * chans, chans)
    blank = jnp.zeros_like(taps[:1])
    taps = jnp.concatenate(
        [jnp.concatenate([taps, blank]), jnp.concatenate([blank, taps])], axis=2
    )
    rays = ray_matrix.reshape(angles * spots, bins, tile_pix)

    block = (part, chans)
    tiled = (tiles, PIX // 2, 2, PIX, chans)
    shape = jax.ShapeDtypeStruct
    slot_out = shape((slots,) + block, bf16)

    def limit(mib):
        return pltpu.CompilerParams(vmem_limit_bytes=mib << 20)

    gather = pl.pallas_call(
        gather_kernel,
        out_shape=[shape((pairs, part, tile_pix), bf16)] * PARTS,
        in_specs=[SMEM, HBM],
        out_specs=[VMEM] * PARTS,
        scratch_shapes=[pltpu.SemaphoreType.DMA((pairs, PARTS))],
        compiler_params=limit(8),
        name="gather",
    )
    conv = pl.pallas_call(
        functools.partial(conv_kernel, tile_cols=tile_cols),
        out_shape=(shape(tiled, f32), shape(tiled, bf16), slot_out),
        in_specs=[SMEM] + [VMEM] * 7,
        out_specs=(VMEM, VMEM, VMEM),
        scratch_shapes=[
            pltpu.VMEM((rows_dev + 2, cols_dev + 16, chans), f32),
            pltpu.VMEM(((rows_dev + 2) // 2, 2, cols_dev, 3 * chans), bf16),
        ],
        compiler_params=limit(20),
        name="conv",
    )
    project = pl.pallas_call(
        project_kernel,
        out_shape=slot_out,
        in_specs=[SMEM, VMEM, VMEM],
        out_specs=VMEM,
        compiler_params=limit(12),
        name="project",
    )
    combine = pl.pallas_call(
        combine_kernel,
        out_shape=(shape((dense,) + block, f32), shape((dense,) + block, bf16)),
        in_specs=[SMEM, VMEM],
        out_specs=(VMEM, VMEM),
        scratch_shapes=[pltpu.VMEM((dense + 1,) + block, f32)],
        compiler_params=limit(8),
        name="combine",
    )
    reply = pl.pallas_call(
        reply_kernel,
        out_shape=slot_out,
        in_specs=[SMEM, VMEM, VMEM, VMEM],
        out_specs=VMEM,
        scratch_shapes=[pltpu.VMEM((dense + 1,) + block, bf16)],
        compiler_params=limit(8),
        name="reply",
    )
    picked = pltpu.VMEM((HITS * part, chans), bf16)
    back = pl.pallas_call(
        back_kernel,
        out_shape=shape(tiled, f32),
        in_specs=[SMEM] + [VMEM] * 3,
        out_specs=VMEM,
        scratch_shapes=[picked],
        compiler_params=limit(16),
        name="back",
    )

    def finish(last):
        return pl.pallas_call(
            functools.partial(finish_kernel, tile_cols=tile_cols, last=last),
            out_shape=[shape(state.shape, f32 if last else bf16)],
            in_specs=[SMEM] + [VMEM] * 5,
            out_specs=[VMEM],
            scratch_shapes=[picked],
            compiler_params=limit(16),
            name="finish",
        )

    def across(value):
        value = value.reshape((peers, cap) + block)
        value = lax.all_to_all(value, GROUP, split_axis=0, concat_axis=0, tiled=True)
        return value.reshape((slots,) + block)

    mats = gather(mat_idx, rays)
    for turn in range(ITERS):
        if turn:
            halo = halo_of(scaled)
        pulled, low, first = conv(send_slot, scaled, *halo, taps, mats[0])
        sent = [first] + [project(send_slot, low, mats[h]) for h in range(1, PARTS)]
        replies = []
        for h in range(PARTS):
            total, mine = combine(table, across(sent[h]))
            replies.append(reply(table, total, exchange(mine), scalings[h]))
        so_far = pulled
        for h in range(PARTS - 1):
            so_far = back(send_slot, across(replies[h]), mats[h], so_far)
        last = turn == ITERS - 1
        (scaled,) = finish(last)(
            send_slot, across(replies[-1]), mats[-1], so_far, grad, state
        )
    return scaled


def solution(mesh):
    nr, nc = mesh.devices.shape
    fine = Mesh(mesh.devices.reshape(nr, 2, RING // 2, nc // RING), ("row",) + COL)
    image = P("row", COL, None)
    placed = (
        image,
        image,
        P(),
        P(),
        P(("row",) + COL, None, None),
        P(),
        image,
        P(),
        P(),
    )
    return jax.shard_map(
        on_device, mesh=fine, in_specs=placed, out_specs=image, check_vma=False
    )
```

```python
import functools

import jax
import jax.numpy as jnp
from jax import lax
from jax.experimental import pallas as pl
from jax.experimental.pallas import tpu as pltpu
from jax.sharding import Mesh, PartitionSpec as P

PIX = 32
ANGLES = 8
HITS = 16
ITERS = 2
RING = 4

relax_rate = 0.25

COL = ("zh", "zl", "x")
GROUP = ("row", "zl", "x")

VMEM = pl.BlockSpec(memory_space=pltpu.VMEM)
SMEM = pl.BlockSpec(memory_space=pltpu.SMEM)


def start_kernel(state, grad, scaled, top, bottom, left, right):
    value = state[...].astype(jnp.float32)
    value = (1.0 - value * value) * grad[...].astype(jnp.float32)
    emit_edges(value, scaled, top, bottom, left, right)


def emit_edges(value, scaled, top, bottom, left, right):
    rows, cols = value.shape[:2]
    scaled[...] = value.astype(jnp.bfloat16)
    top[...] = scaled[0]
    bottom[...] = scaled[rows - 1]
    left[...] = value[:, 0, :].astype(jnp.bfloat16)
    right[...] = value[:, cols - 1, :].astype(jnp.bfloat16)


def sides_kernel(above, below, left, right, first, last):
    rows = left.shape[0]
    cols = above.shape[0]
    f32 = jnp.float32
    for out, edge, at in ((first, left, 0), (last, right, cols - 1)):
        group = at // 16 * 16
        corner_a = above[group : group + 16, :].astype(f32)[at - group : at - group + 1, :]
        corner_b = below[group : group + 16, :].astype(f32)[at - group : at - group + 1, :]
        out[8 : 8 + rows, :] = edge[...].astype(f32)
        out[7:8, :] = corner_a
        out[8 + rows : 9 + rows, :] = corner_b


def load_matrices(mat_idx, rays, held, t):
    bins = rays.shape[1]
    for k in range(HITS):
        held[k * bins : (k + 1) * bins, :] = rays[mat_idx[t * HITS + k]]


def conv_kernel(
    mat_idx, send_slot, scaled, above, below, left, right, taps, rays,
    pulled, out, wide, cols3, held, *, tile_cols,
):
    rows, cols, chans = scaled.shape
    bins = rays.shape[1]
    half = PIX // 2
    f32, bf16 = jnp.float32, jnp.bfloat16
    wide[0, 8 : 8 + cols, :] = above[...].astype(f32)
    wide[rows + 1, 8 : 8 + cols, :] = below[...].astype(f32)
    wide[1 : rows + 1, 8 : 8 + cols, :] = scaled[...].astype(f32)
    for r in range(rows + 2):
        wide[r, 7:8, :] = left[7 + r : 8 + r, :]
        wide[r, 8 + cols : 9 + cols, :] = right[7 + r : 8 + r, :]
    for dc in range(3):
        value = wide[:, 7 + dc : 7 + dc + cols, :].astype(bf16)
        cols3[:, :, :, dc * chans : (dc + 1) * chans] = value.reshape(
            (rows + 2) // 2, 2, cols, chans
        )
    out[...] = jnp.zeros_like(out)

    def body(t, carry):
        r0 = (t // tile_cols) * half
        c0 = pl.multiple_of((t % tile_cols) * PIX, PIX)
        load_matrices(mat_idx, rays, held, t)
        acc = None
        for dr in range(4):
            window = cols3[pl.ds(r0 + dr // 2, half), dr % 2, pl.ds(c0, PIX), :]
            term = jnp.dot(
                window.reshape(half * PIX, 3 * chans), taps[dr], preferred_element_type=f32
            )
            acc = term if acc is None else acc + term
        for odd in range(2):
            value = acc[:, odd * chans : (odd + 1) * chans].reshape(half, PIX, chans)
            pulled[t, :, odd] = value
        low = pulled[t].reshape(PIX * PIX, chans).astype(bf16)
        value = jnp.dot(held[...], low, preferred_element_type=f32).astype(bf16)
        for k in range(HITS):
            out[send_slot[t * HITS + k]] = value[k * bins : (k + 1) * bins, :]
        return carry

    lax.fori_loop(0, pulled.shape[0], body, 0)


def combine_kernel(table, recv, total, low, acc):
    acc[...] = jnp.zeros_like(acc)

    def body(j, carry):
        acc[table[j]] += recv[j].astype(jnp.float32)
        return carry

    lax.fori_loop(0, recv.shape[0], body, 0, unroll=8)
    total[...] = acc[: total.shape[0]]
    low[...] = acc[: total.shape[0]].astype(jnp.bfloat16)


def reply_kernel(table, used, total, other, own_weight, other_weight, out, held):
    n = total.shape[0]
    own = own_weight.shape[0]
    place = used[n]
    for half, weight in enumerate((own_weight, other_weight)):
        first = jnp.where(half == 0, place, n - own - place)
        for b in range(own):
            d = first + b
            scale = used[d].astype(jnp.float32) * weight[b]
            value = total[d] + other[d].astype(jnp.float32)
            held[d] = (scale * value).astype(jnp.bfloat16)
    held[n] = jnp.zeros(held.shape[1:], jnp.bfloat16)

    def body(j, carry):
        out[j] = held[table[j]]
        return carry

    lax.fori_loop(0, out.shape[0], body, 0, unroll=8)


def finish_kernel(
    mat_idx, send_slot, returned, pulled, grad, state, rays, *refs, tile_cols, last,
):
    outs, (whole, picked, held) = refs[:-3], refs[-3:]
    tiles = pulled.shape[0]
    bins = rays.shape[1]
    chans = grad.shape[2]
    f32 = jnp.float32

    def body(t, carry):
        load_matrices(mat_idx, rays, held, t)
        for k in range(HITS):
            picked[k * bins : (k + 1) * bins, :] = returned[send_slot[t * HITS + k]]
        backed = lax.dot_general(
            held[...], picked[...], (((0,), (0,)), ((), ())), preferred_element_type=f32
        )
        change = pulled[t].reshape(backed.shape) - relax_rate * backed
        where = (
            pl.ds((t // tile_cols) * PIX, PIX),
            pl.ds(pl.multiple_of((t % tile_cols) * PIX, PIX), PIX),
        )
        adjoint = grad[where].astype(f32) + change.reshape(PIX, PIX, chans)
        if last:
            outs[0][where] = adjoint
        else:
            value = state[where].astype(f32)
            whole[where] = (1.0 - value * value) * adjoint
        return carry

    lax.fori_loop(0, tiles, body, 0)
    if not last:
        emit_edges(whole[...], *outs)


def on_device(state, grad, kernel, ray_matrix, ray_weight, hits, offsets, block_slot, angle_count):
    f32, bf16, i32 = jnp.float32, jnp.bfloat16, jnp.int32
    rows_dev, cols_dev, chans = state.shape
    angles, spots, bins, tile_pix = ray_matrix.shape
    nr = lax.axis_size("row")
    nx = lax.axis_size("x")
    nc = lax.axis_size(COL)
    devices = nr * nc
    row, zh, zl, x = (lax.axis_index(a) for a in ("row",) + COL)
    tile_rows = rows_dev // PIX
    tile_cols = cols_dev // PIX
    tiles = tile_rows * tile_cols
    pairs = tiles * HITS
    blk_dev = ray_weight.shape[0]
    blocks = blk_dev * devices
    blk_ang = blocks // ANGLES
    cap = 2 * max(2, (pairs + devices - 2) // devices + 1)
    cap = min(cap, pairs)
    peers = nr * 2 * nx
    slots = peers * cap
    dense = 2 * blk_dev
    swap = [(z, RING - 1 - z) for z in range(RING)]

    def exchange(value):
        return lax.ppermute(value, ("zh", "zl"), swap)

    other_weight = exchange(ray_weight)

    everyone = hits.reshape(nr, tile_rows, nc, tile_cols, HITS).transpose(0, 2, 1, 3, 4)
    everyone = everyone.reshape(nr, 2, 2, nx, pairs)
    group = lax.dynamic_index_in_dim(everyone, zh, 1, keepdims=False).reshape(peers, pairs)
    storage = jnp.sum(
        jnp.where(group[:, :, None] == jnp.arange(blocks, dtype=i32), block_slot, 0), axis=2
    )
    owner = storage // blk_dev
    local = storage % blk_dev
    owner_z = (owner % nc) // nx
    owner_zh = owner_z // 2
    owner_zl = owner_z % 2
    side = jnp.where(owner_zh == zh, owner_zl, 1 - owner_zl)
    peer = ((owner // nc) * 2 + side) * nx + owner % nx
    place = owner_zh * blk_dev + local
    earlier = jnp.arange(pairs)[None, :] < jnp.arange(pairs)[:, None]
    ranking = jnp.sum(
        ((peer[:, :, None] == peer[:, None, :]) & earlier[None]).astype(i32), axis=2
    )
    me = (row * 2 + zl) * nx + x
    my_hits = lax.dynamic_index_in_dim(group, me, 0, keepdims=False)
    send_slot = lax.dynamic_index_in_dim(peer * cap + ranking, me, 0, keepdims=False)
    matched = (peer[:, None, :] == me) & (
        ranking[:, None, :] == jnp.arange(cap, dtype=i32)[None, :, None]
    )
    table = dense + jnp.sum(jnp.where(matched, place[:, None, :] - dense, 0), axis=2)
    table = table.reshape(slots)
    mat_idx = (my_hits // blk_ang) * spots + offsets.reshape(pairs)

    my_z = zh * 2 + zl
    half = jnp.arange(dense, dtype=i32) // blk_dev
    dense_z = jnp.where(half == zh, my_z, RING - 1 - my_z)
    dense_place = (row * nc + dense_z * nx + x) * blk_dev + jnp.arange(dense, dtype=i32) % blk_dev
    number = jnp.arange(blocks, dtype=i32)
    active = (
        (number % blk_ang).reshape(ANGLES, blk_ang) < angle_count[:, None]
    ).reshape(1, blocks)
    used = jnp.any((block_slot[None, :] == dense_place[:, None]) & active, axis=1).astype(i32)
    used = jnp.concatenate([used, jnp.full((1,), zh * blk_dev, i32)])

    taps = kernel[::-1, ::-1].transpose(0, 1, 3, 2).reshape(3, 3 * chans, chans)
    blank = jnp.zeros_like(taps[:1])
    taps = jnp.concatenate(
        [jnp.concatenate([taps, blank]), jnp.concatenate([blank, taps])], axis=2
    )
    rays = ray_matrix.reshape(angles * spots, bins, tile_pix)

    block = (bins, chans)
    shape = jax.ShapeDtypeStruct
    slot_out = shape((slots,) + block, bf16)
    edges = (
        shape(state.shape, bf16),
        shape((cols_dev, chans), bf16),
        shape((cols_dev, chans), bf16),
        shape((rows_dev, chans), bf16),
        shape((rows_dev, chans), bf16),
    )

    def limit(mib):
        return pltpu.CompilerParams(vmem_limit_bytes=mib << 20)

    start = pl.pallas_call(
        start_kernel,
        out_shape=edges,
        in_specs=[VMEM] * 2,
        out_specs=(VMEM,) * 5,
        compiler_params=limit(8),
        name="start",
    )
    sides = pl.pallas_call(
        sides_kernel,
        out_shape=[shape((rows_dev + 16, chans), f32)] * 2,
        in_specs=[VMEM] * 4,
        out_specs=[VMEM] * 2,
        compiler_params=limit(4),
        name="sides",
    )
    held = pltpu.VMEM((HITS * bins, tile_pix), bf16)
    conv = pl.pallas_call(
        functools.partial(conv_kernel, tile_cols=tile_cols),
        out_shape=(shape((tiles, PIX // 2, 2, PIX, chans), f32), slot_out),
        in_specs=[SMEM] * 2 + [VMEM] * 7,
        out_specs=(VMEM, VMEM),
        scratch_shapes=[
            pltpu.VMEM((rows_dev + 2, cols_dev + 16, chans), f32),
            pltpu.VMEM(((rows_dev + 2) // 2, 2, cols_dev, 3 * chans), bf16),
            held,
        ],
        compiler_params=limit(20),
        name="conv",
    )
    combine = pl.pallas_call(
        combine_kernel,
        out_shape=(shape((dense,) + block, f32), shape((dense,) + block, bf16)),
        in_specs=[SMEM, VMEM],
        out_specs=(VMEM, VMEM),
        scratch_shapes=[pltpu.VMEM((dense + 1,) + block, f32)],
        compiler_params=limit(8),
        name="combine",
    )
    reply = pl.pallas_call(
        reply_kernel,
        out_shape=slot_out,
        in_specs=[SMEM] * 2 + [VMEM] * 4,
        out_specs=VMEM,
        scratch_shapes=[pltpu.VMEM((dense + 1,) + block, bf16)],
        compiler_params=limit(8),
        name="reply",
    )

    def finish(last):
        return pl.pallas_call(
            functools.partial(finish_kernel, tile_cols=tile_cols, last=last),
            out_shape=(shape(state.shape, f32),) if last else edges,
            in_specs=[SMEM] * 2 + [VMEM] * 5,
            out_specs=(VMEM,) * (1 if last else 5),
            scratch_shapes=[
                pltpu.VMEM((8, 128, 128) if last else state.shape, f32),
                pltpu.VMEM((HITS * bins, chans), bf16),
                held,
            ],
            compiler_params=limit(20),
            name="finish",
        )

    def across(value):
        value = value.reshape((peers, cap) + block)
        value = lax.all_to_all(value, GROUP, split_axis=0, concat_axis=0, tiled=True)
        return value.reshape((slots,) + block)

    up = [(i, i + 1) for i in range(nr - 1)]
    down = [(b, a) for a, b in up]
    rightward = [(i, i + 1) for i in range(nc - 1)]
    leftward = [(b, a) for a, b in rightward]

    def halo_of(top, bottom, left, right):
        above = lax.ppermute(bottom, "row", up)
        below = lax.ppermute(top, "row", down)
        first, last = sides(above, below, left, right)
        lefts = lax.ppermute(last, COL, rightward)
        rights = lax.ppermute(first, COL, leftward)
        return above, below, lefts, rights

    scaled, *rim = start(state, grad)
    halo = halo_of(*rim)
    for turn in range(ITERS):
        if turn:
            halo = halo_of(*rim)
        pulled, outgoing = conv(mat_idx, send_slot, scaled, *halo, taps, rays)
        if not turn:
            outgoing, table, used, other_weight = lax.optimization_barrier(
                (outgoing, table, used, other_weight)
            )
        total, mine = combine(table, across(outgoing))
        replies = reply(table, used, total, exchange(mine), ray_weight, other_weight)
        last = turn == ITERS - 1
        scaled, *rim = finish(last)(
            mat_idx, send_slot, across(replies), pulled, grad, state, rays
        )
    return scaled


def solution(mesh):
    nr, nc = mesh.devices.shape
    fine = Mesh(mesh.devices.reshape(nr, 2, RING // 2, nc // RING), ("row",) + COL)
    image = P("row", COL, None)
    placed = (
        image,
        image,
        P(),
        P(),
        P(("row",) + COL, None, None),
        P(),
        image,
        P(),
        P(),
    )
    return jax.shard_map(
        on_device, mesh=fine, in_specs=placed, out_specs=image, check_vma=False
    )
```

```python
import functools

import jax
import jax.numpy as jnp
from jax import lax
from jax.experimental import pallas as pl
from jax.experimental.pallas import tpu as pltpu
from jax.sharding import Mesh, PartitionSpec as P

PIX = 32
ANGLES = 8
HITS = 16
ITERS = 2
RING = 4

relax_rate = 0.25

COL = ("zh", "zl", "x")
GROUP = ("row", "zl", "x")

VMEM = pl.BlockSpec(memory_space=pltpu.VMEM)
SMEM = pl.BlockSpec(memory_space=pltpu.SMEM)


def start_kernel(state, grad, scaled):
    value = state[...].astype(jnp.float32)
    scaled[...] = ((1.0 - value * value) * grad[...].astype(jnp.float32)).astype(jnp.bfloat16)


def emit_edges(value, scaled, top, bottom, left, right):
    rows, cols = value.shape[:2]
    scaled[...] = value.astype(jnp.bfloat16)
    top[...] = scaled[0]
    bottom[...] = scaled[rows - 1]
    left[...] = value[:, 0, :].astype(jnp.bfloat16)
    right[...] = value[:, cols - 1, :].astype(jnp.bfloat16)


def sides_kernel(above, below, left, right, first, last):
    rows = left.shape[0]
    cols = above.shape[0]
    f32 = jnp.float32
    for out, edge, at in ((first, left, 0), (last, right, cols - 1)):
        group = at // 16 * 16
        corner_a = above[group : group + 16, :].astype(f32)[at - group : at - group + 1, :]
        corner_b = below[group : group + 16, :].astype(f32)[at - group : at - group + 1, :]
        out[8 : 8 + rows, :] = edge[...].astype(f32)
        out[7:8, :] = corner_a
        out[8 + rows : 9 + rows, :] = corner_b


def matrices_of(mat_idx, rays, t):
    return jnp.concatenate([rays[mat_idx[t * HITS + k]] for k in range(HITS)], axis=0)


def forward_tile(mat_idx, send_slot, taps, rays, pulled, out, cols3, t, tile_cols):
    chans = pulled.shape[-1]
    bins = rays.shape[1]
    half = PIX // 2
    r0, c0 = t // tile_cols * half, t % tile_cols * PIX
    window = jnp.concatenate(
        [
            cols3[r0 + dr // 2 : r0 + dr // 2 + half, dr % 2, c0 : c0 + PIX, :].reshape(
                half * PIX, 3 * chans
            )
            for dr in range(4)
        ],
        axis=1,
    )
    acc = jnp.dot(window, taps[...], preferred_element_type=jnp.float32)
    for odd in range(2):
        value = acc[:, odd * chans : (odd + 1) * chans].reshape(half, PIX, chans)
        pulled[t, :, odd] = value
    low = pulled[t].reshape(PIX * PIX, chans).astype(jnp.bfloat16)
    value = jnp.dot(
        matrices_of(mat_idx, rays, t), low, preferred_element_type=jnp.float32
    ).astype(jnp.bfloat16)
    for k in range(HITS):
        out[send_slot[t * HITS + k]] = value[k * bins : (k + 1) * bins, :]


def tiles_at(tiles, tile_cols, inner):
    return [t for t in range(tiles) if (0 < t % tile_cols < tile_cols - 1) == inner]


def inner_kernel(
    mat_idx, send_slot, scaled, above, below, taps, rays, pulled, out, cols3, wide, *, tile_cols,
):
    rows, cols, chans = scaled.shape
    f32, bf16 = jnp.float32, jnp.bfloat16
    wide[0, 8 : 8 + cols, :] = above[...].astype(f32)
    wide[rows + 1, 8 : 8 + cols, :] = below[...].astype(f32)
    wide[1 : rows + 1, 8 : 8 + cols, :] = scaled[...].astype(f32)
    wide[:, 0:8, :] = jnp.zeros((rows + 2, 8, chans), f32)
    wide[:, 8 + cols :, :] = jnp.zeros((rows + 2, 8, chans), f32)
    for dc in range(3):
        value = wide[:, 7 + dc : 7 + dc + cols, :].astype(bf16)
        cols3[:, :, :, dc * chans : (dc + 1) * chans] = value.reshape(
            (rows + 2) // 2, 2, cols, chans
        )
    out[...] = jnp.zeros_like(out)
    for t in tiles_at(pulled.shape[0], tile_cols, True):
        forward_tile(mat_idx, send_slot, taps, rays, pulled, out, cols3, t, tile_cols)


def outer_kernel(
    mat_idx, send_slot, left, right, taps, rays, _pulled, _out, _cols3,
    pulled, out, cols3, *, tile_cols,
):
    cols = cols3.shape[2]
    chans = pulled.shape[-1]
    group = 16
    spot = lax.broadcasted_iota(jnp.int32, (group, chans), 0)
    for edge, dc, first, at in ((left, 0, 0, 0), (right, 2, cols - group, group - 1)):
        lanes = slice(dc * chans, (dc + 1) * chans)
        for r in range(2 * cols3.shape[0]):
            there = (r // 2, r % 2, slice(first, first + group), lanes)
            value = jnp.where(spot == at, edge[7 + r : 8 + r, :], cols3[there].astype(jnp.float32))
            cols3[there] = value.astype(jnp.bfloat16)
    for t in tiles_at(pulled.shape[0], tile_cols, False):
        forward_tile(mat_idx, send_slot, taps, rays, pulled, out, cols3, t, tile_cols)


def combine_kernel(table, recv, total, low, acc):
    acc[...] = jnp.zeros_like(acc)

    def body(j, carry):
        acc[table[j]] += recv[j].astype(jnp.float32)
        return carry

    lax.fori_loop(0, recv.shape[0], body, 0, unroll=8)
    total[...] = acc[: total.shape[0]]
    low[...] = acc[: total.shape[0]].astype(jnp.bfloat16)


def reply_kernel(table, used, total, other, own_weight, other_weight, out, held):
    n = total.shape[0]
    own = own_weight.shape[0]
    place = used[n]
    for half, weight in enumerate((own_weight, other_weight)):
        first = jnp.where(half == 0, place, n - own - place)
        for b in range(own):
            d = first + b
            scale = used[d].astype(jnp.float32) * weight[b]
            value = total[d] + other[d].astype(jnp.float32)
            held[d] = (scale * value).astype(jnp.bfloat16)
    held[n] = jnp.zeros(held.shape[1:], jnp.bfloat16)

    def body(j, carry):
        out[j] = held[table[j]]
        return carry

    lax.fori_loop(0, out.shape[0], body, 0, unroll=8)


def finish_kernel(
    mat_idx, send_slot, returned, pulled, grad, state, rays, *refs, tile_cols, last,
):
    outs, (whole, mark) = refs[:-2], refs[-2:]
    tiles = pulled.shape[0]
    chans = grad.shape[2]
    f32 = jnp.float32

    def place(t):
        r0, c0 = t // tile_cols * PIX, t % tile_cols * PIX
        return slice(r0, r0 + PIX), slice(c0, c0 + PIX)

    def leave(t):
        where = place(t)
        return pltpu.make_async_copy(whole.at[where], outs[0].at[where], mark.at[t])

    for t in range(tiles):
        picked = jnp.concatenate([returned[send_slot[t * HITS + k]] for k in range(HITS)], axis=0)
        backed = lax.dot_general(
            picked,
            matrices_of(mat_idx, rays, t),
            (((0,), (0,)), ((), ())),
            preferred_element_type=f32,
        ).T
        change = pulled[t].reshape(backed.shape) - relax_rate * backed
        where = place(t)
        adjoint = grad[where].astype(f32) + change.reshape(PIX, PIX, chans)
        if last:
            whole[where] = adjoint
            leave(t).start()
        else:
            value = state[where].astype(f32)
            whole[where] = (1.0 - value * value) * adjoint
    if last:
        for t in range(tiles):
            leave(t).wait()
    else:
        emit_edges(whole[...], *outs)


def on_device(state, grad, kernel, ray_matrix, ray_weight, hits, offsets, block_slot, angle_count):
    f32, bf16, i32 = jnp.float32, jnp.bfloat16, jnp.int32
    rows_dev, cols_dev, chans = state.shape
    angles, spots, bins, tile_pix = ray_matrix.shape
    nr = lax.axis_size("row")
    nx = lax.axis_size("x")
    nc = lax.axis_size(COL)
    devices = nr * nc
    row, zh, zl, x = (lax.axis_index(a) for a in ("row",) + COL)
    tile_rows = rows_dev // PIX
    tile_cols = cols_dev // PIX
    tiles = tile_rows * tile_cols
    pairs = tiles * HITS
    blk_dev = ray_weight.shape[0]
    blocks = blk_dev * devices
    blk_ang = blocks // ANGLES
    cap = 2 * max(2, (pairs + devices - 2) // devices + 1)
    cap = min(cap, pairs)
    peers = nr * 2 * nx
    slots = peers * cap
    dense = 2 * blk_dev
    swap = [(z, RING - 1 - z) for z in range(RING)]

    def exchange(value):
        return lax.ppermute(value, ("zh", "zl"), swap)

    everyone = hits.reshape(nr, tile_rows, nc, tile_cols, HITS).transpose(0, 2, 1, 3, 4)
    everyone = everyone.reshape(nr, 2, 2, nx, pairs)
    group = lax.dynamic_index_in_dim(everyone, zh, 1, keepdims=False).reshape(peers, pairs)
    storage = jnp.sum(
        jnp.where(group[:, :, None] == jnp.arange(blocks, dtype=i32), block_slot, 0), axis=2
    )
    owner = storage // blk_dev
    local = storage % blk_dev
    owner_z = (owner % nc) // nx
    owner_zh = owner_z // 2
    owner_zl = owner_z % 2
    side = jnp.where(owner_zh == zh, owner_zl, 1 - owner_zl)
    peer = ((owner // nc) * 2 + side) * nx + owner % nx
    place = owner_zh * blk_dev + local
    earlier = jnp.arange(pairs)[None, :] < jnp.arange(pairs)[:, None]
    ranking = jnp.sum(
        ((peer[:, :, None] == peer[:, None, :]) & earlier[None]).astype(i32), axis=2
    )
    me = (row * 2 + zl) * nx + x
    my_hits = lax.dynamic_index_in_dim(group, me, 0, keepdims=False)
    send_slot = lax.dynamic_index_in_dim(peer * cap + ranking, me, 0, keepdims=False)
    matched = (peer[:, None, :] == me) & (
        ranking[:, None, :] == jnp.arange(cap, dtype=i32)[None, :, None]
    )
    table = dense + jnp.sum(jnp.where(matched, place[:, None, :] - dense, 0), axis=2)
    table = table.reshape(slots)
    mat_idx = (my_hits // blk_ang) * spots + offsets.reshape(pairs)

    my_z = zh * 2 + zl
    half = jnp.arange(dense, dtype=i32) // blk_dev
    dense_z = jnp.where(half == zh, my_z, RING - 1 - my_z)
    dense_place = (row * nc + dense_z * nx + x) * blk_dev + jnp.arange(dense, dtype=i32) % blk_dev
    number = jnp.arange(blocks, dtype=i32)
    active = (
        (number % blk_ang).reshape(ANGLES, blk_ang) < angle_count[:, None]
    ).reshape(1, blocks)
    used = jnp.any((block_slot[None, :] == dense_place[:, None]) & active, axis=1).astype(i32)
    used = jnp.concatenate([used, jnp.full((1,), zh * blk_dev, i32)])

    taps = kernel[::-1, ::-1].transpose(0, 1, 3, 2).reshape(3, 3 * chans, chans)
    blank = jnp.zeros_like(taps[:1])
    taps = jnp.concatenate(
        [jnp.concatenate([taps, blank]), jnp.concatenate([blank, taps])], axis=2
    ).reshape(4 * 3 * chans, 2 * chans)
    rays = ray_matrix.reshape(angles * spots, bins, tile_pix)

    block = (bins, chans)
    shape = jax.ShapeDtypeStruct
    slot_out = shape((slots,) + block, bf16)
    edges = (
        shape(state.shape, bf16),
        shape((cols_dev, chans), bf16),
        shape((cols_dev, chans), bf16),
        shape((rows_dev, chans), bf16),
        shape((rows_dev, chans), bf16),
    )

    def limit(mib):
        return pltpu.CompilerParams(vmem_limit_bytes=mib << 20)

    start = pl.pallas_call(
        start_kernel,
        out_shape=edges[0],
        in_specs=[VMEM] * 2,
        out_specs=VMEM,
        compiler_params=limit(8),
        name="start",
    )
    sides = pl.pallas_call(
        sides_kernel,
        out_shape=[shape((rows_dev + 16, chans), f32)] * 2,
        in_specs=[VMEM] * 4,
        out_specs=[VMEM] * 2,
        compiler_params=limit(4),
        name="sides",
    )
    pulled_out = shape((tiles, PIX // 2, 2, PIX, chans), f32)
    cols3_out = shape(((rows_dev + 2) // 2, 2, cols_dev, 3 * chans), bf16)
    macs = tiles * tile_pix * chans * (9 * chans + HITS * bins)

    def cost(share):
        return pl.CostEstimate(
            flops=2 * macs * share // tiles, bytes_accessed=rays.size * 2, transcendentals=0
        )

    inner = pl.pallas_call(
        functools.partial(inner_kernel, tile_cols=tile_cols),
        out_shape=(pulled_out, slot_out, cols3_out),
        in_specs=[SMEM] * 2 + [VMEM] * 5,
        out_specs=(VMEM,) * 3,
        scratch_shapes=[pltpu.VMEM((rows_dev + 2, cols_dev + 16, chans), f32)],
        compiler_params=limit(16),
        cost_estimate=cost(len(tiles_at(tiles, tile_cols, True))),
        name="inner",
    )
    outer = pl.pallas_call(
        functools.partial(outer_kernel, tile_cols=tile_cols),
        out_shape=(pulled_out, slot_out, cols3_out),
        in_specs=[SMEM] * 2 + [VMEM] * 7,
        out_specs=(VMEM,) * 3,
        input_output_aliases={6: 0, 7: 1, 8: 2},
        compiler_params=limit(16),
        cost_estimate=cost(len(tiles_at(tiles, tile_cols, False))),
        name="outer",
    )
    combine = pl.pallas_call(
        combine_kernel,
        out_shape=(shape((dense,) + block, f32), shape((dense,) + block, bf16)),
        in_specs=[SMEM, VMEM],
        out_specs=(VMEM, VMEM),
        scratch_shapes=[pltpu.VMEM((dense + 1,) + block, f32)],
        compiler_params=limit(8),
        name="combine",
    )
    reply = pl.pallas_call(
        reply_kernel,
        out_shape=slot_out,
        in_specs=[SMEM] * 2 + [VMEM] * 4,
        out_specs=VMEM,
        scratch_shapes=[pltpu.VMEM((dense + 1,) + block, bf16)],
        compiler_params=limit(8),
        name="reply",
    )

    def finish(last):
        return pl.pallas_call(
            functools.partial(finish_kernel, tile_cols=tile_cols, last=last),
            out_shape=(shape(state.shape, f32),) if last else edges,
            in_specs=[SMEM] * 2 + [VMEM] * 5,
            out_specs=(pl.BlockSpec(memory_space=pl.ANY),) if last else (VMEM,) * 5,
            scratch_shapes=[
                pltpu.VMEM(state.shape, f32),
                pltpu.SemaphoreType.DMA((tiles,)),
            ],
            compiler_params=limit(20),
            name="finish",
        )

    def across(value):
        value = value.reshape((peers, cap) + block)
        value = lax.all_to_all(value, GROUP, split_axis=0, concat_axis=0, tiled=True)
        return value.reshape((slots,) + block)

    up = [(i, i + 1) for i in range(nr - 1)]
    down = [(b, a) for a, b in up]
    rightward = [(i, i + 1) for i in range(nc - 1)]
    leftward = [(b, a) for a, b in rightward]

    def forward(scaled, top, bottom, left, right):
        above = lax.ppermute(bottom, "row", up)
        below = lax.ppermute(top, "row", down)
        first, last = sides(above, below, left, right)
        lefts = lax.ppermute(last, COL, rightward)
        rights = lax.ppermute(first, COL, leftward)
        parts = inner(mat_idx, send_slot, scaled, above, below, taps, rays)
        return outer(mat_idx, send_slot, lefts, rights, taps, rays, *parts)[:2]

    def scale(state, grad):
        value = 1.0 - jnp.square(state.astype(f32))
        return (value * grad.astype(f32)).astype(bf16)

    other_weight = exchange(ray_weight)
    scaled = start(state, grad)
    rim = (
        scale(state[0], grad[0]),
        scale(state[rows_dev - 1], grad[rows_dev - 1]),
        scale(state[:, 0], grad[:, 0]),
        scale(state[:, cols_dev - 1], grad[:, cols_dev - 1]),
    )
    for turn in range(ITERS):
        pulled, outgoing = forward(scaled, *rim)
        if not turn:
            outgoing, table, used, other_weight = lax.optimization_barrier(
                (outgoing, table, used, other_weight)
            )
        total, mine = combine(table, across(outgoing))
        replies = reply(table, used, total, exchange(mine), ray_weight, other_weight)
        last = turn == ITERS - 1
        scaled, *rim = finish(last)(
            mat_idx, send_slot, across(replies), pulled, grad, state, rays
        )
    return scaled


def solution(mesh):
    nr, nc = mesh.devices.shape
    fine = Mesh(mesh.devices.reshape(nr, 2, RING // 2, nc // RING), ("row",) + COL)
    image = P("row", COL, None)
    placed = (
        image,
        image,
        P(),
        P(),
        P(("row",) + COL, None, None),
        P(),
        image,
        P(),
        P(),
    )
    return jax.shard_map(
        on_device, mesh=fine, in_specs=placed, out_specs=image, check_vma=False
    )
```

```python
import functools

import jax
import jax.numpy as jnp
from jax import lax
from jax.experimental import pallas as pl
from jax.experimental.pallas import tpu as pltpu
from jax.sharding import Mesh, PartitionSpec as P

PIX = 32
ANGLES = 8
HITS = 16
ITERS = 2
RING = 4

relax_rate = 0.25

COL = ("zh", "zl", "x")
GROUP = ("row", "zl", "x")

VMEM = pl.BlockSpec(memory_space=pltpu.VMEM)
SMEM = pl.BlockSpec(memory_space=pltpu.SMEM)
ANY = pl.BlockSpec(memory_space=pl.ANY)


def start_kernel(state, grad, scaled, top, bottom, left, right, states, grads, whole, mark):
    parts = mark.shape[1]
    rows = states.shape[0] // parts

    def load(a, p):
        source, held = ((state, states), (grad, grads))[a]
        where = pl.ds(p * rows, rows)
        return pltpu.make_async_copy(source.at[where], held.at[where], mark.at[a, p])

    for p in range(parts):
        for a in range(2):
            load(a, p).start()
    for p in range(parts):
        for a in range(2):
            load(a, p).wait()
        where = slice(p * rows, (p + 1) * rows)
        value = states[where].astype(jnp.float32)
        whole[where] = (1.0 - value * value) * grads[where].astype(jnp.float32)
    emit_edges(whole[...], scaled, top, bottom, left, right)


def emit_edges(value, scaled, top, bottom, left, right):
    rows, cols = value.shape[:2]
    scaled[...] = value.astype(jnp.bfloat16)
    top[...] = scaled[0]
    bottom[...] = scaled[rows - 1]
    left[...] = value[:, 0, :].astype(jnp.bfloat16)
    right[...] = value[:, cols - 1, :].astype(jnp.bfloat16)


def sides_kernel(above, below, left, right, first, last):
    rows = left.shape[0]
    cols = above.shape[0]
    f32 = jnp.float32
    for out, edge, at in ((first, left, 0), (last, right, cols - 1)):
        group = at // 16 * 16
        corner_a = above[group : group + 16, :].astype(f32)[at - group : at - group + 1, :]
        corner_b = below[group : group + 16, :].astype(f32)[at - group : at - group + 1, :]
        out[8 : 8 + rows, :] = edge[...].astype(f32)
        out[7:8, :] = corner_a
        out[8 + rows : 9 + rows, :] = corner_b


def matrices_of(mat_idx, rays, t):
    return jnp.concatenate([rays[mat_idx[t * HITS + k]] for k in range(HITS)], axis=0)


def forward_tile(
    mat_idx, send_slot, taps, rays, pulled, out, cols3, t, tile_cols, waiting=()
):
    chans = pulled.shape[-1]
    bins = rays.shape[1]
    half = PIX // 2
    r0, c0 = t // tile_cols * half, t % tile_cols * PIX
    window = jnp.concatenate(
        [
            cols3[r0 + dr // 2 : r0 + dr // 2 + half, dr % 2, c0 : c0 + PIX, :].reshape(
                half * PIX, 3 * chans
            )
            for dr in range(4)
        ],
        axis=1,
    )
    acc = jnp.dot(window, taps[...], preferred_element_type=jnp.float32)
    for odd in range(2):
        value = acc[:, odd * chans : (odd + 1) * chans].reshape(half, PIX, chans)
        pulled[t, :, odd] = value
    low = pulled[t].reshape(PIX * PIX, chans).astype(jnp.bfloat16)
    while waiting:
        waiting.pop().wait()
    value = jnp.dot(
        matrices_of(mat_idx, rays, t), low, preferred_element_type=jnp.float32
    ).astype(jnp.bfloat16)
    for k in range(HITS):
        out[send_slot[t * HITS + k]] = value[k * bins : (k + 1) * bins, :]


def tiles_at(tiles, tile_cols, inner):
    return [t for t in range(tiles) if (0 < t % tile_cols < tile_cols - 1) == inner]


def inner_kernel(
    mat_idx, send_slot, scaled, above, below, kernel, rays, pulled, out, cols3, taps, *refs,
    tile_cols,
):
    wide = refs[-1]
    rows, cols, chans = scaled.shape
    f32, bf16 = jnp.float32, jnp.bfloat16
    load = None
    if len(refs) > 1:
        held, mark = refs[:2]
        load = pltpu.make_async_copy(rays, held, mark.at[0])
        load.start()
        rays = held
    blank = jnp.zeros((3 * chans, chans), bf16)
    for dr in range(4):
        base = dr * 3 * chans
        for side in range(2):
            lanes = slice(side * chans, (side + 1) * chans)
            tap = dr - side
            if not 0 <= tap < 3:
                taps[base : base + 3 * chans, lanes] = blank
                continue
            for dc in range(3):
                taps[base + dc * chans : base + (dc + 1) * chans, lanes] = kernel[2 - tap, 2 - dc].T
    wide[0, 8 : 8 + cols, :] = above[...].astype(f32)
    wide[rows + 1, 8 : 8 + cols, :] = below[...].astype(f32)
    wide[1 : rows + 1, 8 : 8 + cols, :] = scaled[...].astype(f32)
    wide[:, 0:8, :] = jnp.zeros((rows + 2, 8, chans), f32)
    wide[:, 8 + cols :, :] = jnp.zeros((rows + 2, 8, chans), f32)
    for dc in range(3):
        value = wide[:, 7 + dc : 7 + dc + cols, :].astype(bf16)
        cols3[:, :, :, dc * chans : (dc + 1) * chans] = value.reshape(
            (rows + 2) // 2, 2, cols, chans
        )
    out[...] = jnp.zeros_like(out)
    waiting = [load] if load is not None else []
    for t in tiles_at(pulled.shape[0], tile_cols, True):
        forward_tile(mat_idx, send_slot, taps, rays, pulled, out, cols3, t, tile_cols, waiting)
    while waiting:
        waiting.pop().wait()


def outer_kernel(
    mat_idx, send_slot, left, right, taps, rays, _pulled, _out, _cols3,
    pulled, out, cols3, *, tile_cols,
):
    cols = cols3.shape[2]
    chans = pulled.shape[-1]
    group = 16
    spot = lax.broadcasted_iota(jnp.int32, (group, chans), 0)
    for edge, dc, first, at in ((left, 0, 0, 0), (right, 2, cols - group, group - 1)):
        lanes = slice(dc * chans, (dc + 1) * chans)
        for r in range(2 * cols3.shape[0]):
            there = (r // 2, r % 2, slice(first, first + group), lanes)
            value = jnp.where(spot == at, edge[7 + r : 8 + r, :], cols3[there].astype(jnp.float32))
            cols3[there] = value.astype(jnp.bfloat16)
    for t in tiles_at(pulled.shape[0], tile_cols, False):
        forward_tile(mat_idx, send_slot, taps, rays, pulled, out, cols3, t, tile_cols)


def combine_kernel(table, recv, total, low, acc):
    acc[...] = jnp.zeros_like(acc)

    def body(j, carry):
        acc[table[j]] += recv[j].astype(jnp.float32)
        return carry

    lax.fori_loop(0, recv.shape[0], body, 0, unroll=8)
    total[...] = acc[: total.shape[0]]
    low[...] = acc[: total.shape[0]].astype(jnp.bfloat16)


def reply_kernel(table, used, total, other, own_weight, other_weight, out, held):
    n = total.shape[0]
    own = own_weight.shape[0]
    place = used[n]
    for half, weight in enumerate((own_weight, other_weight)):
        first = jnp.where(half == 0, place, n - own - place)
        for b in range(own):
            d = first + b
            scale = used[d].astype(jnp.float32) * weight[b]
            value = total[d] + other[d].astype(jnp.float32)
            held[d] = (scale * value).astype(jnp.bfloat16)
    held[n] = jnp.zeros(held.shape[1:], jnp.bfloat16)

    def body(j, carry):
        out[j] = held[table[j]]
        return carry

    lax.fori_loop(0, out.shape[0], body, 0, unroll=8)


def finish_kernel(
    mat_idx, send_slot, returned, pulled, grad, state, rays, *refs, tile_cols, last,
):
    outs, (whole, mark) = refs[:-2], refs[-2:]
    tiles = pulled.shape[0]
    chans = grad.shape[2]
    f32 = jnp.float32

    def place(t):
        r0, c0 = t // tile_cols * PIX, t % tile_cols * PIX
        return slice(r0, r0 + PIX), slice(c0, c0 + PIX)

    def leave(t):
        where = place(t)
        return pltpu.make_async_copy(whole.at[where], outs[0].at[where], mark.at[t])

    for t in range(tiles):
        picked = jnp.concatenate([returned[send_slot[t * HITS + k]] for k in range(HITS)], axis=0)
        backed = lax.dot_general(
            picked,
            matrices_of(mat_idx, rays, t),
            (((0,), (0,)), ((), ())),
            preferred_element_type=f32,
        ).T
        change = pulled[t].reshape(backed.shape) - relax_rate * backed
        where = place(t)
        adjoint = grad[where].astype(f32) + change.reshape(PIX, PIX, chans)
        if last:
            whole[where] = adjoint
            leave(t).start()
        else:
            value = state[where].astype(f32)
            whole[where] = (1.0 - value * value) * adjoint
    if last:
        for t in range(tiles):
            leave(t).wait()
    else:
        emit_edges(whole[...], *outs)


def on_device(state, grad, kernel, ray_matrix, ray_weight, hits, offsets, block_slot, angle_count):
    f32, bf16, i32 = jnp.float32, jnp.bfloat16, jnp.int32
    rows_dev, cols_dev, chans = state.shape
    angles, spots, bins, tile_pix = ray_matrix.shape
    nr = lax.axis_size("row")
    nx = lax.axis_size("x")
    nc = lax.axis_size(COL)
    devices = nr * nc
    row, zh, zl, x = (lax.axis_index(a) for a in ("row",) + COL)
    tile_rows = rows_dev // PIX
    tile_cols = cols_dev // PIX
    tiles = tile_rows * tile_cols
    pairs = tiles * HITS
    blk_dev = ray_weight.shape[0]
    blocks = blk_dev * devices
    blk_ang = blocks // ANGLES
    cap = 2 * max(2, (pairs + devices - 2) // devices + 1)
    cap = min(cap, pairs)
    peers = nr * 2 * nx
    slots = peers * cap
    dense = 2 * blk_dev
    swap = [(z, RING - 1 - z) for z in range(RING)]

    def exchange(value):
        return lax.ppermute(value, ("zh", "zl"), swap)

    everyone = hits.reshape(nr, tile_rows, nc, tile_cols, HITS).transpose(0, 2, 1, 3, 4)
    everyone = everyone.reshape(nr, 2, 2, nx, pairs)
    group = lax.dynamic_index_in_dim(everyone, zh, 1, keepdims=False).reshape(peers, pairs)
    storage = jnp.sum(
        jnp.where(group[:, :, None] == jnp.arange(blocks, dtype=i32), block_slot, 0), axis=2
    )
    owner = storage // blk_dev
    local = storage % blk_dev
    owner_z = (owner % nc) // nx
    owner_zh = owner_z // 2
    owner_zl = owner_z % 2
    side = jnp.where(owner_zh == zh, owner_zl, 1 - owner_zl)
    peer = ((owner // nc) * 2 + side) * nx + owner % nx
    place = owner_zh * blk_dev + local
    earlier = jnp.arange(pairs)[None, :] < jnp.arange(pairs)[:, None]
    ranking = jnp.sum(
        ((peer[:, :, None] == peer[:, None, :]) & earlier[None]).astype(i32), axis=2
    )
    me = (row * 2 + zl) * nx + x
    my_hits = lax.dynamic_index_in_dim(group, me, 0, keepdims=False)
    send_slot = lax.dynamic_index_in_dim(peer * cap + ranking, me, 0, keepdims=False)
    matched = (peer[:, None, :] == me) & (
        ranking[:, None, :] == jnp.arange(cap, dtype=i32)[None, :, None]
    )
    table = dense + jnp.sum(jnp.where(matched, place[:, None, :] - dense, 0), axis=2)
    table = table.reshape(slots)
    mat_idx = (my_hits // blk_ang) * spots + offsets.reshape(pairs)

    my_z = zh * 2 + zl
    half = jnp.arange(dense, dtype=i32) // blk_dev
    dense_z = jnp.where(half == zh, my_z, RING - 1 - my_z)
    dense_place = (row * nc + dense_z * nx + x) * blk_dev + jnp.arange(dense, dtype=i32) % blk_dev
    number = jnp.arange(blocks, dtype=i32)
    active = (
        (number % blk_ang).reshape(ANGLES, blk_ang) < angle_count[:, None]
    ).reshape(1, blocks)
    used = jnp.any((block_slot[None, :] == dense_place[:, None]) & active, axis=1).astype(i32)
    used = jnp.concatenate([used, jnp.full((1,), zh * blk_dev, i32)])

    rays = ray_matrix.reshape(angles * spots, bins, tile_pix)

    block = (bins, chans)
    shape = jax.ShapeDtypeStruct
    slot_out = shape((slots,) + block, bf16)
    edges = (
        shape(state.shape, bf16),
        shape((cols_dev, chans), bf16),
        shape((cols_dev, chans), bf16),
        shape((rows_dev, chans), bf16),
        shape((rows_dev, chans), bf16),
    )

    def limit(mib):
        return pltpu.CompilerParams(vmem_limit_bytes=mib << 20)

    start = pl.pallas_call(
        start_kernel,
        out_shape=edges,
        in_specs=[ANY] * 2,
        out_specs=(VMEM,) * 5,
        scratch_shapes=[
            pltpu.VMEM(state.shape, bf16),
            pltpu.VMEM(state.shape, bf16),
            pltpu.VMEM(state.shape, f32),
            pltpu.SemaphoreType.DMA((2, 4)),
        ],
        compiler_params=limit(8),
        name="start",
    )
    sides = pl.pallas_call(
        sides_kernel,
        out_shape=[shape((rows_dev + 16, chans), f32)] * 2,
        in_specs=[VMEM] * 4,
        out_specs=[VMEM] * 2,
        compiler_params=limit(4),
        name="sides",
    )
    pulled_out = shape((tiles, PIX // 2, 2, PIX, chans), f32)
    cols3_out = shape(((rows_dev + 2) // 2, 2, cols_dev, 3 * chans), bf16)
    macs = tiles * tile_pix * chans * (9 * chans + HITS * bins)

    def cost(share):
        return pl.CostEstimate(
            flops=2 * macs * share // tiles, bytes_accessed=rays.size * 2, transcendentals=0
        )

    taps_out = shape((4 * 3 * chans, 2 * chans), bf16)

    def inner(early):
        held = (shape(rays.shape, bf16),) if early else ()
        mark = [pltpu.SemaphoreType.DMA((1,))] if early else []
        return pl.pallas_call(
            functools.partial(inner_kernel, tile_cols=tile_cols),
            out_shape=(pulled_out, slot_out, cols3_out, taps_out) + held,
            in_specs=[SMEM] * 2 + [VMEM] * 4 + [ANY if early else VMEM],
            out_specs=(VMEM,) * (4 + len(held)),
            scratch_shapes=mark + [pltpu.VMEM((rows_dev + 2, cols_dev + 16, chans), f32)],
            compiler_params=limit(16),
            cost_estimate=cost(len(tiles_at(tiles, tile_cols, True))),
            name="inner",
        )

    outer = pl.pallas_call(
        functools.partial(outer_kernel, tile_cols=tile_cols),
        out_shape=(pulled_out, slot_out, cols3_out),
        in_specs=[SMEM] * 2 + [VMEM] * 7,
        out_specs=(VMEM,) * 3,
        input_output_aliases={6: 0, 7: 1, 8: 2},
        compiler_params=limit(16),
        cost_estimate=cost(len(tiles_at(tiles, tile_cols, False))),
        name="outer",
    )
    combine = pl.pallas_call(
        combine_kernel,
        out_shape=(shape((dense,) + block, f32), shape((dense,) + block, bf16)),
        in_specs=[SMEM, VMEM],
        out_specs=(VMEM, VMEM),
        scratch_shapes=[pltpu.VMEM((dense + 1,) + block, f32)],
        compiler_params=limit(8),
        name="combine",
    )
    reply = pl.pallas_call(
        reply_kernel,
        out_shape=slot_out,
        in_specs=[SMEM] * 2 + [VMEM] * 4,
        out_specs=VMEM,
        scratch_shapes=[pltpu.VMEM((dense + 1,) + block, bf16)],
        compiler_params=limit(8),
        name="reply",
    )

    def finish(last):
        return pl.pallas_call(
            functools.partial(finish_kernel, tile_cols=tile_cols, last=last),
            out_shape=(shape(state.shape, f32),) if last else edges,
            in_specs=[SMEM] * 2 + [VMEM] * 5,
            out_specs=(pl.BlockSpec(memory_space=pl.ANY),) if last else (VMEM,) * 5,
            scratch_shapes=[
                pltpu.VMEM(state.shape, f32),
                pltpu.SemaphoreType.DMA((tiles,)),
            ],
            compiler_params=limit(20),
            name="finish",
        )

    def across(value):
        value = value.reshape((peers, cap) + block)
        value = lax.all_to_all(value, GROUP, split_axis=0, concat_axis=0, tiled=True)
        return value.reshape((slots,) + block)

    up = [(i, i + 1) for i in range(nr - 1)]
    down = [(b, a) for a, b in up]
    rightward = [(i, i + 1) for i in range(nc - 1)]
    leftward = [(b, a) for a, b in rightward]

    def apart(value):
        return pltpu.with_memory_space_constraint(value, pltpu.HBM)

    def forward(early, scaled, top, bottom, left, right):
        above = lax.ppermute(bottom, "row", up)
        below = lax.ppermute(top, "row", down)
        first, last = sides(above, below, left, right)
        lefts = lax.ppermute(last, COL, rightward)
        rights = lax.ppermute(first, COL, leftward)
        *parts, taps = inner(early)(
            mat_idx, send_slot, scaled, above, below, kernel, apart(rays) if early else rays
        )[: 4 + early]
        near = rays
        if early:
            near, taps = taps, parts.pop()
        return outer(mat_idx, send_slot, lefts, rights, taps, near, *parts)[:2]

    scaled, *rim = start(apart(state), apart(grad))
    for turn in range(ITERS):
        pulled, outgoing = forward(turn == 0, scaled, *rim)
        if not turn:
            outgoing, weight = lax.optimization_barrier((outgoing, ray_weight))
            other_weight = exchange(weight)
        total, mine = combine(table, across(outgoing))
        replies = reply(table, used, total, exchange(mine), ray_weight, other_weight)
        last = turn == ITERS - 1
        scaled, *rim = finish(last)(
            mat_idx, send_slot, across(replies), pulled, grad, state, rays
        )
    return scaled


def solution(mesh):
    nr, nc = mesh.devices.shape
    fine = Mesh(mesh.devices.reshape(nr, 2, RING // 2, nc // RING), ("row",) + COL)
    image = P("row", COL, None)
    placed = (
        image,
        image,
        P(),
        P(),
        P(("row",) + COL, None, None),
        P(),
        image,
        P(),
        P(),
    )
    return jax.shard_map(
        on_device, mesh=fine, in_specs=placed, out_specs=image, check_vma=False
    )
```

```python
import functools

import jax
import jax.numpy as jnp
from jax import lax
from jax.experimental import pallas as pl
from jax.experimental.pallas import tpu as pltpu
from jax.sharding import Mesh, PartitionSpec as P

PIX = 32
ANGLES = 8
HITS = 16
ITERS = 2
RING = 4

relax_rate = 0.25

COL = ("zh", "zl", "x")
GROUP = ("row", "zl", "x")

VMEM = pl.BlockSpec(memory_space=pltpu.VMEM)
SMEM = pl.BlockSpec(memory_space=pltpu.SMEM)
ANY = pl.BlockSpec(memory_space=pl.ANY)


def start_kernel(state, grad, scaled, top, bottom, left, right, states, grads, whole, mark):
    parts = mark.shape[1]
    rows = states.shape[0] // parts

    def load(a, p):
        source, held = ((state, states), (grad, grads))[a]
        where = pl.ds(p * rows, rows)
        return pltpu.make_async_copy(source.at[where], held.at[where], mark.at[a, p])

    for p in range(parts):
        for a in range(2):
            load(a, p).start()
    for p in range(parts):
        for a in range(2):
            load(a, p).wait()
        where = slice(p * rows, (p + 1) * rows)
        value = states[where].astype(jnp.float32)
        whole[where] = (1.0 - value * value) * grads[where].astype(jnp.float32)
    emit_edges(whole[...], scaled, top, bottom, left, right)


def emit_edges(value, scaled, top, bottom, left, right):
    rows, cols = value.shape[:2]
    scaled[...] = value.astype(jnp.bfloat16)
    top[...] = scaled[0]
    bottom[...] = scaled[rows - 1]
    left[...] = value[:, 0, :].astype(jnp.bfloat16)
    right[...] = value[:, cols - 1, :].astype(jnp.bfloat16)


def sides_kernel(above, below, left, right, first, last):
    rows = left.shape[0]
    cols = above.shape[0]
    f32 = jnp.float32
    for out, edge, at in ((first, left, 0), (last, right, cols - 1)):
        group = at // 16 * 16
        corner_a = above[group : group + 16, :].astype(f32)[at - group : at - group + 1, :]
        corner_b = below[group : group + 16, :].astype(f32)[at - group : at - group + 1, :]
        out[8 : 8 + rows, :] = edge[...].astype(f32)
        out[7:8, :] = corner_a
        out[8 + rows : 9 + rows, :] = corner_b


def matrices_of(mat_idx, rays, t):
    return jnp.concatenate([rays[mat_idx[t * HITS + k]] for k in range(HITS)], axis=0)


def forward_tile(
    mat_idx, send_slot, taps, rays, pulled, out, cols3, t, tile_cols, waiting=()
):
    chans = pulled.shape[-1]
    bins = rays.shape[1]
    half = PIX // 2
    r0, c0 = t // tile_cols * half, t % tile_cols * PIX
    window = jnp.concatenate(
        [
            cols3[r0 + dr // 2 : r0 + dr // 2 + half, dr % 2, c0 : c0 + PIX, :].reshape(
                half * PIX, 3 * chans
            )
            for dr in range(4)
        ],
        axis=1,
    )
    acc = jnp.dot(window, taps[...], preferred_element_type=jnp.float32)
    for odd in range(2):
        value = acc[:, odd * chans : (odd + 1) * chans].reshape(half, PIX, chans)
        pulled[t, :, odd] = value
    low = pulled[t].reshape(PIX * PIX, chans).astype(jnp.bfloat16)
    while waiting:
        waiting.pop().wait()
    value = jnp.dot(
        matrices_of(mat_idx, rays, t), low, preferred_element_type=jnp.float32
    ).astype(jnp.bfloat16)
    for k in range(HITS):
        out[send_slot[t * HITS + k]] = value[k * bins : (k + 1) * bins, :]


def tiles_at(tiles, tile_cols, inner):
    return [t for t in range(tiles) if (0 < t % tile_cols < tile_cols - 1) == inner]


def inner_kernel(
    mat_idx, send_slot, scaled, above, below, kernel, rays, pulled, out, cols3, taps, *refs,
    tile_cols,
):
    wide = refs[-1]
    rows, cols, chans = scaled.shape
    f32, bf16 = jnp.float32, jnp.bfloat16
    load = None
    if len(refs) > 1:
        held, mark = refs[:2]
        load = pltpu.make_async_copy(rays, held, mark.at[0])
        load.start()
        rays = held
    blank = jnp.zeros((3 * chans, chans), bf16)
    for dr in range(4):
        base = dr * 3 * chans
        for side in range(2):
            lanes = slice(side * chans, (side + 1) * chans)
            tap = dr - side
            if not 0 <= tap < 3:
                taps[base : base + 3 * chans, lanes] = blank
                continue
            for dc in range(3):
                taps[base + dc * chans : base + (dc + 1) * chans, lanes] = kernel[2 - tap, 2 - dc].T
    wide[0, 8 : 8 + cols, :] = above[...].astype(f32)
    wide[rows + 1, 8 : 8 + cols, :] = below[...].astype(f32)
    wide[1 : rows + 1, 8 : 8 + cols, :] = scaled[...].astype(f32)
    wide[:, 0:8, :] = jnp.zeros((rows + 2, 8, chans), f32)
    wide[:, 8 + cols :, :] = jnp.zeros((rows + 2, 8, chans), f32)
    for dc in range(3):
        value = wide[:, 7 + dc : 7 + dc + cols, :].astype(bf16)
        cols3[:, :, :, dc * chans : (dc + 1) * chans] = value.reshape(
            (rows + 2) // 2, 2, cols, chans
        )
    out[...] = jnp.zeros_like(out)
    waiting = [load] if load is not None else []
    for t in tiles_at(pulled.shape[0], tile_cols, True):
        forward_tile(mat_idx, send_slot, taps, rays, pulled, out, cols3, t, tile_cols, waiting)
    while waiting:
        waiting.pop().wait()


def outer_kernel(
    mat_idx, send_slot, left, right, taps, rays, _pulled, _out, _cols3,
    pulled, out, cols3, *, tile_cols,
):
    cols = cols3.shape[2]
    chans = pulled.shape[-1]
    group = 16
    spot = lax.broadcasted_iota(jnp.int32, (group, chans), 0)
    for edge, dc, first, at in ((left, 0, 0, 0), (right, 2, cols - group, group - 1)):
        lanes = slice(dc * chans, (dc + 1) * chans)
        for r in range(2 * cols3.shape[0]):
            there = (r // 2, r % 2, slice(first, first + group), lanes)
            value = jnp.where(spot == at, edge[7 + r : 8 + r, :], cols3[there].astype(jnp.float32))
            cols3[there] = value.astype(jnp.bfloat16)
    for t in tiles_at(pulled.shape[0], tile_cols, False):
        forward_tile(mat_idx, send_slot, taps, rays, pulled, out, cols3, t, tile_cols)


def combine_kernel(table, recv, total, low, acc):
    acc[...] = jnp.zeros_like(acc)

    def body(j, carry):
        acc[table[j]] += recv[j].astype(jnp.float32)
        return carry

    lax.fori_loop(0, recv.shape[0], body, 0, unroll=8)
    total[...] = acc[: total.shape[0]]
    low[...] = acc[: total.shape[0]].astype(jnp.bfloat16)


def reply_kernel(table, used, total, other, own_weight, other_weight, out, held):
    n = total.shape[0]
    own = own_weight.shape[0]
    place = used[n]
    for half, weight in enumerate((own_weight, other_weight)):
        first = jnp.where(half == 0, place, n - own - place)
        for b in range(own):
            d = first + b
            scale = used[d].astype(jnp.float32) * weight[b]
            value = total[d] + other[d].astype(jnp.float32)
            held[d] = (scale * value).astype(jnp.bfloat16)
    held[n] = jnp.zeros(held.shape[1:], jnp.bfloat16)

    def body(j, carry):
        out[j] = held[table[j]]
        return carry

    lax.fori_loop(0, out.shape[0], body, 0, unroll=8)


def finish_kernel(
    mat_idx, send_slot, returned, pulled, grad, state, rays, *refs, tile_cols, last,
):
    outs, (whole, mark) = refs[:-2], refs[-2:]
    tiles = pulled.shape[0]
    chans = grad.shape[2]
    f32 = jnp.float32

    def place(t):
        r0, c0 = t // tile_cols * PIX, t % tile_cols * PIX
        return slice(r0, r0 + PIX), slice(c0, c0 + PIX)

    def leave(t):
        where = place(t)
        return pltpu.make_async_copy(whole.at[where], outs[0].at[where], mark.at[t])

    for t in range(tiles):
        picked = jnp.concatenate([returned[send_slot[t * HITS + k]] for k in range(HITS)], axis=0)
        backed = lax.dot_general(
            picked,
            matrices_of(mat_idx, rays, t),
            (((0,), (0,)), ((), ())),
            preferred_element_type=f32,
        ).T
        change = pulled[t].reshape(backed.shape) - relax_rate * backed
        where = place(t)
        adjoint = grad[where].astype(f32) + change.reshape(PIX, PIX, chans)
        if last:
            whole[where] = adjoint
            leave(t).start()
        else:
            value = state[where].astype(f32)
            whole[where] = (1.0 - value * value) * adjoint
    if last:
        for t in range(tiles):
            leave(t).wait()
    else:
        emit_edges(whole[...], *outs)


def on_device(state, grad, kernel, ray_matrix, ray_weight, hits, offsets, block_slot, angle_count):
    f32, bf16, i32 = jnp.float32, jnp.bfloat16, jnp.int32
    rows_dev, cols_dev, chans = state.shape
    angles, spots, bins, tile_pix = ray_matrix.shape
    nr = lax.axis_size("row")
    nx = lax.axis_size("x")
    nc = lax.axis_size(COL)
    devices = nr * nc
    row, zh, zl, x = (lax.axis_index(a) for a in ("row",) + COL)
    tile_rows = rows_dev // PIX
    tile_cols = cols_dev // PIX
    tiles = tile_rows * tile_cols
    pairs = tiles * HITS
    blk_dev = ray_weight.shape[0]
    blocks = blk_dev * devices
    blk_ang = blocks // ANGLES
    cap = 2 * max(2, (pairs + devices - 2) // devices + 1)
    cap = min(cap, pairs)
    peers = nr * 2 * nx
    slots = peers * cap
    dense = 2 * blk_dev
    swap = [(z, RING - 1 - z) for z in range(RING)]

    def exchange(value):
        return lax.ppermute(value, ("zh", "zl"), swap)

    everyone = hits.reshape(nr, tile_rows, nc, tile_cols, HITS).transpose(0, 2, 1, 3, 4)
    everyone = everyone.reshape(nr, 2, 2, nx, pairs)
    group = lax.dynamic_index_in_dim(everyone, zh, 1, keepdims=False).reshape(peers, pairs)
    storage = jnp.sum(
        jnp.where(group[:, :, None] == jnp.arange(blocks, dtype=i32), block_slot, 0), axis=2
    )
    owner = storage // blk_dev
    local = storage % blk_dev
    owner_z = (owner % nc) // nx
    owner_zh = owner_z // 2
    owner_zl = owner_z % 2
    side = jnp.where(owner_zh == zh, owner_zl, 1 - owner_zl)
    peer = ((owner // nc) * 2 + side) * nx + owner % nx
    place = owner_zh * blk_dev + local
    earlier = jnp.arange(pairs)[None, :] < jnp.arange(pairs)[:, None]
    ranking = jnp.sum(
        ((peer[:, :, None] == peer[:, None, :]) & earlier[None]).astype(i32), axis=2
    )
    me = (row * 2 + zl) * nx + x
    my_hits = lax.dynamic_index_in_dim(group, me, 0, keepdims=False)
    send_slot = lax.dynamic_index_in_dim(peer * cap + ranking, me, 0, keepdims=False)
    matched = (peer[:, None, :] == me) & (
        ranking[:, None, :] == jnp.arange(cap, dtype=i32)[None, :, None]
    )
    table = dense + jnp.sum(jnp.where(matched, place[:, None, :] - dense, 0), axis=2)
    table = table.reshape(slots)
    mat_idx = (my_hits // blk_ang) * spots + offsets.reshape(pairs)

    my_z = zh * 2 + zl
    half = jnp.arange(dense, dtype=i32) // blk_dev
    dense_z = jnp.where(half == zh, my_z, RING - 1 - my_z)
    dense_place = (row * nc + dense_z * nx + x) * blk_dev + jnp.arange(dense, dtype=i32) % blk_dev
    number = jnp.arange(blocks, dtype=i32)
    active = (
        (number % blk_ang).reshape(ANGLES, blk_ang) < angle_count[:, None]
    ).reshape(1, blocks)
    used = jnp.any((block_slot[None, :] == dense_place[:, None]) & active, axis=1).astype(i32)
    used = jnp.concatenate([used, jnp.full((1,), zh * blk_dev, i32)])

    rays = ray_matrix.reshape(angles * spots, bins, tile_pix)

    block = (bins, chans)
    shape = jax.ShapeDtypeStruct
    slot_out = shape((slots,) + block, bf16)
    edges = (
        shape(state.shape, bf16),
        shape((cols_dev, chans), bf16),
        shape((cols_dev, chans), bf16),
        shape((rows_dev, chans), bf16),
        shape((rows_dev, chans), bf16),
    )

    def limit(mib):
        return pltpu.CompilerParams(vmem_limit_bytes=mib << 20)

    start = pl.pallas_call(
        start_kernel,
        out_shape=edges,
        in_specs=[ANY] * 2,
        out_specs=(VMEM,) * 5,
        scratch_shapes=[
            pltpu.VMEM(state.shape, bf16),
            pltpu.VMEM(state.shape, bf16),
            pltpu.VMEM(state.shape, f32),
            pltpu.SemaphoreType.DMA((2, 4)),
        ],
        compiler_params=limit(8),
        name="start",
    )
    sides = pl.pallas_call(
        sides_kernel,
        out_shape=[shape((rows_dev + 16, chans), f32)] * 2,
        in_specs=[VMEM] * 4,
        out_specs=[VMEM] * 2,
        compiler_params=limit(4),
        name="sides",
    )
    pulled_out = shape((tiles, PIX // 2, 2, PIX, chans), f32)
    cols3_out = shape(((rows_dev + 2) // 2, 2, cols_dev, 3 * chans), bf16)
    macs = tiles * tile_pix * chans * (9 * chans + HITS * bins)

    def cost(share):
        return pl.CostEstimate(
            flops=2 * macs * share // tiles, bytes_accessed=rays.size * 2, transcendentals=0
        )

    taps_out = shape((4 * 3 * chans, 2 * chans), bf16)

    def inner(early):
        held = (shape(rays.shape, bf16),) if early else ()
        mark = [pltpu.SemaphoreType.DMA((1,))] if early else []
        return pl.pallas_call(
            functools.partial(inner_kernel, tile_cols=tile_cols),
            out_shape=(pulled_out, slot_out, cols3_out, taps_out) + held,
            in_specs=[SMEM] * 2 + [VMEM] * 4 + [ANY if early else VMEM],
            out_specs=(VMEM,) * (4 + len(held)),
            scratch_shapes=mark + [pltpu.VMEM((rows_dev + 2, cols_dev + 16, chans), f32)],
            compiler_params=limit(16),
            cost_estimate=cost(len(tiles_at(tiles, tile_cols, True))),
            name="inner",
        )

    outer = pl.pallas_call(
        functools.partial(outer_kernel, tile_cols=tile_cols),
        out_shape=(pulled_out, slot_out, cols3_out),
        in_specs=[SMEM] * 2 + [VMEM] * 7,
        out_specs=(VMEM,) * 3,
        input_output_aliases={6: 0, 7: 1, 8: 2},
        compiler_params=limit(16),
        cost_estimate=cost(len(tiles_at(tiles, tile_cols, False))),
        name="outer",
    )
    combine = pl.pallas_call(
        combine_kernel,
        out_shape=(shape((dense,) + block, f32), shape((dense,) + block, bf16)),
        in_specs=[SMEM, VMEM],
        out_specs=(VMEM, VMEM),
        scratch_shapes=[pltpu.VMEM((dense + 1,) + block, f32)],
        compiler_params=limit(8),
        name="combine",
    )
    reply = pl.pallas_call(
        reply_kernel,
        out_shape=slot_out,
        in_specs=[SMEM] * 2 + [VMEM] * 4,
        out_specs=VMEM,
        scratch_shapes=[pltpu.VMEM((dense + 1,) + block, bf16)],
        compiler_params=limit(8),
        name="reply",
    )

    def finish(last):
        return pl.pallas_call(
            functools.partial(finish_kernel, tile_cols=tile_cols, last=last),
            out_shape=(shape(state.shape, f32),) if last else edges,
            in_specs=[SMEM] * 2 + [VMEM] * 5,
            out_specs=(pl.BlockSpec(memory_space=pl.ANY),) if last else (VMEM,) * 5,
            scratch_shapes=[
                pltpu.VMEM(state.shape, f32),
                pltpu.SemaphoreType.DMA((tiles,)),
            ],
            compiler_params=limit(20),
            name="finish",
        )

    def across(value):
        value = value.reshape((peers, cap) + block)
        value = lax.all_to_all(value, GROUP, split_axis=0, concat_axis=0, tiled=True)
        return value.reshape((slots,) + block)

    up = [(i, i + 1) for i in range(nr - 1)]
    down = [(b, a) for a, b in up]
    rightward = [(i, i + 1) for i in range(nc - 1)]
    leftward = [(b, a) for a, b in rightward]

    def apart(value):
        return pltpu.with_memory_space_constraint(value, pltpu.HBM)

    def forward(early, scaled, top, bottom, left, right):
        above = lax.ppermute(bottom, "row", up)
        below = lax.ppermute(top, "row", down)
        first, last = sides(above, below, left, right)
        if early:
            last, weight = lax.optimization_barrier((last, ray_weight))
        lefts = lax.ppermute(last, COL, rightward)
        rights = lax.ppermute(first, COL, leftward)
        other_weight = exchange(weight) if early else None
        *parts, taps = inner(early)(
            mat_idx, send_slot, scaled, above, below, kernel, apart(rays) if early else rays
        )[: 4 + early]
        near = rays
        if early:
            near, taps = taps, parts.pop()
        pulled, outgoing, _ = outer(mat_idx, send_slot, lefts, rights, taps, near, *parts)
        return pulled, outgoing, other_weight

    scaled, *rim = start(apart(state), apart(grad))
    for turn in range(ITERS):
        pulled, outgoing, swapped = forward(turn == 0, scaled, *rim)
        if not turn:
            other_weight = swapped
            outgoing, table, used, other_weight = lax.optimization_barrier(
                (outgoing, table, used, other_weight)
            )
        total, mine = combine(table, across(outgoing))
        replies = reply(table, used, total, exchange(mine), ray_weight, other_weight)
        last = turn == ITERS - 1
        scaled, *rim = finish(last)(
            mat_idx, send_slot, across(replies), pulled, grad, state, rays
        )
    return scaled


def solution(mesh):
    nr, nc = mesh.devices.shape
    fine = Mesh(mesh.devices.reshape(nr, 2, RING // 2, nc // RING), ("row",) + COL)
    image = P("row", COL, None)
    placed = (
        image,
        image,
        P(),
        P(),
        P(("row",) + COL, None, None),
        P(),
        image,
        P(),
        P(),
    )
    return jax.shard_map(
        on_device, mesh=fine, in_specs=placed, out_specs=image, check_vma=False
    )
```

```python
import functools

import jax
import jax.numpy as jnp
from jax import lax
from jax.experimental import pallas as pl
from jax.experimental.pallas import tpu as pltpu
from jax.sharding import Mesh, PartitionSpec as P

PIX = 32
ANGLES = 8
HITS = 16
ITERS = 2
RING = 4

relax_rate = 0.25

COL = ("zh", "zl", "x")
GROUP = ("row", "zl", "x")

VMEM = pl.BlockSpec(memory_space=pltpu.VMEM)
SMEM = pl.BlockSpec(memory_space=pltpu.SMEM)
ANY = pl.BlockSpec(memory_space=pl.ANY)


def start_kernel(odd, state, grad, scaled, row_a, row_b, col_a, col_b, states, grads, whole, mark):
    parts = mark.shape[1]
    rows = states.shape[0] // parts

    def load(a, p):
        source, held = ((state, states), (grad, grads))[a]
        where = pl.ds(p * rows, rows)
        return pltpu.make_async_copy(source.at[where], held.at[where], mark.at[a, p])

    for p in range(parts):
        for a in range(2):
            load(a, p).start()
    for p in range(parts):
        for a in range(2):
            load(a, p).wait()
        where = slice(p * rows, (p + 1) * rows)
        value = states[where].astype(jnp.float32)
        whole[where] = (1.0 - value * value) * grads[where].astype(jnp.float32)
    emit_edges(whole[...], odd, scaled, row_a, row_b, col_a, col_b)


def pick(flag, yes, no):
    return jnp.where(flag == 1, yes, no)


def emit_edges(value, odd, scaled, row_a, row_b, col_a, col_b):
    rows, cols = value.shape[:2]
    scaled[...] = value.astype(jnp.bfloat16)
    row_a[...] = pick(odd[0], value[0], value[rows - 1]).astype(jnp.bfloat16)
    row_b[...] = pick(odd[0], value[rows - 1], value[0]).astype(jnp.bfloat16)
    left, right = value[:, 0, :], value[:, cols - 1, :]
    col_a[...] = pick(odd[1], left, right)
    col_b[...] = pick(odd[1], right, left)


def sides_kernel(odd, near_a, near_b, col_a, col_b, out_a, out_b):
    rows = col_a.shape[0]
    cols = near_a.shape[0]
    f32 = jnp.float32

    def ends(ref):
        low = ref[0:16, :].astype(f32)[0:1, :]
        high = ref[cols - 16 : cols, :].astype(f32)[15:16, :]
        return low, high

    a, b = ends(near_a), ends(near_b)
    above = [pick(odd[0], a[i], b[i]) for i in range(2)]
    below = [pick(odd[0], b[i], a[i]) for i in range(2)]
    for out, edge, order in ((out_a, col_a, (0, 1)), (out_b, col_b, (1, 0))):
        yes, no = order
        out[8 : 8 + rows, :] = edge[...]
        out[7:8, :] = pick(odd[1], above[yes], above[no])
        out[8 + rows : 9 + rows, :] = pick(odd[1], below[yes], below[no])


def matrices_of(mat_idx, rays, t):
    return jnp.concatenate([rays[mat_idx[t * HITS + k]] for k in range(HITS)], axis=0)


def forward_tile(
    mat_idx, send_slot, taps, rays, pulled, out, cols3, t, tile_cols, waiting=()
):
    chans = pulled.shape[-1]
    bins = rays.shape[1]
    half = PIX // 2
    r0, c0 = t // tile_cols * half, t % tile_cols * PIX
    window = jnp.concatenate(
        [
            cols3[r0 + dr // 2 : r0 + dr // 2 + half, dr % 2, c0 : c0 + PIX, :].reshape(
                half * PIX, 3 * chans
            )
            for dr in range(4)
        ],
        axis=1,
    )
    acc = jnp.dot(window, taps[...], preferred_element_type=jnp.float32)
    for odd in range(2):
        value = acc[:, odd * chans : (odd + 1) * chans].reshape(half, PIX, chans)
        pulled[t, :, odd] = value
    low = pulled[t].reshape(PIX * PIX, chans).astype(jnp.bfloat16)
    while waiting:
        waiting.pop().wait()
    value = jnp.dot(
        matrices_of(mat_idx, rays, t), low, preferred_element_type=jnp.float32
    ).astype(jnp.bfloat16)
    for k in range(HITS):
        out[send_slot[t * HITS + k]] = value[k * bins : (k + 1) * bins, :]


def tiles_at(tiles, tile_cols, inner):
    return [t for t in range(tiles) if (0 < t % tile_cols < tile_cols - 1) == inner]


def inner_kernel(
    odd, mat_idx, send_slot, scaled, near_a, near_b, kernel, rays,
    pulled, out, cols3, taps, *refs, tile_cols,
):
    wide = refs[-1]
    rows, cols, chans = scaled.shape
    f32, bf16 = jnp.float32, jnp.bfloat16
    waiting = []
    if len(refs) > 1:
        held, mark = refs[:2]
        count = rays.shape[0] // mark.shape[0]
        for i in range(mark.shape[0]):
            where = pl.ds(i * count, count)
            waiting.append(pltpu.make_async_copy(rays.at[where], held.at[where], mark.at[i]))
            waiting[-1].start()
        rays = held
    blank = jnp.zeros((3 * chans, chans), bf16)
    for dr in range(4):
        base = dr * 3 * chans
        for side in range(2):
            lanes = slice(side * chans, (side + 1) * chans)
            tap = dr - side
            if not 0 <= tap < 3:
                taps[base : base + 3 * chans, lanes] = blank
                continue
            for dc in range(3):
                taps[base + dc * chans : base + (dc + 1) * chans, lanes] = kernel[2 - tap, 2 - dc].T
    a, b = near_a[...].astype(f32), near_b[...].astype(f32)
    wide[0, 8 : 8 + cols, :] = pick(odd[0], a, b)
    wide[rows + 1, 8 : 8 + cols, :] = pick(odd[0], b, a)
    wide[1 : rows + 1, 8 : 8 + cols, :] = scaled[...].astype(f32)
    wide[:, 0:8, :] = jnp.zeros((rows + 2, 8, chans), f32)
    wide[:, 8 + cols :, :] = jnp.zeros((rows + 2, 8, chans), f32)
    for dc in range(3):
        value = wide[:, 7 + dc : 7 + dc + cols, :].astype(bf16)
        cols3[:, :, :, dc * chans : (dc + 1) * chans] = value.reshape(
            (rows + 2) // 2, 2, cols, chans
        )
    out[...] = jnp.zeros_like(out)
    for t in tiles_at(pulled.shape[0], tile_cols, True):
        forward_tile(mat_idx, send_slot, taps, rays, pulled, out, cols3, t, tile_cols, waiting)
    while waiting:
        waiting.pop().wait()


def outer_kernel(
    odd, mat_idx, send_slot, near_a, near_b, taps, rays, _pulled, _out, _cols3,
    pulled, out, cols3, *, tile_cols,
):
    cols = cols3.shape[2]
    chans = pulled.shape[-1]
    group = 16
    spot = lax.broadcasted_iota(jnp.int32, (group, chans), 0)
    a, b = near_a[...], near_b[...]
    left, right = pick(odd[1], a, b), pick(odd[1], b, a)
    for edge, dc, first, at in ((left, 0, 0, 0), (right, 2, cols - group, group - 1)):
        lanes = slice(dc * chans, (dc + 1) * chans)
        for r in range(2 * cols3.shape[0]):
            there = (r // 2, r % 2, slice(first, first + group), lanes)
            value = jnp.where(spot == at, edge[7 + r : 8 + r, :], cols3[there].astype(jnp.float32))
            cols3[there] = value.astype(jnp.bfloat16)
    for t in tiles_at(pulled.shape[0], tile_cols, False):
        forward_tile(mat_idx, send_slot, taps, rays, pulled, out, cols3, t, tile_cols)


def combine_kernel(table, recv, total, low, acc):
    acc[...] = jnp.zeros_like(acc)

    def body(j, carry):
        acc[table[j]] += recv[j].astype(jnp.float32)
        return carry

    lax.fori_loop(0, recv.shape[0], body, 0, unroll=8)
    total[...] = acc[: total.shape[0]]
    low[...] = acc[: total.shape[0]].astype(jnp.bfloat16)


def reply_kernel(table, used, total, other, own_weight, other_weight, out, held):
    n = total.shape[0]
    own = own_weight.shape[0]
    place = used[n]
    for half, weight in enumerate((own_weight, other_weight)):
        first = jnp.where(half == 0, place, n - own - place)
        for b in range(own):
            d = first + b
            scale = used[d].astype(jnp.float32) * weight[b]
            value = total[d] + other[d].astype(jnp.float32)
            held[d] = (scale * value).astype(jnp.bfloat16)
    held[n] = jnp.zeros(held.shape[1:], jnp.bfloat16)

    def body(j, carry):
        out[j] = held[table[j]]
        return carry

    lax.fori_loop(0, out.shape[0], body, 0, unroll=8)


def finish_kernel(
    odd, mat_idx, send_slot, returned, pulled, grad, state, rays, *refs, tile_cols, last,
):
    outs, (whole, mark) = refs[:-2], refs[-2:]
    tiles = pulled.shape[0]
    chans = grad.shape[2]
    f32 = jnp.float32

    def place(t):
        r0, c0 = t // tile_cols * PIX, t % tile_cols * PIX
        return slice(r0, r0 + PIX), slice(c0, c0 + PIX)

    def leave(t):
        where = place(t)
        return pltpu.make_async_copy(whole.at[where], outs[0].at[where], mark.at[t])

    for t in range(tiles):
        picked = jnp.concatenate([returned[send_slot[t * HITS + k]] for k in range(HITS)], axis=0)
        backed = lax.dot_general(
            picked,
            matrices_of(mat_idx, rays, t),
            (((0,), (0,)), ((), ())),
            preferred_element_type=f32,
        ).T
        change = pulled[t].reshape(backed.shape) - relax_rate * backed
        where = place(t)
        adjoint = grad[where].astype(f32) + change.reshape(PIX, PIX, chans)
        if last:
            whole[where] = adjoint
            leave(t).start()
        else:
            value = state[where].astype(f32)
            whole[where] = (1.0 - value * value) * adjoint
    if last:
        for t in range(tiles):
            leave(t).wait()
    else:
        emit_edges(whole[...], odd, *outs)


def on_device(state, grad, kernel, ray_matrix, ray_weight, hits, offsets, block_slot, angle_count):
    f32, bf16, i32 = jnp.float32, jnp.bfloat16, jnp.int32
    rows_dev, cols_dev, chans = state.shape
    angles, spots, bins, tile_pix = ray_matrix.shape
    nr = lax.axis_size("row")
    nx = lax.axis_size("x")
    nc = lax.axis_size(COL)
    devices = nr * nc
    row, zh, zl, x = (lax.axis_index(a) for a in ("row",) + COL)
    tile_rows = rows_dev // PIX
    tile_cols = cols_dev // PIX
    tiles = tile_rows * tile_cols
    pairs = tiles * HITS
    blk_dev = ray_weight.shape[0]
    blocks = blk_dev * devices
    blk_ang = blocks // ANGLES
    cap = 2 * max(2, (pairs + devices - 2) // devices + 1)
    cap = min(cap, pairs)
    peers = nr * 2 * nx
    slots = peers * cap
    dense = 2 * blk_dev

    def exchange(value):
        return lax.ppermute(value, "zh", [(0, 1), (1, 0)])

    everyone = hits.reshape(nr, tile_rows, nc, tile_cols, HITS).transpose(0, 2, 1, 3, 4)
    everyone = everyone.reshape(nr, 2, 2, nx, pairs)
    group = lax.dynamic_index_in_dim(everyone, zh, 1, keepdims=False).reshape(peers, pairs)
    storage = jnp.sum(
        jnp.where(group[:, :, None] == jnp.arange(blocks, dtype=i32), block_slot, 0), axis=2
    )
    owner = storage // blk_dev
    local = storage % blk_dev
    owner_z = (owner % nc) // nx
    owner_zh = owner_z // 2
    owner_zl = owner_z % 2
    peer = ((owner // nc) * 2 + owner_zl) * nx + owner % nx
    place = owner_zh * blk_dev + local
    earlier = jnp.arange(pairs)[None, :] < jnp.arange(pairs)[:, None]
    ranking = jnp.sum(
        ((peer[:, :, None] == peer[:, None, :]) & earlier[None]).astype(i32), axis=2
    )
    me = (row * 2 + zl) * nx + x
    my_hits = lax.dynamic_index_in_dim(group, me, 0, keepdims=False)
    send_slot = lax.dynamic_index_in_dim(peer * cap + ranking, me, 0, keepdims=False)
    matched = (peer[:, None, :] == me) & (
        ranking[:, None, :] == jnp.arange(cap, dtype=i32)[None, :, None]
    )
    table = dense + jnp.sum(jnp.where(matched, place[:, None, :] - dense, 0), axis=2)
    table = table.reshape(slots)
    mat_idx = (my_hits // blk_ang) * spots + offsets.reshape(pairs)

    dense_z = jnp.arange(dense, dtype=i32) // blk_dev * 2 + zl
    dense_place = (row * nc + dense_z * nx + x) * blk_dev + jnp.arange(dense, dtype=i32) % blk_dev
    number = jnp.arange(blocks, dtype=i32)
    active = (
        (number % blk_ang).reshape(ANGLES, blk_ang) < angle_count[:, None]
    ).reshape(1, blocks)
    used = jnp.any((block_slot[None, :] == dense_place[:, None]) & active, axis=1).astype(i32)
    used = jnp.concatenate([used, jnp.full((1,), zh * blk_dev, i32)])

    rays = ray_matrix.reshape(angles * spots, bins, tile_pix)

    block = (bins, chans)
    shape = jax.ShapeDtypeStruct
    slot_out = shape((slots,) + block, bf16)
    edges = (
        shape(state.shape, bf16),
        shape((cols_dev, chans), bf16),
        shape((cols_dev, chans), bf16),
        shape((rows_dev, chans), f32),
        shape((rows_dev, chans), f32),
    )
    odd = jnp.stack([row % 2, (zh * (RING // 2) * nx + zl * nx + x) % 2])

    def limit(mib):
        return pltpu.CompilerParams(vmem_limit_bytes=mib << 20)

    start = pl.pallas_call(
        start_kernel,
        out_shape=edges,
        in_specs=[SMEM] + [ANY] * 2,
        out_specs=(VMEM,) * 5,
        scratch_shapes=[
            pltpu.VMEM(state.shape, bf16),
            pltpu.VMEM(state.shape, bf16),
            pltpu.VMEM(state.shape, f32),
            pltpu.SemaphoreType.DMA((2, 4)),
        ],
        compiler_params=limit(8),
        name="start",
    )
    sides = pl.pallas_call(
        sides_kernel,
        out_shape=[shape((rows_dev + 16, chans), f32)] * 2,
        in_specs=[SMEM] + [VMEM] * 4,
        out_specs=[VMEM] * 2,
        compiler_params=limit(4),
        name="sides",
    )
    pulled_out = shape((tiles, PIX // 2, 2, PIX, chans), f32)
    cols3_out = shape(((rows_dev + 2) // 2, 2, cols_dev, 3 * chans), bf16)
    macs = tiles * tile_pix * chans * (9 * chans + HITS * bins)

    def cost(share):
        return pl.CostEstimate(
            flops=2 * macs * share // tiles, bytes_accessed=rays.size * 2, transcendentals=0
        )

    taps_out = shape((4 * 3 * chans, 2 * chans), bf16)

    def inner(early):
        held = (shape(rays.shape, bf16),) if early else ()
        mark = [pltpu.SemaphoreType.DMA((angles,))] if early else []
        return pl.pallas_call(
            functools.partial(inner_kernel, tile_cols=tile_cols),
            out_shape=(pulled_out, slot_out, cols3_out, taps_out) + held,
            in_specs=[SMEM] * 3 + [VMEM] * 4 + [ANY if early else VMEM],
            out_specs=(VMEM,) * (4 + len(held)),
            scratch_shapes=mark + [pltpu.VMEM((rows_dev + 2, cols_dev + 16, chans), f32)],
            compiler_params=limit(16),
            cost_estimate=cost(len(tiles_at(tiles, tile_cols, True))),
            name="inner",
        )

    outer = pl.pallas_call(
        functools.partial(outer_kernel, tile_cols=tile_cols),
        out_shape=(pulled_out, slot_out, cols3_out),
        in_specs=[SMEM] * 3 + [VMEM] * 7,
        out_specs=(VMEM,) * 3,
        input_output_aliases={7: 0, 8: 1, 9: 2},
        compiler_params=limit(16),
        cost_estimate=cost(len(tiles_at(tiles, tile_cols, False))),
        name="outer",
    )
    combine = pl.pallas_call(
        combine_kernel,
        out_shape=(shape((dense,) + block, f32), shape((dense,) + block, bf16)),
        in_specs=[SMEM, VMEM],
        out_specs=(VMEM, VMEM),
        scratch_shapes=[pltpu.VMEM((dense + 1,) + block, f32)],
        compiler_params=limit(8),
        name="combine",
    )
    reply = pl.pallas_call(
        reply_kernel,
        out_shape=slot_out,
        in_specs=[SMEM] * 2 + [VMEM] * 4,
        out_specs=VMEM,
        scratch_shapes=[pltpu.VMEM((dense + 1,) + block, bf16)],
        compiler_params=limit(8),
        name="reply",
    )

    def finish(last):
        return pl.pallas_call(
            functools.partial(finish_kernel, tile_cols=tile_cols, last=last),
            out_shape=(shape(state.shape, f32),) if last else edges,
            in_specs=[SMEM] * 3 + [VMEM] * 5,
            out_specs=(pl.BlockSpec(memory_space=pl.ANY),) if last else (VMEM,) * 5,
            scratch_shapes=[
                pltpu.VMEM(state.shape, f32),
                pltpu.SemaphoreType.DMA((tiles,)),
            ],
            compiler_params=limit(20),
            name="finish",
        )

    def across(value):
        value = value.reshape((peers, cap) + block)
        value = lax.all_to_all(value, GROUP, split_axis=0, concat_axis=0, tiled=True)
        return value.reshape((slots,) + block)

    def swaps(value_a, value_b, axis):
        count = lax.axis_size(axis)
        even = [(i, i ^ 1) for i in range(count)]
        uneven = [(i, ((i + 1) ^ 1) - 1) for i in range(1, count - 1)]
        return lax.ppermute(value_a, axis, even), lax.ppermute(value_b, axis, uneven)

    def apart(value):
        return pltpu.with_memory_space_constraint(value, pltpu.HBM)

    def forward(early, scaled, row_a, row_b, col_a, col_b):
        above = swaps(row_a, row_b, "row")
        side_a, side_b = sides(odd, *above, col_a, col_b)
        other_weight = None
        if early:
            side_b, weight = lax.optimization_barrier((side_b, ray_weight))
            other_weight = exchange(weight)
        beside = swaps(side_a, side_b, COL)
        *parts, taps = inner(early)(
            odd, mat_idx, send_slot, scaled, *above, kernel, apart(rays) if early else rays
        )[: 4 + early]
        near = rays
        if early:
            near, taps = taps, parts.pop()
        pulled, outgoing, _ = outer(odd, mat_idx, send_slot, *beside, taps, near, *parts)
        return pulled, outgoing, other_weight

    scaled, *rim = start(odd, apart(state), apart(grad))
    for turn in range(ITERS):
        pulled, outgoing, swapped = forward(turn == 0, scaled, *rim)
        if not turn:
            other_weight = swapped
            outgoing, table, used, other_weight = lax.optimization_barrier(
                (outgoing, table, used, other_weight)
            )
        total, mine = combine(table, across(outgoing))
        replies = reply(table, used, total, exchange(mine), ray_weight, other_weight)
        last = turn == ITERS - 1
        scaled, *rim = finish(last)(
            odd, mat_idx, send_slot, across(replies), pulled, grad, state, rays
        )
    return scaled


def solution(mesh):
    nr, nc = mesh.devices.shape
    fine = Mesh(mesh.devices.reshape(nr, 2, RING // 2, nc // RING), ("row",) + COL)
    image = P("row", COL, None)
    placed = (
        image,
        image,
        P(),
        P(),
        P(("row",) + COL, None, None),
        P(),
        image,
        P(),
        P(),
    )
    return jax.shard_map(
        on_device, mesh=fine, in_specs=placed, out_specs=image, check_vma=False
    )
```

```python
import functools

import jax
import jax.numpy as jnp
from jax import lax
from jax.experimental import pallas as pl
from jax.experimental.pallas import tpu as pltpu
from jax.sharding import Mesh, PartitionSpec as P

PIX = 32
ANGLES = 8
HITS = 16
ITERS = 2
RING = 4

relax_rate = 0.25

COL = ("zh", "zl", "x")
GROUP = ("row", "zl", "x")

VMEM = pl.BlockSpec(memory_space=pltpu.VMEM)
SMEM = pl.BlockSpec(memory_space=pltpu.SMEM)
ANY = pl.BlockSpec(memory_space=pl.ANY)


def start_kernel(odd, state, grad, scaled, row_a, row_b, col_a, col_b, states, grads, whole, mark):
    parts = mark.shape[1]
    rows = states.shape[0] // parts

    def load(a, p):
        source, held = ((state, states), (grad, grads))[a]
        where = pl.ds(p * rows, rows)
        return pltpu.make_async_copy(source.at[where], held.at[where], mark.at[a, p])

    for p in range(parts):
        for a in range(2):
            load(a, p).start()
    for p in range(parts):
        for a in range(2):
            load(a, p).wait()
        where = slice(p * rows, (p + 1) * rows)
        value = states[where].astype(jnp.float32)
        whole[where] = (1.0 - value * value) * grads[where].astype(jnp.float32)
    emit_edges(whole[...], odd, scaled, row_a, row_b, col_a, col_b)


def pick(flag, yes, no):
    return jnp.where(flag == 1, yes, no)


def emit_edges(value, odd, scaled, row_a, row_b, col_a, col_b):
    rows, cols = value.shape[:2]
    scaled[...] = value.astype(jnp.bfloat16)
    row_a[...] = pick(odd[0], value[0], value[rows - 1]).astype(jnp.bfloat16)
    row_b[...] = pick(odd[0], value[rows - 1], value[0]).astype(jnp.bfloat16)
    left, right = value[:, 0, :], value[:, cols - 1, :]
    col_a[...] = pick(odd[1], left, right)
    col_b[...] = pick(odd[1], right, left)


def sides_kernel(odd, near_a, near_b, col_a, col_b, out_a, out_b):
    rows = col_a.shape[0]
    cols = near_a.shape[0]
    f32 = jnp.float32

    def ends(ref):
        low = ref[0:16, :].astype(f32)[0:1, :]
        high = ref[cols - 16 : cols, :].astype(f32)[15:16, :]
        return low, high

    a, b = ends(near_a), ends(near_b)
    above = [pick(odd[0], a[i], b[i]) for i in range(2)]
    below = [pick(odd[0], b[i], a[i]) for i in range(2)]
    for out, edge, order in ((out_a, col_a, (0, 1)), (out_b, col_b, (1, 0))):
        yes, no = order
        out[8 : 8 + rows, :] = edge[...]
        out[7:8, :] = pick(odd[1], above[yes], above[no])
        out[8 + rows : 9 + rows, :] = pick(odd[1], below[yes], below[no])


def matrices_of(mat_idx, rays, t):
    return jnp.concatenate([rays[mat_idx[t * HITS + k]] for k in range(HITS)], axis=0)


def forward_tile(
    mat_idx, send_slot, taps, rays, pulled, out, cols3, t, tile_cols, waiting=()
):
    chans = pulled.shape[-1]
    bins = rays.shape[1]
    half = PIX // 2
    r0, c0 = t // tile_cols * half, t % tile_cols * PIX
    window = jnp.concatenate(
        [
            cols3[r0 + dr // 2 : r0 + dr // 2 + half, dr % 2, c0 : c0 + PIX, :].reshape(
                half * PIX, 3 * chans
            )
            for dr in range(4)
        ],
        axis=1,
    )
    acc = jnp.dot(window, taps[...], preferred_element_type=jnp.float32)
    for odd in range(2):
        value = acc[:, odd * chans : (odd + 1) * chans].reshape(half, PIX, chans)
        pulled[t, :, odd] = value
    low = pulled[t].reshape(PIX * PIX, chans).astype(jnp.bfloat16)
    while waiting:
        waiting.pop().wait()
    value = jnp.dot(
        matrices_of(mat_idx, rays, t), low, preferred_element_type=jnp.float32
    ).astype(jnp.bfloat16)
    for k in range(HITS):
        out[send_slot[t * HITS + k]] = value[k * bins : (k + 1) * bins, :]


def tiles_at(tiles, tile_cols, inner):
    return [t for t in range(tiles) if (0 < t % tile_cols < tile_cols - 1) == inner]


def inner_kernel(
    odd, mat_idx, send_slot, scaled, near_a, near_b, kernel, rays,
    pulled, out, cols3, taps, *refs, tile_cols,
):
    wide = refs[-1]
    rows, cols, chans = scaled.shape
    f32, bf16 = jnp.float32, jnp.bfloat16
    waiting = []
    if len(refs) > 1:
        held, mark = refs[:2]
        count = rays.shape[0] // mark.shape[0]
        for i in range(mark.shape[0]):
            where = pl.ds(i * count, count)
            waiting.append(pltpu.make_async_copy(rays.at[where], held.at[where], mark.at[i]))
            waiting[-1].start()
        rays = held
    blank = jnp.zeros((3 * chans, chans), bf16)
    for dr in range(4):
        base = dr * 3 * chans
        for side in range(2):
            lanes = slice(side * chans, (side + 1) * chans)
            tap = dr - side
            if not 0 <= tap < 3:
                taps[base : base + 3 * chans, lanes] = blank
                continue
            for dc in range(3):
                taps[base + dc * chans : base + (dc + 1) * chans, lanes] = kernel[2 - tap, 2 - dc].T
    a, b = near_a[...].astype(f32), near_b[...].astype(f32)
    wide[0, 8 : 8 + cols, :] = pick(odd[0], a, b)
    wide[rows + 1, 8 : 8 + cols, :] = pick(odd[0], b, a)
    wide[1 : rows + 1, 8 : 8 + cols, :] = scaled[...].astype(f32)
    wide[:, 0:8, :] = jnp.zeros((rows + 2, 8, chans), f32)
    wide[:, 8 + cols :, :] = jnp.zeros((rows + 2, 8, chans), f32)
    for dc in range(3):
        value = wide[:, 7 + dc : 7 + dc + cols, :].astype(bf16)
        cols3[:, :, :, dc * chans : (dc + 1) * chans] = value.reshape(
            (rows + 2) // 2, 2, cols, chans
        )
    out[...] = jnp.zeros_like(out)
    for t in tiles_at(pulled.shape[0], tile_cols, True):
        forward_tile(mat_idx, send_slot, taps, rays, pulled, out, cols3, t, tile_cols, waiting)
    while waiting:
        waiting.pop().wait()


def outer_kernel(
    odd, mat_idx, send_slot, near_a, near_b, taps, rays, _pulled, _out, _cols3,
    pulled, out, cols3, *, tile_cols,
):
    cols = cols3.shape[2]
    chans = pulled.shape[-1]
    group = 16
    spot = lax.broadcasted_iota(jnp.int32, (group, chans), 0)
    a, b = near_a[...], near_b[...]
    left, right = pick(odd[1], a, b), pick(odd[1], b, a)
    for edge, dc, first, at in ((left, 0, 0, 0), (right, 2, cols - group, group - 1)):
        lanes = slice(dc * chans, (dc + 1) * chans)
        for r in range(2 * cols3.shape[0]):
            there = (r // 2, r % 2, slice(first, first + group), lanes)
            value = jnp.where(spot == at, edge[7 + r : 8 + r, :], cols3[there].astype(jnp.float32))
            cols3[there] = value.astype(jnp.bfloat16)
    for t in tiles_at(pulled.shape[0], tile_cols, False):
        forward_tile(mat_idx, send_slot, taps, rays, pulled, out, cols3, t, tile_cols)


def combine_kernel(table, recv, total, low, acc_a, acc_b):
    acc_a[...] = jnp.zeros_like(acc_a)
    acc_b[...] = jnp.zeros_like(acc_b)

    def body(j, carry):
        acc_a[table[2 * j]] += recv[2 * j].astype(jnp.float32)
        acc_b[table[2 * j + 1]] += recv[2 * j + 1].astype(jnp.float32)
        return carry

    lax.fori_loop(0, recv.shape[0] // 2, body, 0, unroll=4)
    n = total.shape[0]
    value = acc_a[:n] + acc_b[:n]
    total[...] = value
    low[...] = value.astype(jnp.bfloat16)


def reply_kernel(table, used, total, other, own_weight, other_weight, out, held):
    n = total.shape[0]
    own = own_weight.shape[0]
    place = used[n]
    for half, weight in enumerate((own_weight, other_weight)):
        first = jnp.where(half == 0, place, n - own - place)
        for b in range(own):
            d = first + b
            scale = used[d].astype(jnp.float32) * weight[b]
            value = total[d] + other[d].astype(jnp.float32)
            held[d] = (scale * value).astype(jnp.bfloat16)
    held[n] = jnp.zeros(held.shape[1:], jnp.bfloat16)

    def body(j, carry):
        out[j] = held[table[j]]
        return carry

    lax.fori_loop(0, out.shape[0], body, 0, unroll=8)


def finish_kernel(
    odd, mat_idx, send_slot, returned, pulled, grad, state, rays, *refs, tile_cols, last,
):
    outs, (whole, mark) = refs[:-2], refs[-2:]
    tiles = pulled.shape[0]
    chans = grad.shape[2]
    f32 = jnp.float32

    def place(t):
        r0, c0 = t // tile_cols * PIX, t % tile_cols * PIX
        return slice(r0, r0 + PIX), slice(c0, c0 + PIX)

    def leave(t):
        where = place(t)
        return pltpu.make_async_copy(whole.at[where], outs[0].at[where], mark.at[t])

    for t in range(tiles):
        picked = jnp.concatenate([returned[send_slot[t * HITS + k]] for k in range(HITS)], axis=0)
        backed = lax.dot_general(
            picked,
            matrices_of(mat_idx, rays, t),
            (((0,), (0,)), ((), ())),
            preferred_element_type=f32,
        ).T
        change = pulled[t].reshape(backed.shape) - relax_rate * backed
        where = place(t)
        adjoint = grad[where].astype(f32) + change.reshape(PIX, PIX, chans)
        if last:
            whole[where] = adjoint
            leave(t).start()
        else:
            value = state[where].astype(f32)
            whole[where] = (1.0 - value * value) * adjoint
    if last:
        for t in range(tiles):
            leave(t).wait()
    else:
        emit_edges(whole[...], odd, *outs)


def on_device(state, grad, kernel, ray_matrix, ray_weight, hits, offsets, block_slot, angle_count):
    f32, bf16, i32 = jnp.float32, jnp.bfloat16, jnp.int32
    rows_dev, cols_dev, chans = state.shape
    angles, spots, bins, tile_pix = ray_matrix.shape
    nr = lax.axis_size("row")
    nx = lax.axis_size("x")
    nc = lax.axis_size(COL)
    devices = nr * nc
    row, zh, zl, x = (lax.axis_index(a) for a in ("row",) + COL)
    tile_rows = rows_dev // PIX
    tile_cols = cols_dev // PIX
    tiles = tile_rows * tile_cols
    pairs = tiles * HITS
    blk_dev = ray_weight.shape[0]
    blocks = blk_dev * devices
    blk_ang = blocks // ANGLES
    cap = 2 * max(2, (pairs + devices - 2) // devices + 1)
    cap = min(cap, pairs)
    peers = nr * 2 * nx
    slots = peers * cap
    dense = 2 * blk_dev

    def exchange(value):
        return lax.ppermute(value, "zh", [(0, 1), (1, 0)])

    everyone = hits.reshape(nr, tile_rows, nc, tile_cols, HITS).transpose(0, 2, 1, 3, 4)
    everyone = everyone.reshape(nr, 2, 2, nx, pairs)
    group = lax.dynamic_index_in_dim(everyone, zh, 1, keepdims=False).reshape(peers, pairs)
    storage = jnp.sum(
        jnp.where(group[:, :, None] == jnp.arange(blocks, dtype=i32), block_slot, 0), axis=2
    )
    owner = storage // blk_dev
    local = storage % blk_dev
    owner_z = (owner % nc) // nx
    owner_zh = owner_z // 2
    owner_zl = owner_z % 2
    peer = ((owner // nc) * 2 + owner_zl) * nx + owner % nx
    place = owner_zh * blk_dev + local
    earlier = jnp.arange(pairs)[None, :] < jnp.arange(pairs)[:, None]
    ranking = jnp.sum(
        ((peer[:, :, None] == peer[:, None, :]) & earlier[None]).astype(i32), axis=2
    )
    me = (row * 2 + zl) * nx + x
    my_hits = lax.dynamic_index_in_dim(group, me, 0, keepdims=False)
    send_slot = lax.dynamic_index_in_dim(peer * cap + ranking, me, 0, keepdims=False)
    matched = (peer[:, None, :] == me) & (
        ranking[:, None, :] == jnp.arange(cap, dtype=i32)[None, :, None]
    )
    table = dense + jnp.sum(jnp.where(matched, place[:, None, :] - dense, 0), axis=2)
    table = table.reshape(slots)
    mat_idx = (my_hits // blk_ang) * spots + offsets.reshape(pairs)

    dense_z = jnp.arange(dense, dtype=i32) // blk_dev * 2 + zl
    dense_place = (row * nc + dense_z * nx + x) * blk_dev + jnp.arange(dense, dtype=i32) % blk_dev
    number = jnp.arange(blocks, dtype=i32)
    active = (
        (number % blk_ang).reshape(ANGLES, blk_ang) < angle_count[:, None]
    ).reshape(1, blocks)
    used = jnp.any((block_slot[None, :] == dense_place[:, None]) & active, axis=1).astype(i32)
    used = jnp.concatenate([used, jnp.full((1,), zh * blk_dev, i32)])

    rays = ray_matrix.reshape(angles * spots, bins, tile_pix)

    block = (bins, chans)
    shape = jax.ShapeDtypeStruct
    slot_out = shape((slots,) + block, bf16)
    edges = (
        shape(state.shape, bf16),
        shape((cols_dev, chans), bf16),
        shape((cols_dev, chans), bf16),
        shape((rows_dev, chans), f32),
        shape((rows_dev, chans), f32),
    )
    odd = jnp.stack([row % 2, (zh * (RING // 2) * nx + zl * nx + x) % 2])

    def limit(mib):
        return pltpu.CompilerParams(vmem_limit_bytes=mib << 20)

    start = pl.pallas_call(
        start_kernel,
        out_shape=edges,
        in_specs=[SMEM] + [ANY] * 2,
        out_specs=(VMEM,) * 5,
        scratch_shapes=[
            pltpu.VMEM(state.shape, bf16),
            pltpu.VMEM(state.shape, bf16),
            pltpu.VMEM(state.shape, f32),
            pltpu.SemaphoreType.DMA((2, 4)),
        ],
        compiler_params=limit(8),
        name="start",
    )
    sides = pl.pallas_call(
        sides_kernel,
        out_shape=[shape((rows_dev + 16, chans), f32)] * 2,
        in_specs=[SMEM] + [VMEM] * 4,
        out_specs=[VMEM] * 2,
        compiler_params=limit(4),
        name="sides",
    )
    pulled_out = shape((tiles, PIX // 2, 2, PIX, chans), f32)
    cols3_out = shape(((rows_dev + 2) // 2, 2, cols_dev, 3 * chans), bf16)
    macs = tiles * tile_pix * chans * (9 * chans + HITS * bins)

    def cost(share):
        return pl.CostEstimate(
            flops=2 * macs * share // tiles, bytes_accessed=rays.size * 2, transcendentals=0
        )

    taps_out = shape((4 * 3 * chans, 2 * chans), bf16)

    def inner(early):
        held = (shape(rays.shape, bf16),) if early else ()
        mark = [pltpu.SemaphoreType.DMA((angles * spots,))] if early else []
        return pl.pallas_call(
            functools.partial(inner_kernel, tile_cols=tile_cols),
            out_shape=(pulled_out, slot_out, cols3_out, taps_out) + held,
            in_specs=[SMEM] * 3 + [VMEM] * 4 + [ANY if early else VMEM],
            out_specs=(VMEM,) * (4 + len(held)),
            scratch_shapes=mark + [pltpu.VMEM((rows_dev + 2, cols_dev + 16, chans), f32)],
            compiler_params=limit(16),
            cost_estimate=cost(len(tiles_at(tiles, tile_cols, True))),
            name="inner",
        )

    outer = pl.pallas_call(
        functools.partial(outer_kernel, tile_cols=tile_cols),
        out_shape=(pulled_out, slot_out, cols3_out),
        in_specs=[SMEM] * 3 + [VMEM] * 7,
        out_specs=(VMEM,) * 3,
        input_output_aliases={7: 0, 8: 1, 9: 2},
        compiler_params=limit(16),
        cost_estimate=cost(len(tiles_at(tiles, tile_cols, False))),
        name="outer",
    )
    combine = pl.pallas_call(
        combine_kernel,
        out_shape=(shape((dense,) + block, f32), shape((dense,) + block, bf16)),
        in_specs=[SMEM, VMEM],
        out_specs=(VMEM, VMEM),
        scratch_shapes=[pltpu.VMEM((dense + 1,) + block, f32)] * 2,
        compiler_params=limit(8),
        name="combine",
    )
    reply = pl.pallas_call(
        reply_kernel,
        out_shape=slot_out,
        in_specs=[SMEM] * 2 + [VMEM] * 4,
        out_specs=VMEM,
        scratch_shapes=[pltpu.VMEM((dense + 1,) + block, bf16)],
        compiler_params=limit(8),
        name="reply",
    )

    def finish(last):
        return pl.pallas_call(
            functools.partial(finish_kernel, tile_cols=tile_cols, last=last),
            out_shape=(shape(state.shape, f32),) if last else edges,
            in_specs=[SMEM] * 3 + [VMEM] * 5,
            out_specs=(pl.BlockSpec(memory_space=pl.ANY),) if last else (VMEM,) * 5,
            scratch_shapes=[
                pltpu.VMEM(state.shape, f32),
                pltpu.SemaphoreType.DMA((tiles,)),
            ],
            compiler_params=limit(20),
            name="finish",
        )

    def across(value):
        value = value.reshape((peers, cap) + block)
        value = lax.all_to_all(value, GROUP, split_axis=0, concat_axis=0, tiled=True)
        return value.reshape((slots,) + block)

    def swaps(value_a, value_b, axis):
        count = lax.axis_size(axis)
        even = [(i, i ^ 1) for i in range(count)]
        uneven = [(i, ((i + 1) ^ 1) - 1) for i in range(1, count - 1)]
        return lax.ppermute(value_a, axis, even), lax.ppermute(value_b, axis, uneven)

    def apart(value):
        return pltpu.with_memory_space_constraint(value, pltpu.HBM)

    def forward(early, scaled, row_a, row_b, col_a, col_b):
        above = swaps(row_a, row_b, "row")
        side_a, side_b = sides(odd, *above, col_a, col_b)
        beside = swaps(side_a, side_b, COL)
        other_weight = None
        if early:
            arrived, weight = lax.optimization_barrier((beside[0], ray_weight))
            beside = (arrived, beside[1])
            other_weight = exchange(weight)
        *parts, taps = inner(early)(
            odd, mat_idx, send_slot, scaled, *above, kernel, apart(rays) if early else rays
        )[: 4 + early]
        near = rays
        if early:
            near, taps = taps, parts.pop()
        pulled, outgoing, _ = outer(odd, mat_idx, send_slot, *beside, taps, near, *parts)
        return pulled, outgoing, other_weight

    scaled, *rim = start(odd, apart(state), apart(grad))
    for turn in range(ITERS):
        pulled, outgoing, swapped = forward(turn == 0, scaled, *rim)
        if not turn:
            other_weight = swapped
            outgoing, table, used, other_weight = lax.optimization_barrier(
                (outgoing, table, used, other_weight)
            )
        total, mine = combine(table, across(outgoing))
        replies = reply(table, used, total, exchange(mine), ray_weight, other_weight)
        last = turn == ITERS - 1
        scaled, *rim = finish(last)(
            odd, mat_idx, send_slot, across(replies), pulled, grad, state, rays
        )
    return scaled


def solution(mesh):
    nr, nc = mesh.devices.shape
    fine = Mesh(mesh.devices.reshape(nr, 2, RING // 2, nc // RING), ("row",) + COL)
    image = P("row", COL, None)
    placed = (
        image,
        image,
        P(),
        P(),
        P(("row",) + COL, None, None),
        P(),
        image,
        P(),
        P(),
    )
    return jax.shard_map(
        on_device, mesh=fine, in_specs=placed, out_specs=image, check_vma=False
    )
```

```python
import functools

import jax
import jax.numpy as jnp
from jax import lax
from jax.experimental import pallas as pl
from jax.experimental.pallas import tpu as pltpu
from jax.sharding import Mesh, PartitionSpec as P

PIX = 32
ANGLES = 8
HITS = 16
ITERS = 2
RING = 4

relax_rate = 0.25

COL = ("zh", "zl", "x")
GROUP = ("row", "zl", "x")

VMEM = pl.BlockSpec(memory_space=pltpu.VMEM)
SMEM = pl.BlockSpec(memory_space=pltpu.SMEM)
ANY = pl.BlockSpec(memory_space=pl.ANY)


def start_kernel(odd, state, grad, scaled, row_a, row_b, col_a, col_b, states, grads, whole, mark):
    parts = mark.shape[1]
    rows = states.shape[0] // parts

    def load(a, p):
        source, held = ((state, states), (grad, grads))[a]
        where = pl.ds(p * rows, rows)
        return pltpu.make_async_copy(source.at[where], held.at[where], mark.at[a, p])

    for p in range(parts):
        for a in range(2):
            load(a, p).start()
    for p in range(parts):
        for a in range(2):
            load(a, p).wait()
        where = slice(p * rows, (p + 1) * rows)
        value = states[where].astype(jnp.float32)
        whole[where] = (1.0 - value * value) * grads[where].astype(jnp.float32)
    emit_edges(whole[...], odd, scaled, row_a, row_b, col_a, col_b)


def pick(flag, yes, no):
    return jnp.where(flag == 1, yes, no)


def emit_edges(value, odd, scaled, row_a, row_b, col_a, col_b):
    rows, cols = value.shape[:2]
    scaled[...] = value.astype(jnp.bfloat16)
    row_a[...] = pick(odd[0], value[0], value[rows - 1]).astype(jnp.bfloat16)
    row_b[...] = pick(odd[0], value[rows - 1], value[0]).astype(jnp.bfloat16)
    left, right = value[:, 0, :], value[:, cols - 1, :]
    col_a[...] = pick(odd[1], left, right)
    col_b[...] = pick(odd[1], right, left)


def sides_kernel(odd, near_a, near_b, col_a, col_b, out_a, out_b):
    rows = col_a.shape[0]
    cols = near_a.shape[0]
    f32 = jnp.float32

    def ends(ref):
        low = ref[0:16, :].astype(f32)[0:1, :]
        high = ref[cols - 16 : cols, :].astype(f32)[15:16, :]
        return low, high

    a, b = ends(near_a), ends(near_b)
    above = [pick(odd[0], a[i], b[i]) for i in range(2)]
    below = [pick(odd[0], b[i], a[i]) for i in range(2)]
    for out, edge, order in ((out_a, col_a, (0, 1)), (out_b, col_b, (1, 0))):
        yes, no = order
        out[8 : 8 + rows, :] = edge[...]
        out[7:8, :] = pick(odd[1], above[yes], above[no])
        out[8 + rows : 9 + rows, :] = pick(odd[1], below[yes], below[no])


def matrices_of(mat_idx, rays, t):
    return jnp.concatenate([rays[mat_idx[t * HITS + k]] for k in range(HITS)], axis=0)


def forward_tile(mat_idx, send_slot, taps, rays, pulled, out, cols3, t, tile_cols):
    chans = pulled.shape[-1]
    bins = rays.shape[1]
    half = PIX // 2
    r0, c0 = t // tile_cols * half, t % tile_cols * PIX
    window = jnp.concatenate(
        [
            cols3[r0 + dr // 2 : r0 + dr // 2 + half, dr % 2, c0 : c0 + PIX, :].reshape(
                half * PIX, 3 * chans
            )
            for dr in range(4)
        ],
        axis=1,
    )
    acc = jnp.dot(window, taps[...], preferred_element_type=jnp.float32)
    for odd in range(2):
        value = acc[:, odd * chans : (odd + 1) * chans].reshape(half, PIX, chans)
        pulled[t, :, odd] = value
    low = pulled[t].reshape(PIX * PIX, chans).astype(jnp.bfloat16)
    value = jnp.dot(
        matrices_of(mat_idx, rays, t), low, preferred_element_type=jnp.float32
    ).astype(jnp.bfloat16)
    for k in range(HITS):
        out[send_slot[t * HITS + k]] = value[k * bins : (k + 1) * bins, :]


def tiles_at(tiles, tile_cols, inner):
    return [t for t in range(tiles) if (0 < t % tile_cols < tile_cols - 1) == inner]


def inner_kernel(
    odd, mat_idx, send_slot, scaled, near_a, near_b, kernel, rays,
    pulled, out, cols3, taps, wide, *, tile_cols,
):
    rows, cols, chans = scaled.shape
    f32, bf16 = jnp.float32, jnp.bfloat16
    blank = jnp.zeros((3 * chans, chans), bf16)
    for dr in range(4):
        base = dr * 3 * chans
        for side in range(2):
            lanes = slice(side * chans, (side + 1) * chans)
            tap = dr - side
            if not 0 <= tap < 3:
                taps[base : base + 3 * chans, lanes] = blank
                continue
            for dc in range(3):
                taps[base + dc * chans : base + (dc + 1) * chans, lanes] = kernel[2 - tap, 2 - dc].T
    a, b = near_a[...].astype(f32), near_b[...].astype(f32)
    wide[0, 8 : 8 + cols, :] = pick(odd[0], a, b)
    wide[rows + 1, 8 : 8 + cols, :] = pick(odd[0], b, a)
    wide[1 : rows + 1, 8 : 8 + cols, :] = scaled[...].astype(f32)
    wide[:, 0:8, :] = jnp.zeros((rows + 2, 8, chans), f32)
    wide[:, 8 + cols :, :] = jnp.zeros((rows + 2, 8, chans), f32)
    for dc in range(3):
        value = wide[:, 7 + dc : 7 + dc + cols, :].astype(bf16)
        cols3[:, :, :, dc * chans : (dc + 1) * chans] = value.reshape(
            (rows + 2) // 2, 2, cols, chans
        )
    out[...] = jnp.zeros_like(out)
    for t in tiles_at(pulled.shape[0], tile_cols, True):
        forward_tile(mat_idx, send_slot, taps, rays, pulled, out, cols3, t, tile_cols)


def outer_kernel(
    odd, mat_idx, send_slot, near_a, near_b, taps, rays, _pulled, _out, _cols3,
    pulled, out, cols3, *, tile_cols,
):
    cols = cols3.shape[2]
    chans = pulled.shape[-1]
    group = 16
    spot = lax.broadcasted_iota(jnp.int32, (group, chans), 0)
    a, b = near_a[...], near_b[...]
    left, right = pick(odd[1], a, b), pick(odd[1], b, a)
    for edge, dc, first, at in ((left, 0, 0, 0), (right, 2, cols - group, group - 1)):
        lanes = slice(dc * chans, (dc + 1) * chans)
        for r in range(2 * cols3.shape[0]):
            there = (r // 2, r % 2, slice(first, first + group), lanes)
            value = jnp.where(spot == at, edge[7 + r : 8 + r, :], cols3[there].astype(jnp.float32))
            cols3[there] = value.astype(jnp.bfloat16)
    for t in tiles_at(pulled.shape[0], tile_cols, False):
        forward_tile(mat_idx, send_slot, taps, rays, pulled, out, cols3, t, tile_cols)


def combine_kernel(table, recv, total, low, acc_a, acc_b):
    acc_a[...] = jnp.zeros_like(acc_a)
    acc_b[...] = jnp.zeros_like(acc_b)

    def body(j, carry):
        acc_a[table[2 * j]] += recv[2 * j].astype(jnp.float32)
        acc_b[table[2 * j + 1]] += recv[2 * j + 1].astype(jnp.float32)
        return carry

    lax.fori_loop(0, recv.shape[0] // 2, body, 0, unroll=4)
    n = total.shape[0]
    value = acc_a[:n] + acc_b[:n]
    total[...] = value
    low[...] = value.astype(jnp.bfloat16)


def reply_kernel(table, used, total, other, own_weight, other_weight, out, held):
    n = total.shape[0]
    own = own_weight.shape[0]
    place = used[n]
    for half, weight in enumerate((own_weight, other_weight)):
        first = jnp.where(half == 0, place, n - own - place)
        for b in range(own):
            d = first + b
            scale = used[d].astype(jnp.float32) * weight[b].astype(jnp.float32)
            value = total[d] + other[d].astype(jnp.float32)
            held[d] = (scale * value).astype(jnp.bfloat16)
    held[n] = jnp.zeros(held.shape[1:], jnp.bfloat16)

    def body(j, carry):
        out[j] = held[table[j]]
        return carry

    lax.fori_loop(0, out.shape[0], body, 0, unroll=8)


def finish_kernel(
    odd, mat_idx, send_slot, returned, pulled, grad, state, rays, *refs, tile_cols, last,
):
    outs, (whole, mark) = refs[:-2], refs[-2:]
    tiles = pulled.shape[0]
    chans = grad.shape[2]
    f32 = jnp.float32

    def place(t):
        r0, c0 = t // tile_cols * PIX, t % tile_cols * PIX
        return slice(r0, r0 + PIX), slice(c0, c0 + PIX)

    def leave(t):
        where = place(t)
        return pltpu.make_async_copy(whole.at[where], outs[0].at[where], mark.at[t])

    for t in range(tiles):
        picked = jnp.concatenate([returned[send_slot[t * HITS + k]] for k in range(HITS)], axis=0)
        backed = lax.dot_general(
            picked,
            matrices_of(mat_idx, rays, t),
            (((0,), (0,)), ((), ())),
            preferred_element_type=f32,
        ).T
        change = pulled[t].reshape(backed.shape) - relax_rate * backed
        where = place(t)
        adjoint = grad[where].astype(f32) + change.reshape(PIX, PIX, chans)
        if last:
            whole[where] = adjoint
            leave(t).start()
        else:
            value = state[where].astype(f32)
            whole[where] = (1.0 - value * value) * adjoint
    if last:
        for t in range(tiles):
            leave(t).wait()
    else:
        emit_edges(whole[...], odd, *outs)


def on_device(state, grad, kernel, ray_matrix, ray_weight, hits, offsets, block_slot, angle_count):
    f32, bf16, i32 = jnp.float32, jnp.bfloat16, jnp.int32
    rows_dev, cols_dev, chans = state.shape
    angles, spots, bins, tile_pix = ray_matrix.shape
    nr = lax.axis_size("row")
    nx = lax.axis_size("x")
    nc = lax.axis_size(COL)
    devices = nr * nc
    row, zh, zl, x = (lax.axis_index(a) for a in ("row",) + COL)
    tile_rows = rows_dev // PIX
    tile_cols = cols_dev // PIX
    tiles = tile_rows * tile_cols
    pairs = tiles * HITS
    blk_dev = ray_weight.shape[0]
    blocks = blk_dev * devices
    blk_ang = blocks // ANGLES
    cap = 2 * max(2, (pairs + devices - 2) // devices + 1)
    cap = min(cap, pairs)
    peers = nr * 2 * nx
    slots = peers * cap
    dense = 2 * blk_dev

    def exchange(value):
        return lax.ppermute(value, "zh", [(0, 1), (1, 0)])

    everyone = hits.reshape(nr, tile_rows, nc, tile_cols, HITS).transpose(0, 2, 1, 3, 4)
    everyone = everyone.reshape(nr, 2, 2, nx, pairs)
    group = lax.dynamic_index_in_dim(everyone, zh, 1, keepdims=False).reshape(peers, pairs)
    storage = jnp.sum(
        jnp.where(group[:, :, None] == jnp.arange(blocks, dtype=i32), block_slot, 0), axis=2
    )
    owner = storage // blk_dev
    local = storage % blk_dev
    owner_z = (owner % nc) // nx
    owner_zh = owner_z // 2
    owner_zl = owner_z % 2
    peer = ((owner // nc) * 2 + owner_zl) * nx + owner % nx
    place = owner_zh * blk_dev + local
    earlier = jnp.arange(pairs)[None, :] < jnp.arange(pairs)[:, None]
    ranking = jnp.sum(
        ((peer[:, :, None] == peer[:, None, :]) & earlier[None]).astype(i32), axis=2
    )
    me = (row * 2 + zl) * nx + x
    my_hits = lax.dynamic_index_in_dim(group, me, 0, keepdims=False)
    send_slot = lax.dynamic_index_in_dim(peer * cap + ranking, me, 0, keepdims=False)
    matched = (peer[:, None, :] == me) & (
        ranking[:, None, :] == jnp.arange(cap, dtype=i32)[None, :, None]
    )
    table = dense + jnp.sum(jnp.where(matched, place[:, None, :] - dense, 0), axis=2)
    table = table.reshape(slots)
    mat_idx = (my_hits // blk_ang) * spots + offsets.reshape(pairs)

    dense_z = jnp.arange(dense, dtype=i32) // blk_dev * 2 + zl
    dense_place = (row * nc + dense_z * nx + x) * blk_dev + jnp.arange(dense, dtype=i32) % blk_dev
    number = jnp.arange(blocks, dtype=i32)
    active = (
        (number % blk_ang).reshape(ANGLES, blk_ang) < angle_count[:, None]
    ).reshape(1, blocks)
    used = jnp.any((block_slot[None, :] == dense_place[:, None]) & active, axis=1).astype(i32)
    used = jnp.concatenate([used, jnp.full((1,), zh * blk_dev, i32)])

    rays = ray_matrix.reshape(angles * spots, bins, tile_pix)

    block = (bins, chans)
    shape = jax.ShapeDtypeStruct
    slot_out = shape((slots,) + block, bf16)
    edges = (
        shape(state.shape, bf16),
        shape((cols_dev, chans), bf16),
        shape((cols_dev, chans), bf16),
        shape((rows_dev, chans), f32),
        shape((rows_dev, chans), f32),
    )
    odd = jnp.stack([row % 2, (zh * (RING // 2) * nx + zl * nx + x) % 2])

    def limit(mib):
        return pltpu.CompilerParams(vmem_limit_bytes=mib << 20)

    start = pl.pallas_call(
        start_kernel,
        out_shape=edges,
        in_specs=[SMEM] + [ANY] * 2,
        out_specs=(VMEM,) * 5,
        scratch_shapes=[
            pltpu.VMEM(state.shape, bf16),
            pltpu.VMEM(state.shape, bf16),
            pltpu.VMEM(state.shape, f32),
            pltpu.SemaphoreType.DMA((2, 4)),
        ],
        compiler_params=limit(8),
        name="start",
    )
    sides = pl.pallas_call(
        sides_kernel,
        out_shape=[shape((rows_dev + 16, chans), f32)] * 2,
        in_specs=[SMEM] + [VMEM] * 4,
        out_specs=[VMEM] * 2,
        compiler_params=limit(4),
        cost_estimate=pl.CostEstimate(
            flops=4 * rays.size * 512, bytes_accessed=rays.size * 2, transcendentals=0
        ),
        name="sides",
    )
    pulled_out = shape((tiles, PIX // 2, 2, PIX, chans), f32)
    cols3_out = shape(((rows_dev + 2) // 2, 2, cols_dev, 3 * chans), bf16)
    macs = tiles * tile_pix * chans * (9 * chans + HITS * bins)

    def cost(share):
        return pl.CostEstimate(
            flops=2 * macs * share // tiles, bytes_accessed=rays.size * 2, transcendentals=0
        )

    taps_out = shape((4 * 3 * chans, 2 * chans), bf16)

    inner = pl.pallas_call(
        functools.partial(inner_kernel, tile_cols=tile_cols),
        out_shape=(pulled_out, slot_out, cols3_out, taps_out),
        in_specs=[SMEM] * 3 + [VMEM] * 5,
        out_specs=(VMEM,) * 4,
        scratch_shapes=[pltpu.VMEM((rows_dev + 2, cols_dev + 16, chans), f32)],
        compiler_params=limit(16),
        cost_estimate=cost(len(tiles_at(tiles, tile_cols, True))),
        name="inner",
    )
    outer = pl.pallas_call(
        functools.partial(outer_kernel, tile_cols=tile_cols),
        out_shape=(pulled_out, slot_out, cols3_out),
        in_specs=[SMEM] * 3 + [VMEM] * 7,
        out_specs=(VMEM,) * 3,
        input_output_aliases={7: 0, 8: 1, 9: 2},
        compiler_params=limit(16),
        cost_estimate=cost(len(tiles_at(tiles, tile_cols, False))),
        name="outer",
    )
    combine = pl.pallas_call(
        combine_kernel,
        out_shape=(shape((dense,) + block, f32), shape((dense,) + block, bf16)),
        in_specs=[SMEM, VMEM],
        out_specs=(VMEM, VMEM),
        scratch_shapes=[pltpu.VMEM((dense + 1,) + block, f32)] * 2,
        compiler_params=limit(8),
        name="combine",
    )
    reply = pl.pallas_call(
        reply_kernel,
        out_shape=slot_out,
        in_specs=[SMEM] * 2 + [VMEM] * 4,
        out_specs=VMEM,
        scratch_shapes=[pltpu.VMEM((dense + 1,) + block, bf16)],
        compiler_params=limit(8),
        name="reply",
    )

    def finish(last):
        return pl.pallas_call(
            functools.partial(finish_kernel, tile_cols=tile_cols, last=last),
            out_shape=(shape(state.shape, f32),) if last else edges,
            in_specs=[SMEM] * 3 + [VMEM] * 5,
            out_specs=(pl.BlockSpec(memory_space=pl.ANY),) if last else (VMEM,) * 5,
            scratch_shapes=[
                pltpu.VMEM(state.shape, f32),
                pltpu.SemaphoreType.DMA((tiles,)),
            ],
            compiler_params=limit(20),
            name="finish",
        )

    def across(value):
        value = value.reshape((peers, cap) + block)
        value = lax.all_to_all(value, GROUP, split_axis=0, concat_axis=0, tiled=True)
        return value.reshape((slots,) + block)

    def swaps(value_a, value_b, axis):
        count = lax.axis_size(axis)
        even = [(i, i ^ 1) for i in range(count)]
        uneven = [(i, ((i + 1) ^ 1) - 1) for i in range(1, count - 1)]
        return lax.ppermute(value_a, axis, even), lax.ppermute(value_b, axis, uneven)

    def apart(value):
        return pltpu.with_memory_space_constraint(value, pltpu.HBM)

    def forward(early, scaled, row_a, row_b, col_a, col_b):
        above = swaps(row_a, row_b, "row")
        side_a, side_b = sides(odd, *above, col_a, col_b)
        other_weight = None
        if early:
            side_b, weight = lax.optimization_barrier((side_b, ray_weight.astype(bf16)))
            other_weight = exchange(weight)
        beside = swaps(side_a, side_b, COL)
        *parts, taps = inner(odd, mat_idx, send_slot, scaled, *above, kernel, rays)
        pulled, outgoing, _ = outer(odd, mat_idx, send_slot, *beside, taps, rays, *parts)
        return pulled, outgoing, other_weight

    scaled, *rim = start(odd, apart(state), apart(grad))
    for turn in range(ITERS):
        pulled, outgoing, swapped = forward(turn == 0, scaled, *rim)
        if not turn:
            other_weight = swapped
            outgoing, table, used, other_weight = lax.optimization_barrier(
                (outgoing, table, used, other_weight)
            )
        total, mine = combine(table, across(outgoing))
        replies = reply(table, used, total, exchange(mine), ray_weight, other_weight)
        last = turn == ITERS - 1
        scaled, *rim = finish(last)(
            odd, mat_idx, send_slot, across(replies), pulled, grad, state, rays
        )
    return scaled


def solution(mesh):
    nr, nc = mesh.devices.shape
    fine = Mesh(mesh.devices.reshape(nr, 2, RING // 2, nc // RING), ("row",) + COL)
    image = P("row", COL, None)
    placed = (
        image,
        image,
        P(),
        P(),
        P(("row",) + COL, None, None),
        P(),
        image,
        P(),
        P(),
    )
    return jax.shard_map(
        on_device, mesh=fine, in_specs=placed, out_specs=image, check_vma=False
    )
```

```python
import functools

import jax
import jax.numpy as jnp
from jax import lax
from jax.experimental import pallas as pl
from jax.experimental.pallas import tpu as pltpu
from jax.sharding import Mesh, PartitionSpec as P

PIX = 32
ANGLES = 8
HITS = 16
ITERS = 2
RING = 4

relax_rate = 0.25

COL = ("zh", "zl", "x")
GROUP = ("row", "zl", "x")

VMEM = pl.BlockSpec(memory_space=pltpu.VMEM)
SMEM = pl.BlockSpec(memory_space=pltpu.SMEM)
ANY = pl.BlockSpec(memory_space=pl.ANY)


def start_kernel(odd, state, grad, scaled, row_a, row_b, col_a, col_b, states, grads, whole, mark):
    parts = mark.shape[1]
    rows = states.shape[0] // parts

    def load(a, p):
        source, held = ((state, states), (grad, grads))[a]
        where = pl.ds(p * rows, rows)
        return pltpu.make_async_copy(source.at[where], held.at[where], mark.at[a, p])

    for p in range(parts):
        for a in range(2):
            load(a, p).start()
    for p in range(parts):
        for a in range(2):
            load(a, p).wait()
        where = slice(p * rows, (p + 1) * rows)
        value = states[where].astype(jnp.float32)
        whole[where] = (1.0 - value * value) * grads[where].astype(jnp.float32)
    emit_edges(whole[...], odd, scaled, row_a, row_b, col_a, col_b)


def pick(flag, yes, no):
    return jnp.where(flag == 1, yes, no)


def emit_edges(value, odd, scaled, row_a, row_b, col_a, col_b):
    rows = value.shape[0]
    row_a[...] = pick(odd[0], value[0], value[rows - 1]).astype(jnp.bfloat16)
    row_b[...] = pick(odd[0], value[rows - 1], value[0]).astype(jnp.bfloat16)
    emit_sides(value, odd, scaled, col_a, col_b)


def emit_sides(value, odd, scaled, col_a, col_b):
    cols = value.shape[1]
    scaled[...] = value.astype(jnp.bfloat16)
    left, right = value[:, 0, :], value[:, cols - 1, :]
    col_a[...] = pick(odd[1], left, right)
    col_b[...] = pick(odd[1], right, left)


def sides_kernel(odd, near_a, near_b, col_a, col_b, out_a, out_b):
    rows = col_a.shape[0]
    cols = near_a.shape[0]
    f32 = jnp.float32

    def ends(ref):
        low = ref[0:16, :].astype(f32)[0:1, :]
        high = ref[cols - 16 : cols, :].astype(f32)[15:16, :]
        return low, high

    a, b = ends(near_a), ends(near_b)
    above = [pick(odd[0], a[i], b[i]) for i in range(2)]
    below = [pick(odd[0], b[i], a[i]) for i in range(2)]
    for out, edge, order in ((out_a, col_a, (0, 1)), (out_b, col_b, (1, 0))):
        yes, no = order
        out[8 : 8 + rows, :] = edge[...]
        out[7:8, :] = pick(odd[1], above[yes], above[no])
        out[8 + rows : 9 + rows, :] = pick(odd[1], below[yes], below[no])


def matrices_of(mat_idx, rays, t):
    return jnp.concatenate([rays[mat_idx[t * HITS + k]] for k in range(HITS)], axis=0)


def forward_tile(mat_idx, send_slot, taps, rays, pulled, out, cols3, t, tile_cols):
    chans = pulled.shape[-1]
    bins = rays.shape[1]
    half = PIX // 2
    r0, c0 = t // tile_cols * half, t % tile_cols * PIX
    window = jnp.concatenate(
        [
            cols3[r0 + dr // 2 : r0 + dr // 2 + half, dr % 2, c0 : c0 + PIX, :].reshape(
                half * PIX, 3 * chans
            )
            for dr in range(4)
        ],
        axis=1,
    )
    acc = jnp.dot(window, taps[...], preferred_element_type=jnp.float32)
    for odd in range(2):
        value = acc[:, odd * chans : (odd + 1) * chans].reshape(half, PIX, chans)
        pulled[t, :, odd] = value
    low = pulled[t].reshape(PIX * PIX, chans).astype(jnp.bfloat16)
    value = jnp.dot(
        matrices_of(mat_idx, rays, t), low, preferred_element_type=jnp.float32
    ).astype(jnp.bfloat16)
    for k in range(HITS):
        out[send_slot[t * HITS + k]] = value[k * bins : (k + 1) * bins, :]


def tiles_at(tiles, tile_cols, inner):
    return [t for t in range(tiles) if (0 < t % tile_cols < tile_cols - 1) == inner]


def inner_kernel(
    odd, mat_idx, send_slot, scaled, near_a, near_b, kernel, rays,
    pulled, out, cols3, taps, wide, *, tile_cols,
):
    rows, cols, chans = scaled.shape
    f32, bf16 = jnp.float32, jnp.bfloat16
    blank = jnp.zeros((3 * chans, chans), bf16)
    for dr in range(4):
        base = dr * 3 * chans
        for side in range(2):
            lanes = slice(side * chans, (side + 1) * chans)
            tap = dr - side
            if not 0 <= tap < 3:
                taps[base : base + 3 * chans, lanes] = blank
                continue
            for dc in range(3):
                taps[base + dc * chans : base + (dc + 1) * chans, lanes] = kernel[2 - tap, 2 - dc].T
    a, b = near_a[...].astype(f32), near_b[...].astype(f32)
    wide[0, 8 : 8 + cols, :] = pick(odd[0], a, b)
    wide[rows + 1, 8 : 8 + cols, :] = pick(odd[0], b, a)
    wide[1 : rows + 1, 8 : 8 + cols, :] = scaled[...].astype(f32)
    wide[:, 0:8, :] = jnp.zeros((rows + 2, 8, chans), f32)
    wide[:, 8 + cols :, :] = jnp.zeros((rows + 2, 8, chans), f32)
    for dc in range(3):
        value = wide[:, 7 + dc : 7 + dc + cols, :].astype(bf16)
        cols3[:, :, :, dc * chans : (dc + 1) * chans] = value.reshape(
            (rows + 2) // 2, 2, cols, chans
        )
    out[...] = jnp.zeros_like(out)
    for t in tiles_at(pulled.shape[0], tile_cols, True):
        forward_tile(mat_idx, send_slot, taps, rays, pulled, out, cols3, t, tile_cols)


def outer_kernel(
    odd, mat_idx, send_slot, near_a, near_b, taps, rays, _pulled, _out, _cols3,
    pulled, out, cols3, *, tile_cols,
):
    cols = cols3.shape[2]
    chans = pulled.shape[-1]
    group = 16
    spot = lax.broadcasted_iota(jnp.int32, (group, chans), 0)
    a, b = near_a[...], near_b[...]
    left, right = pick(odd[1], a, b), pick(odd[1], b, a)
    for edge, dc, first, at in ((left, 0, 0, 0), (right, 2, cols - group, group - 1)):
        lanes = slice(dc * chans, (dc + 1) * chans)
        for r in range(2 * cols3.shape[0]):
            there = (r // 2, r % 2, slice(first, first + group), lanes)
            value = jnp.where(spot == at, edge[7 + r : 8 + r, :], cols3[there].astype(jnp.float32))
            cols3[there] = value.astype(jnp.bfloat16)
    for t in tiles_at(pulled.shape[0], tile_cols, False):
        forward_tile(mat_idx, send_slot, taps, rays, pulled, out, cols3, t, tile_cols)


def combine_kernel(table, recv, total, low, acc_a, acc_b):
    acc_a[...] = jnp.zeros_like(acc_a)
    acc_b[...] = jnp.zeros_like(acc_b)

    def body(j, carry):
        acc_a[table[2 * j]] += recv[2 * j].astype(jnp.float32)
        acc_b[table[2 * j + 1]] += recv[2 * j + 1].astype(jnp.float32)
        return carry

    lax.fori_loop(0, recv.shape[0] // 2, body, 0, unroll=4)
    n = total.shape[0]
    value = acc_a[:n] + acc_b[:n]
    total[...] = value
    low[...] = value.astype(jnp.bfloat16)


def reply_kernel(table, used, total, other, own_weight, other_weight, out, held):
    n = total.shape[0]
    own = own_weight.shape[0]
    place = used[n]
    for half, weight in enumerate((own_weight, other_weight)):
        first = jnp.where(half == 0, place, n - own - place)
        for b in range(own):
            d = first + b
            scale = used[d].astype(jnp.float32) * weight[b].astype(jnp.float32)
            value = total[d] + other[d].astype(jnp.float32)
            held[d] = (scale * value).astype(jnp.bfloat16)
    held[n] = jnp.zeros(held.shape[1:], jnp.bfloat16)

    def body(j, carry):
        out[j] = held[table[j]]
        return carry

    lax.fori_loop(0, out.shape[0], body, 0, unroll=8)


def rim_kernel(
    odd, mat_idx, send_slot, returned, pulled, grad, state, rays, row_a, row_b, *, tile_cols,
):
    tiles = pulled.shape[0]
    rows, cols, chans = grad.shape
    tile_pix = rays.shape[2]
    f32 = jnp.float32
    lanes = 128
    edges = ((0, 0, slice(0, lanes)), (rows - 1, PIX - 1, slice(tile_pix - lanes, tile_pix)))
    for t in range(tiles):
        c0 = t % tile_cols * PIX
        picked = jnp.concatenate([returned[send_slot[t * HITS + k]] for k in range(HITS)], axis=0)
        for which, (row, line, part) in enumerate(edges):
            if not 0 <= row - t // tile_cols * PIX < PIX:
                continue
            matrix = jnp.concatenate(
                [rays[mat_idx[t * HITS + k], :, part] for k in range(HITS)], axis=0
            )
            backed = lax.dot_general(
                picked, matrix, (((0,), (0,)), ((), ())), preferred_element_type=f32
            ).T
            backed = backed[:PIX] if which == 0 else backed[lanes - PIX :]
            change = pulled[t, line // 2, line % 2] - relax_rate * backed
            adjoint = grad[row, c0 : c0 + PIX, :].astype(f32) + change
            value = state[row, c0 : c0 + PIX, :].astype(f32)
            value = ((1.0 - value * value) * adjoint).astype(jnp.bfloat16)

            @pl.when(odd[0] == which)
            def _():
                row_b[c0 : c0 + PIX, :] = value

            @pl.when(odd[0] != which)
            def _():
                row_a[c0 : c0 + PIX, :] = value


def finish_kernel(
    odd, mat_idx, send_slot, returned, pulled, grad, state, rays, *refs, tile_cols, last,
):
    outs, (whole, mark) = refs[:-2], refs[-2:]
    tiles = pulled.shape[0]
    chans = grad.shape[2]
    f32 = jnp.float32

    def place(t):
        r0, c0 = t // tile_cols * PIX, t % tile_cols * PIX
        return slice(r0, r0 + PIX), slice(c0, c0 + PIX)

    def leave(t):
        where = place(t)
        return pltpu.make_async_copy(whole.at[where], outs[0].at[where], mark.at[t])

    for t in range(tiles):
        picked = jnp.concatenate([returned[send_slot[t * HITS + k]] for k in range(HITS)], axis=0)
        backed = lax.dot_general(
            picked,
            matrices_of(mat_idx, rays, t),
            (((0,), (0,)), ((), ())),
            preferred_element_type=f32,
        ).T
        change = pulled[t].reshape(backed.shape) - relax_rate * backed
        where = place(t)
        adjoint = grad[where].astype(f32) + change.reshape(PIX, PIX, chans)
        if last:
            whole[where] = adjoint
            leave(t).start()
        else:
            value = state[where].astype(f32)
            whole[where] = (1.0 - value * value) * adjoint
    if last:
        for t in range(tiles):
            leave(t).wait()
    else:
        emit_sides(whole[...], odd, *outs)


def on_device(state, grad, kernel, ray_matrix, ray_weight, hits, offsets, block_slot, angle_count):
    f32, bf16, i32 = jnp.float32, jnp.bfloat16, jnp.int32
    rows_dev, cols_dev, chans = state.shape
    angles, spots, bins, tile_pix = ray_matrix.shape
    nr = lax.axis_size("row")
    nx = lax.axis_size("x")
    nc = lax.axis_size(COL)
    devices = nr * nc
    row, zh, zl, x = (lax.axis_index(a) for a in ("row",) + COL)
    tile_rows = rows_dev // PIX
    tile_cols = cols_dev // PIX
    tiles = tile_rows * tile_cols
    pairs = tiles * HITS
    blk_dev = ray_weight.shape[0]
    blocks = blk_dev * devices
    blk_ang = blocks // ANGLES
    cap = 2 * max(2, (pairs + devices - 2) // devices + 1)
    cap = min(cap, pairs)
    peers = nr * 2 * nx
    slots = peers * cap
    dense = 2 * blk_dev

    def exchange(value):
        return lax.ppermute(value, "zh", [(0, 1), (1, 0)])

    everyone = hits.reshape(nr, tile_rows, nc, tile_cols, HITS).transpose(0, 2, 1, 3, 4)
    everyone = everyone.reshape(nr, 2, 2, nx, pairs)
    group = lax.dynamic_index_in_dim(everyone, zh, 1, keepdims=False).reshape(peers, pairs)
    storage = jnp.sum(
        jnp.where(group[:, :, None] == jnp.arange(blocks, dtype=i32), block_slot, 0), axis=2
    )
    owner = storage // blk_dev
    local = storage % blk_dev
    owner_z = (owner % nc) // nx
    owner_zh = owner_z // 2
    owner_zl = owner_z % 2
    peer = ((owner // nc) * 2 + owner_zl) * nx + owner % nx
    place = owner_zh * blk_dev + local
    earlier = jnp.arange(pairs)[None, :] < jnp.arange(pairs)[:, None]
    ranking = jnp.sum(
        ((peer[:, :, None] == peer[:, None, :]) & earlier[None]).astype(i32), axis=2
    )
    me = (row * 2 + zl) * nx + x
    my_hits = lax.dynamic_index_in_dim(group, me, 0, keepdims=False)
    send_slot = lax.dynamic_index_in_dim(peer * cap + ranking, me, 0, keepdims=False)
    matched = (peer[:, None, :] == me) & (
        ranking[:, None, :] == jnp.arange(cap, dtype=i32)[None, :, None]
    )
    table = dense + jnp.sum(jnp.where(matched, place[:, None, :] - dense, 0), axis=2)
    table = table.reshape(slots)
    mat_idx = (my_hits // blk_ang) * spots + offsets.reshape(pairs)

    rays = ray_matrix.reshape(angles * spots, bins, tile_pix)

    block = (bins, chans)
    shape = jax.ShapeDtypeStruct
    slot_out = shape((slots,) + block, bf16)
    edges = (
        shape(state.shape, bf16),
        shape((cols_dev, chans), bf16),
        shape((cols_dev, chans), bf16),
        shape((rows_dev, chans), f32),
        shape((rows_dev, chans), f32),
    )
    odd = jnp.stack([row % 2, (zh * (RING // 2) * nx + zl * nx + x) % 2])

    def limit(mib):
        return pltpu.CompilerParams(vmem_limit_bytes=mib << 20)

    start = pl.pallas_call(
        start_kernel,
        out_shape=edges,
        in_specs=[SMEM] + [ANY] * 2,
        out_specs=(VMEM,) * 5,
        scratch_shapes=[
            pltpu.VMEM(state.shape, bf16),
            pltpu.VMEM(state.shape, bf16),
            pltpu.VMEM(state.shape, f32),
            pltpu.SemaphoreType.DMA((2, 4)),
        ],
        compiler_params=limit(8),
        name="start",
    )
    sides = pl.pallas_call(
        sides_kernel,
        out_shape=[shape((rows_dev + 16, chans), f32)] * 2,
        in_specs=[SMEM] + [VMEM] * 4,
        out_specs=[VMEM] * 2,
        compiler_params=limit(4),
        cost_estimate=pl.CostEstimate(
            flops=4 * rays.size * 512, bytes_accessed=rays.size * 2, transcendentals=0
        ),
        name="sides",
    )
    pulled_out = shape((tiles, PIX // 2, 2, PIX, chans), f32)
    cols3_out = shape(((rows_dev + 2) // 2, 2, cols_dev, 3 * chans), bf16)
    macs = tiles * tile_pix * chans * (9 * chans + HITS * bins)

    def cost(share):
        return pl.CostEstimate(
            flops=2 * macs * share // tiles, bytes_accessed=rays.size * 2, transcendentals=0
        )

    taps_out = shape((4 * 3 * chans, 2 * chans), bf16)

    inner = pl.pallas_call(
        functools.partial(inner_kernel, tile_cols=tile_cols),
        out_shape=(pulled_out, slot_out, cols3_out, taps_out),
        in_specs=[SMEM] * 3 + [VMEM] * 5,
        out_specs=(VMEM,) * 4,
        scratch_shapes=[pltpu.VMEM((rows_dev + 2, cols_dev + 16, chans), f32)],
        compiler_params=limit(16),
        cost_estimate=cost(len(tiles_at(tiles, tile_cols, True))),
        name="inner",
    )
    outer = pl.pallas_call(
        functools.partial(outer_kernel, tile_cols=tile_cols),
        out_shape=(pulled_out, slot_out, cols3_out),
        in_specs=[SMEM] * 3 + [VMEM] * 7,
        out_specs=(VMEM,) * 3,
        input_output_aliases={7: 0, 8: 1, 9: 2},
        compiler_params=limit(16),
        cost_estimate=cost(len(tiles_at(tiles, tile_cols, False))),
        name="outer",
    )
    combine = pl.pallas_call(
        combine_kernel,
        out_shape=(shape((dense,) + block, f32), shape((dense,) + block, bf16)),
        in_specs=[SMEM, VMEM],
        out_specs=(VMEM, VMEM),
        scratch_shapes=[pltpu.VMEM((dense + 1,) + block, f32)] * 2,
        compiler_params=limit(8),
        name="combine",
    )
    reply = pl.pallas_call(
        reply_kernel,
        out_shape=slot_out,
        in_specs=[SMEM] * 2 + [VMEM] * 4,
        out_specs=VMEM,
        scratch_shapes=[pltpu.VMEM((dense + 1,) + block, bf16)],
        compiler_params=limit(8),
        name="reply",
    )

    def finish(last):
        return pl.pallas_call(
            functools.partial(finish_kernel, tile_cols=tile_cols, last=last),
            out_shape=(shape(state.shape, f32),) if last else edges[:1] + edges[3:],
            in_specs=[SMEM] * 3 + [VMEM] * 5,
            out_specs=(ANY,) if last else (VMEM,) * 3,
            scratch_shapes=[
                pltpu.VMEM(state.shape, f32),
                pltpu.SemaphoreType.DMA((tiles,)),
            ],
            compiler_params=limit(20),
            cost_estimate=cost(tiles),
            name="finish",
        )

    rim_of = pl.pallas_call(
        functools.partial(rim_kernel, tile_cols=tile_cols),
        out_shape=edges[1:3],
        in_specs=[SMEM] * 3 + [VMEM] * 5,
        out_specs=(VMEM,) * 2,
        compiler_params=limit(16),
        name="rim",
    )

    dense_z = jnp.arange(dense, dtype=i32) // blk_dev * 2 + zl
    dense_place = (row * nc + dense_z * nx + x) * blk_dev + jnp.arange(dense, dtype=i32) % blk_dev
    own_first = jnp.full((1,), zh * blk_dev, i32)

    def in_use(counts, dense_place, own_first):
        number = jnp.arange(blocks, dtype=i32)
        active = (
            (number % blk_ang).reshape(ANGLES, blk_ang) < counts[:, None]
        ).reshape(1, blocks)
        used = jnp.any((block_slot[None, :] == dense_place[:, None]) & active, axis=1).astype(i32)
        return jnp.concatenate([used, own_first])

    def across(value):
        value = value.reshape((peers, cap) + block)
        value = lax.all_to_all(value, GROUP, split_axis=0, concat_axis=0, tiled=True)
        return value.reshape((slots,) + block)

    def swaps(value_a, value_b, axis):
        count = lax.axis_size(axis)
        even = [(i, i ^ 1) for i in range(count)]
        uneven = [(i, ((i + 1) ^ 1) - 1) for i in range(1, count - 1)]
        return lax.ppermute(value_a, axis, even), lax.ppermute(value_b, axis, uneven)

    def apart(value):
        return pltpu.with_memory_space_constraint(value, pltpu.HBM)

    def forward(early, scaled, row_a, row_b, col_a, col_b):
        above = swaps(row_a, row_b, "row")
        side_a, side_b = sides(odd, *above, col_a, col_b)
        other_weight = None
        if early:
            side_b, weight = lax.optimization_barrier((side_b, ray_weight.astype(bf16)))
            other_weight = exchange(weight)
        beside = swaps(side_a, side_b, COL)
        *parts, taps = inner(odd, mat_idx, send_slot, scaled, *above, kernel, rays)
        pulled, outgoing, _ = outer(odd, mat_idx, send_slot, *beside, taps, rays, *parts)
        return pulled, outgoing, other_weight

    scaled, *rim = start(odd, apart(state), apart(grad))
    for turn in range(ITERS):
        pulled, outgoing, swapped = forward(turn == 0, scaled, *rim)
        if not turn:
            other_weight = swapped
            outgoing, table, other_weight, dense_place, own_first = lax.optimization_barrier(
                (outgoing, table, other_weight, dense_place, own_first)
            )
        total, mine = combine(table, across(outgoing))
        if not turn:
            mine, *own = lax.optimization_barrier((mine, angle_count, dense_place, own_first))
            used = in_use(*own)
        replies = reply(table, used, total, exchange(mine), ray_weight, other_weight)
        last = turn == ITERS - 1
        given = (odd, mat_idx, send_slot, across(replies), pulled, grad, state, rays)
        scaled, *sides_of = finish(last)(*given)
        if not last:
            rim = (*rim_of(*given), *sides_of)
    return scaled


def solution(mesh):
    nr, nc = mesh.devices.shape
    fine = Mesh(mesh.devices.reshape(nr, 2, RING // 2, nc // RING), ("row",) + COL)
    image = P("row", COL, None)
    placed = (
        image,
        image,
        P(),
        P(),
        P(("row",) + COL, None, None),
        P(),
        image,
        P(),
        P(),
    )
    return jax.shard_map(
        on_device, mesh=fine, in_specs=placed, out_specs=image, check_vma=False
    )
```

```python
import functools

import jax
import jax.numpy as jnp
from jax import lax
from jax.experimental import pallas as pl
from jax.experimental.pallas import tpu as pltpu
from jax.sharding import Mesh, PartitionSpec as P

PIX = 32
ANGLES = 8
HITS = 16
ITERS = 2
RING = 4

relax_rate = 0.25

COL = ("zh", "zl", "x")
GROUP = ("row", "zl", "x")

VMEM = pl.BlockSpec(memory_space=pltpu.VMEM)
SMEM = pl.BlockSpec(memory_space=pltpu.SMEM)
ANY = pl.BlockSpec(memory_space=pl.ANY)


def start_kernel(odd, state, grad, scaled, row_a, row_b, col_a, col_b, states, grads, whole, mark):
    parts = mark.shape[1]
    rows = states.shape[0] // parts

    def load(a, p):
        source, held = ((state, states), (grad, grads))[a]
        where = pl.ds(p * rows, rows)
        return pltpu.make_async_copy(source.at[where], held.at[where], mark.at[a, p])

    for p in range(parts):
        for a in range(2):
            load(a, p).start()
    for p in range(parts):
        for a in range(2):
            load(a, p).wait()
        where = slice(p * rows, (p + 1) * rows)
        value = states[where].astype(jnp.float32)
        whole[where] = (1.0 - value * value) * grads[where].astype(jnp.float32)
    emit_edges(whole[...], odd, scaled, row_a, row_b, col_a, col_b)


def pick(flag, yes, no):
    return jnp.where(flag == 1, yes, no)


def emit_edges(value, odd, scaled, row_a, row_b, col_a, col_b):
    rows, cols = value.shape[:2]
    scaled[...] = value.astype(jnp.bfloat16)
    row_a[...] = pick(odd[0], value[0], value[rows - 1]).astype(jnp.bfloat16)
    row_b[...] = pick(odd[0], value[rows - 1], value[0]).astype(jnp.bfloat16)
    left, right = value[:, 0, :], value[:, cols - 1, :]
    col_a[...] = pick(odd[1], left, right)
    col_b[...] = pick(odd[1], right, left)


def sides_kernel(odd, near_a, near_b, col_a, col_b, out_a, out_b):
    rows = col_a.shape[0]
    cols = near_a.shape[0]
    f32 = jnp.float32

    def ends(ref):
        low = ref[0:16, :].astype(f32)[0:1, :]
        high = ref[cols - 16 : cols, :].astype(f32)[15:16, :]
        return low, high

    a, b = ends(near_a), ends(near_b)
    above = [pick(odd[0], a[i], b[i]) for i in range(2)]
    below = [pick(odd[0], b[i], a[i]) for i in range(2)]
    for out, edge, order in ((out_a, col_a, (0, 1)), (out_b, col_b, (1, 0))):
        yes, no = order
        out[8 : 8 + rows, :] = edge[...]
        out[7:8, :] = pick(odd[1], above[yes], above[no])
        out[8 + rows : 9 + rows, :] = pick(odd[1], below[yes], below[no])


def matrices_of(mat_idx, rays, t):
    return jnp.concatenate([rays[mat_idx[t * HITS + k]] for k in range(HITS)], axis=0)


def forward_tile(mat_idx, send_slot, taps, rays, pulled, out, cols3, t, tile_cols):
    chans = pulled.shape[-1]
    bins = rays.shape[1]
    half = PIX // 2
    r0, c0 = t // tile_cols * half, t % tile_cols * PIX
    window = jnp.concatenate(
        [
            cols3[r0 + dr // 2 : r0 + dr // 2 + half, dr % 2, c0 : c0 + PIX, :].reshape(
                half * PIX, 3 * chans
            )
            for dr in range(4)
        ],
        axis=1,
    )
    acc = jnp.dot(window, taps[...], preferred_element_type=jnp.float32)
    for odd in range(2):
        value = acc[:, odd * chans : (odd + 1) * chans].reshape(half, PIX, chans)
        pulled[t, :, odd] = value
    low = pulled[t].reshape(PIX * PIX, chans).astype(jnp.bfloat16)
    value = jnp.dot(
        matrices_of(mat_idx, rays, t), low, preferred_element_type=jnp.float32
    ).astype(jnp.bfloat16)
    for k in range(HITS):
        out[send_slot[t * HITS + k]] = value[k * bins : (k + 1) * bins, :]


def tiles_at(tiles, tile_cols, inner):
    return [t for t in range(tiles) if (0 < t % tile_cols < tile_cols - 1) == inner]


def spread(rows, wide, cols3, first):
    count, cols, chans = rows.shape
    f32, bf16 = jnp.float32, jnp.bfloat16
    blank = jnp.zeros((count, 8, chans), f32)
    wide[:, 0:8, :] = blank
    wide[:, 8 + cols : 16 + cols, :] = blank
    wide[:, 8 : 8 + cols, :] = rows.astype(f32)
    for dc in range(3):
        lanes = slice(dc * chans, (dc + 1) * chans)
        value = wide[:, 7 + dc : 7 + dc + cols, :].astype(bf16)
        for r in range(count):
            cols3[(first + r) // 2, (first + r) % 2, :, lanes] = value[r]


def centre_kernel(scaled, kernel, out, cols3, taps, wide):
    chans = scaled.shape[2]
    blank = jnp.zeros((3 * chans, chans), jnp.bfloat16)
    for dr in range(4):
        base = dr * 3 * chans
        for side in range(2):
            lanes = slice(side * chans, (side + 1) * chans)
            tap = dr - side
            if not 0 <= tap < 3:
                taps[base : base + 3 * chans, lanes] = blank
                continue
            for dc in range(3):
                taps[base + dc * chans : base + (dc + 1) * chans, lanes] = kernel[2 - tap, 2 - dc].T
    spread(scaled[...], wide, cols3, 1)
    out[...] = jnp.zeros_like(out)


def inner_kernel(
    odd, mat_idx, send_slot, near_a, near_b, taps, rays, _out, _cols3,
    pulled, out, cols3, wide, *, tile_cols,
):
    a, b = near_a[...], near_b[...]
    last = 2 * cols3.shape[0] - 1
    spread(pick(odd[0], a, b)[None], wide, cols3, 0)
    spread(pick(odd[0], b, a)[None], wide, cols3, last)
    for t in tiles_at(pulled.shape[0], tile_cols, True):
        forward_tile(mat_idx, send_slot, taps, rays, pulled, out, cols3, t, tile_cols)


def outer_kernel(
    odd, mat_idx, send_slot, near_a, near_b, taps, rays, _pulled, _out, _cols3,
    pulled, out, cols3, *, tile_cols,
):
    cols = cols3.shape[2]
    chans = pulled.shape[-1]
    group = 16
    spot = lax.broadcasted_iota(jnp.int32, (group, chans), 0)
    a, b = near_a[...], near_b[...]
    left, right = pick(odd[1], a, b), pick(odd[1], b, a)
    for edge, dc, first, at in ((left, 0, 0, 0), (right, 2, cols - group, group - 1)):
        lanes = slice(dc * chans, (dc + 1) * chans)
        for r in range(2 * cols3.shape[0]):
            there = (r // 2, r % 2, slice(first, first + group), lanes)
            value = jnp.where(spot == at, edge[7 + r : 8 + r, :], cols3[there].astype(jnp.float32))
            cols3[there] = value.astype(jnp.bfloat16)
    for t in tiles_at(pulled.shape[0], tile_cols, False):
        forward_tile(mat_idx, send_slot, taps, rays, pulled, out, cols3, t, tile_cols)


def combine_kernel(table, recv, total, low, acc_a, acc_b):
    acc_a[...] = jnp.zeros_like(acc_a)
    acc_b[...] = jnp.zeros_like(acc_b)

    def body(j, carry):
        acc_a[table[2 * j]] += recv[2 * j].astype(jnp.float32)
        acc_b[table[2 * j + 1]] += recv[2 * j + 1].astype(jnp.float32)
        return carry

    lax.fori_loop(0, recv.shape[0] // 2, body, 0, unroll=4)
    n = total.shape[0]
    value = acc_a[:n] + acc_b[:n]
    total[...] = value
    low[...] = value.astype(jnp.bfloat16)


def reply_kernel(table, used, total, other, own_weight, other_weight, out, held):
    n = total.shape[0]
    own = own_weight.shape[0]
    place = used[n]
    for half, weight in enumerate((own_weight, other_weight)):
        first = jnp.where(half == 0, place, n - own - place)
        for b in range(own):
            d = first + b
            scale = used[d].astype(jnp.float32) * weight[b].astype(jnp.float32)
            value = total[d] + other[d].astype(jnp.float32)
            held[d] = (scale * value).astype(jnp.bfloat16)
    held[n] = jnp.zeros(held.shape[1:], jnp.bfloat16)

    def body(j, carry):
        out[j] = held[table[j]]
        return carry

    lax.fori_loop(0, out.shape[0], body, 0, unroll=8)


def finish_kernel(
    odd, mat_idx, send_slot, returned, pulled, grad, state, rays, *refs, tile_cols, last,
):
    outs, (whole, mark) = refs[:-2], refs[-2:]
    tiles = pulled.shape[0]
    chans = grad.shape[2]
    f32 = jnp.float32

    def place(t):
        r0, c0 = t // tile_cols * PIX, t % tile_cols * PIX
        return slice(r0, r0 + PIX), slice(c0, c0 + PIX)

    def leave(t):
        where = place(t)
        return pltpu.make_async_copy(whole.at[where], outs[0].at[where], mark.at[t])

    for t in range(tiles):
        picked = jnp.concatenate([returned[send_slot[t * HITS + k]] for k in range(HITS)], axis=0)
        backed = lax.dot_general(
            picked,
            matrices_of(mat_idx, rays, t),
            (((0,), (0,)), ((), ())),
            preferred_element_type=f32,
        ).T
        change = pulled[t].reshape(backed.shape) - relax_rate * backed
        where = place(t)
        adjoint = grad[where].astype(f32) + change.reshape(PIX, PIX, chans)
        if last:
            whole[where] = adjoint
            leave(t).start()
        else:
            value = state[where].astype(f32)
            whole[where] = (1.0 - value * value) * adjoint
    if last:
        for t in range(tiles):
            leave(t).wait()
    else:
        emit_edges(whole[...], odd, *outs)


def on_device(state, grad, kernel, ray_matrix, ray_weight, hits, offsets, block_slot, angle_count):
    f32, bf16, i32 = jnp.float32, jnp.bfloat16, jnp.int32
    rows_dev, cols_dev, chans = state.shape
    angles, spots, bins, tile_pix = ray_matrix.shape
    nr = lax.axis_size("row")
    nx = lax.axis_size("x")
    nc = lax.axis_size(COL)
    devices = nr * nc
    row, zh, zl, x = (lax.axis_index(a) for a in ("row",) + COL)
    tile_rows = rows_dev // PIX
    tile_cols = cols_dev // PIX
    tiles = tile_rows * tile_cols
    pairs = tiles * HITS
    blk_dev = ray_weight.shape[0]
    blocks = blk_dev * devices
    blk_ang = blocks // ANGLES
    cap = 2 * max(2, (pairs + devices - 2) // devices + 1)
    cap = min(cap, pairs)
    peers = nr * 2 * nx
    slots = peers * cap
    dense = 2 * blk_dev

    def exchange(value):
        return lax.ppermute(value, "zh", [(0, 1), (1, 0)])

    everyone = hits.reshape(nr, tile_rows, nc, tile_cols, HITS).transpose(0, 2, 1, 3, 4)
    everyone = everyone.reshape(nr, 2, 2, nx, pairs)
    group = lax.dynamic_index_in_dim(everyone, zh, 1, keepdims=False).reshape(peers, pairs)
    storage = jnp.sum(
        jnp.where(group[:, :, None] == jnp.arange(blocks, dtype=i32), block_slot, 0), axis=2
    )
    owner = storage // blk_dev
    local = storage % blk_dev
    owner_z = (owner % nc) // nx
    owner_zh = owner_z // 2
    owner_zl = owner_z % 2
    peer = ((owner // nc) * 2 + owner_zl) * nx + owner % nx
    place = owner_zh * blk_dev + local
    earlier = jnp.arange(pairs)[None, :] < jnp.arange(pairs)[:, None]
    ranking = jnp.sum(
        ((peer[:, :, None] == peer[:, None, :]) & earlier[None]).astype(i32), axis=2
    )
    me = (row * 2 + zl) * nx + x
    my_hits = lax.dynamic_index_in_dim(group, me, 0, keepdims=False)
    send_slot = lax.dynamic_index_in_dim(peer * cap + ranking, me, 0, keepdims=False)
    matched = (peer[:, None, :] == me) & (
        ranking[:, None, :] == jnp.arange(cap, dtype=i32)[None, :, None]
    )
    table = dense + jnp.sum(jnp.where(matched, place[:, None, :] - dense, 0), axis=2)
    table = table.reshape(slots)
    mat_idx = (my_hits // blk_ang) * spots + offsets.reshape(pairs)

    rays = ray_matrix.reshape(angles * spots, bins, tile_pix)

    block = (bins, chans)
    shape = jax.ShapeDtypeStruct
    slot_out = shape((slots,) + block, bf16)
    edges = (
        shape(state.shape, bf16),
        shape((cols_dev, chans), bf16),
        shape((cols_dev, chans), bf16),
        shape((rows_dev, chans), f32),
        shape((rows_dev, chans), f32),
    )
    odd = jnp.stack([row % 2, (zh * (RING // 2) * nx + zl * nx + x) % 2])

    def limit(mib):
        return pltpu.CompilerParams(vmem_limit_bytes=mib << 20)

    start = pl.pallas_call(
        start_kernel,
        out_shape=edges,
        in_specs=[SMEM] + [ANY] * 2,
        out_specs=(VMEM,) * 5,
        scratch_shapes=[
            pltpu.VMEM(state.shape, bf16),
            pltpu.VMEM(state.shape, bf16),
            pltpu.VMEM(state.shape, f32),
            pltpu.SemaphoreType.DMA((2, 4)),
        ],
        compiler_params=limit(8),
        name="start",
    )
    sides = pl.pallas_call(
        sides_kernel,
        out_shape=[shape((rows_dev + 16, chans), f32)] * 2,
        in_specs=[SMEM] + [VMEM] * 4,
        out_specs=[VMEM] * 2,
        compiler_params=limit(4),
        cost_estimate=pl.CostEstimate(
            flops=4 * rays.size * 512, bytes_accessed=rays.size * 2, transcendentals=0
        ),
        name="sides",
    )
    pulled_out = shape((tiles, PIX // 2, 2, PIX, chans), f32)
    cols3_out = shape(((rows_dev + 2) // 2, 2, cols_dev, 3 * chans), bf16)
    macs = tiles * tile_pix * chans * (9 * chans + HITS * bins)

    def cost(share):
        return pl.CostEstimate(
            flops=2 * macs * share // tiles, bytes_accessed=rays.size * 2, transcendentals=0
        )

    taps_out = shape((4 * 3 * chans, 2 * chans), bf16)

    centre = pl.pallas_call(
        centre_kernel,
        out_shape=(slot_out, cols3_out, taps_out),
        in_specs=[VMEM] * 2,
        out_specs=(VMEM,) * 3,
        scratch_shapes=[pltpu.VMEM((rows_dev, cols_dev + 16, chans), f32)],
        compiler_params=limit(12),
        cost_estimate=cost(1),
        name="centre",
    )
    inner = pl.pallas_call(
        functools.partial(inner_kernel, tile_cols=tile_cols),
        out_shape=(pulled_out, slot_out, cols3_out),
        in_specs=[SMEM] * 3 + [VMEM] * 6,
        out_specs=(VMEM,) * 3,
        scratch_shapes=[pltpu.VMEM((1, cols_dev + 16, chans), f32)],
        input_output_aliases={7: 1, 8: 2},
        compiler_params=limit(12),
        cost_estimate=cost(len(tiles_at(tiles, tile_cols, True))),
        name="inner",
    )
    outer = pl.pallas_call(
        functools.partial(outer_kernel, tile_cols=tile_cols),
        out_shape=(pulled_out, slot_out, cols3_out),
        in_specs=[SMEM] * 3 + [VMEM] * 7,
        out_specs=(VMEM,) * 3,
        input_output_aliases={7: 0, 8: 1, 9: 2},
        compiler_params=limit(16),
        cost_estimate=cost(len(tiles_at(tiles, tile_cols, False))),
        name="outer",
    )
    combine = pl.pallas_call(
        combine_kernel,
        out_shape=(shape((dense,) + block, f32), shape((dense,) + block, bf16)),
        in_specs=[SMEM, VMEM],
        out_specs=(VMEM, VMEM),
        scratch_shapes=[pltpu.VMEM((dense + 1,) + block, f32)] * 2,
        compiler_params=limit(8),
        name="combine",
    )
    reply = pl.pallas_call(
        reply_kernel,
        out_shape=slot_out,
        in_specs=[SMEM] * 2 + [VMEM] * 4,
        out_specs=VMEM,
        scratch_shapes=[pltpu.VMEM((dense + 1,) + block, bf16)],
        compiler_params=limit(8),
        name="reply",
    )

    def finish(last):
        return pl.pallas_call(
            functools.partial(finish_kernel, tile_cols=tile_cols, last=last),
            out_shape=(shape(state.shape, f32),) if last else edges,
            in_specs=[SMEM] * 3 + [VMEM] * 5,
            out_specs=(ANY,) if last else (VMEM,) * 5,
            scratch_shapes=[
                pltpu.VMEM(state.shape, f32),
                pltpu.SemaphoreType.DMA((tiles,)),
            ],
            compiler_params=limit(20),
            cost_estimate=cost(tiles),
            name="finish",
        )

    dense_z = jnp.arange(dense, dtype=i32) // blk_dev * 2 + zl
    dense_place = (row * nc + dense_z * nx + x) * blk_dev + jnp.arange(dense, dtype=i32) % blk_dev
    own_first = jnp.full((1,), zh * blk_dev, i32)

    def in_use(counts, dense_place, own_first):
        number = jnp.arange(blocks, dtype=i32)
        active = (
            (number % blk_ang).reshape(ANGLES, blk_ang) < counts[:, None]
        ).reshape(1, blocks)
        used = jnp.any((block_slot[None, :] == dense_place[:, None]) & active, axis=1).astype(i32)
        return jnp.concatenate([used, own_first])

    def across(value):
        value = value.reshape((peers, cap) + block)
        value = lax.all_to_all(value, GROUP, split_axis=0, concat_axis=0, tiled=True)
        return value.reshape((slots,) + block)

    def swaps(value_a, value_b, axis):
        count = lax.axis_size(axis)
        even = [(i, i ^ 1) for i in range(count)]
        uneven = [(i, ((i + 1) ^ 1) - 1) for i in range(1, count - 1)]
        return lax.ppermute(value_a, axis, even), lax.ppermute(value_b, axis, uneven)

    def apart(value):
        return pltpu.with_memory_space_constraint(value, pltpu.HBM)

    def forward(early, scaled, row_a, row_b, col_a, col_b):
        above = swaps(row_a, row_b, "row")
        side_a, side_b = sides(odd, *above, col_a, col_b)
        other_weight = None
        if early:
            side_b, weight, scaled = lax.optimization_barrier(
                (side_b, ray_weight.astype(bf16), scaled)
            )
            other_weight = exchange(weight)
        beside = swaps(side_a, side_b, COL)
        outgoing, cols3, taps = centre(scaled, kernel)
        parts = inner(odd, mat_idx, send_slot, *above, taps, rays, outgoing, cols3)
        pulled, outgoing, _ = outer(odd, mat_idx, send_slot, *beside, taps, rays, *parts)
        return pulled, outgoing, other_weight

    scaled, *rim = start(odd, apart(state), apart(grad))
    for turn in range(ITERS):
        pulled, outgoing, swapped = forward(turn == 0, scaled, *rim)
        if not turn:
            other_weight = swapped
            outgoing, table, other_weight, dense_place, own_first = lax.optimization_barrier(
                (outgoing, table, other_weight, dense_place, own_first)
            )
        total, mine = combine(table, across(outgoing))
        if not turn:
            mine, *own = lax.optimization_barrier((mine, angle_count, dense_place, own_first))
            used = in_use(*own)
        replies = reply(table, used, total, exchange(mine), ray_weight, other_weight)
        last = turn == ITERS - 1
        scaled, *rim = finish(last)(
            odd, mat_idx, send_slot, across(replies), pulled, grad, state, rays
        )
    return scaled


def solution(mesh):
    nr, nc = mesh.devices.shape
    fine = Mesh(mesh.devices.reshape(nr, 2, RING // 2, nc // RING), ("row",) + COL)
    image = P("row", COL, None)
    placed = (
        image,
        image,
        P(),
        P(),
        P(("row",) + COL, None, None),
        P(),
        image,
        P(),
        P(),
    )
    return jax.shard_map(
        on_device, mesh=fine, in_specs=placed, out_specs=image, check_vma=False
    )
```

```python
import functools

import jax
import jax.numpy as jnp
from jax import lax
from jax.experimental import pallas as pl
from jax.experimental.pallas import tpu as pltpu
from jax.sharding import Mesh, PartitionSpec as P

PIX = 32
ANGLES = 8
HITS = 16
ITERS = 2
RING = 4

relax_rate = 0.25

COL = ("zh", "zl", "x")
GROUP = ("row", "zl", "x")

VMEM = pl.BlockSpec(memory_space=pltpu.VMEM)
SMEM = pl.BlockSpec(memory_space=pltpu.SMEM)
ANY = pl.BlockSpec(memory_space=pl.ANY)


def start_kernel(state, grad, scaled, row_a, row_b, col_a, col_b, states, grads, whole, mark):
    parts = mark.shape[1]
    rows = states.shape[0] // parts

    def load(a, p):
        source, held = ((state, states), (grad, grads))[a]
        where = pl.ds(p * rows, rows)
        return pltpu.make_async_copy(source.at[where], held.at[where], mark.at[a, p])

    for p in range(parts):
        for a in range(2):
            load(a, p).start()
    for p in range(parts):
        for a in range(2):
            load(a, p).wait()
        where = slice(p * rows, (p + 1) * rows)
        value = states[where].astype(jnp.float32)
        whole[where] = (1.0 - value * value) * grads[where].astype(jnp.float32)
    emit_edges(whole[...], scaled, row_a, row_b, col_a, col_b)


def parity(dim):
    if dim == 0:
        return lax.axis_index("row") % 2
    return (lax.axis_index("zl") * lax.axis_size("x") + lax.axis_index("x")) % 2


def pick(dim, yes, no):
    return jnp.where(parity(dim) == 1, yes, no)


def emit_edges(value, scaled, row_a, row_b, col_a, col_b):
    rows, cols = value.shape[:2]
    scaled[...] = value.astype(jnp.bfloat16)
    row_a[...] = pick(0, value[0], value[rows - 1]).astype(jnp.bfloat16)
    row_b[...] = pick(0, value[rows - 1], value[0]).astype(jnp.bfloat16)
    left, right = value[:, 0, :], value[:, cols - 1, :]
    col_a[...] = pick(1, left, right)
    col_b[...] = pick(1, right, left)


def sides_kernel(near_a, near_b, col_a, col_b, out_a, out_b):
    rows = col_a.shape[0]
    cols = near_a.shape[0]
    f32 = jnp.float32

    def ends(ref):
        low = ref[0:16, :].astype(f32)[0:1, :]
        high = ref[cols - 16 : cols, :].astype(f32)[15:16, :]
        return low, high

    a, b = ends(near_a), ends(near_b)
    above = [pick(0, a[i], b[i]) for i in range(2)]
    below = [pick(0, b[i], a[i]) for i in range(2)]
    for out, edge, order in ((out_a, col_a, (0, 1)), (out_b, col_b, (1, 0))):
        yes, no = order
        out[8 : 8 + rows, :] = edge[...]
        out[7:8, :] = pick(1, above[yes], above[no])
        out[8 + rows : 9 + rows, :] = pick(1, below[yes], below[no])


def matrices_of(routes, rays, t):
    return jnp.concatenate([rays[routes[t * HITS + k]] for k in range(HITS)], axis=0)


def forward_tile(routes, taps, rays, pulled, out, cols3, t, tile_cols):
    chans = pulled.shape[-1]
    bins = rays.shape[1]
    slot = pulled.shape[0] * HITS
    half = PIX // 2
    r0, c0 = t // tile_cols * half, t % tile_cols * PIX
    window = jnp.concatenate(
        [
            cols3[r0 + dr // 2 : r0 + dr // 2 + half, dr % 2, c0 : c0 + PIX, :].reshape(
                half * PIX, 3 * chans
            )
            for dr in range(4)
        ],
        axis=1,
    )
    acc = jnp.dot(window, taps[...], preferred_element_type=jnp.float32)
    for odd in range(2):
        value = acc[:, odd * chans : (odd + 1) * chans].reshape(half, PIX, chans)
        pulled[t, :, odd] = value
    low = pulled[t].reshape(PIX * PIX, chans).astype(jnp.bfloat16)
    value = jnp.dot(
        matrices_of(routes, rays, t), low, preferred_element_type=jnp.float32
    ).astype(jnp.bfloat16)
    for k in range(HITS):
        out[routes[slot + t * HITS + k]] = value[k * bins : (k + 1) * bins, :]


def tiles_at(tiles, tile_cols, inner):
    return [t for t in range(tiles) if (0 < t % tile_cols < tile_cols - 1) == inner]


def inner_kernel(
    routes, scaled, near_a, near_b, kernel, rays,
    pulled, out, cols3, taps, wide, *, tile_cols,
):
    rows, cols, chans = scaled.shape
    f32, bf16 = jnp.float32, jnp.bfloat16
    blank = jnp.zeros((3 * chans, chans), bf16)
    for dr in range(4):
        base = dr * 3 * chans
        for side in range(2):
            lanes = slice(side * chans, (side + 1) * chans)
            tap = dr - side
            if not 0 <= tap < 3:
                taps[base : base + 3 * chans, lanes] = blank
                continue
            for dc in range(3):
                taps[base + dc * chans : base + (dc + 1) * chans, lanes] = kernel[2 - tap, 2 - dc].T
    a, b = near_a[...].astype(f32), near_b[...].astype(f32)
    wide[0, 8 : 8 + cols, :] = pick(0, a, b)
    wide[rows + 1, 8 : 8 + cols, :] = pick(0, b, a)
    wide[1 : rows + 1, 8 : 8 + cols, :] = scaled[...].astype(f32)
    wide[:, 0:8, :] = jnp.zeros((rows + 2, 8, chans), f32)
    wide[:, 8 + cols :, :] = jnp.zeros((rows + 2, 8, chans), f32)
    for dc in range(3):
        value = wide[:, 7 + dc : 7 + dc + cols, :].astype(bf16)
        cols3[:, :, :, dc * chans : (dc + 1) * chans] = value.reshape(
            (rows + 2) // 2, 2, cols, chans
        )
    out[...] = jnp.zeros_like(out)
    for t in tiles_at(pulled.shape[0], tile_cols, True):
        forward_tile(routes, taps, rays, pulled, out, cols3, t, tile_cols)


def outer_kernel(
    routes, near_a, near_b, taps, rays, _pulled, _out, _cols3,
    pulled, out, cols3, *, tile_cols,
):
    cols = cols3.shape[2]
    chans = pulled.shape[-1]
    group = 16
    spot = lax.broadcasted_iota(jnp.int32, (group, chans), 0)
    a, b = near_a[...], near_b[...]
    left, right = pick(1, a, b), pick(1, b, a)
    for edge, dc, first, at in ((left, 0, 0, 0), (right, 2, cols - group, group - 1)):
        lanes = slice(dc * chans, (dc + 1) * chans)
        for r in range(2 * cols3.shape[0]):
            there = (r // 2, r % 2, slice(first, first + group), lanes)
            value = jnp.where(spot == at, edge[7 + r : 8 + r, :], cols3[there].astype(jnp.float32))
            cols3[there] = value.astype(jnp.bfloat16)
    for t in tiles_at(pulled.shape[0], tile_cols, False):
        forward_tile(routes, taps, rays, pulled, out, cols3, t, tile_cols)


def combine_kernel(table, recv, total, low, acc_a, acc_b):
    acc_a[...] = jnp.zeros_like(acc_a)
    acc_b[...] = jnp.zeros_like(acc_b)

    def body(j, carry):
        acc_a[table[2 * j]] += recv[2 * j].astype(jnp.float32)
        acc_b[table[2 * j + 1]] += recv[2 * j + 1].astype(jnp.float32)
        return carry

    lax.fori_loop(0, recv.shape[0] // 2, body, 0, unroll=4)
    n = total.shape[0]
    value = acc_a[:n] + acc_b[:n]
    total[...] = value
    low[...] = value.astype(jnp.bfloat16)


def reply_kernel(table, used, total, other, own_weight, other_weight, out, held):
    n = total.shape[0]
    own = own_weight.shape[0]
    place = used[n]
    for half, weight in enumerate((own_weight, other_weight)):
        first = jnp.where(half == 0, place, n - own - place)
        for b in range(own):
            d = first + b
            scale = used[d].astype(jnp.float32) * weight[b].astype(jnp.float32)
            value = total[d] + other[d].astype(jnp.float32)
            held[d] = (scale * value).astype(jnp.bfloat16)
    held[n] = jnp.zeros(held.shape[1:], jnp.bfloat16)

    def body(j, carry):
        out[j] = held[table[j]]
        return carry

    lax.fori_loop(0, out.shape[0], body, 0, unroll=8)


def finish_kernel(
    routes, returned, pulled, grad, state, rays, *refs, tile_cols, last,
):
    outs, (whole, mark) = refs[:-2], refs[-2:]
    tiles = pulled.shape[0]
    slot = tiles * HITS
    chans = grad.shape[2]
    f32 = jnp.float32

    def place(t):
        r0, c0 = t // tile_cols * PIX, t % tile_cols * PIX
        return slice(r0, r0 + PIX), slice(c0, c0 + PIX)

    def leave(t):
        where = place(t)
        return pltpu.make_async_copy(whole.at[where], outs[0].at[where], mark.at[t])

    for t in range(tiles):
        picked = jnp.concatenate([returned[routes[slot + t * HITS + k]] for k in range(HITS)], axis=0)
        backed = lax.dot_general(
            picked,
            matrices_of(routes, rays, t),
            (((0,), (0,)), ((), ())),
            preferred_element_type=f32,
        ).T
        change = pulled[t].reshape(backed.shape) - relax_rate * backed
        where = place(t)
        adjoint = grad[where].astype(f32) + change.reshape(PIX, PIX, chans)
        if last:
            whole[where] = adjoint
            leave(t).start()
        else:
            value = state[where].astype(f32)
            whole[where] = (1.0 - value * value) * adjoint
    if last:
        for t in range(tiles):
            leave(t).wait()
    else:
        emit_edges(whole[...], *outs)


def on_device(state, grad, kernel, ray_matrix, ray_weight, hits, offsets, block_slot, angle_count):
    f32, bf16, i32 = jnp.float32, jnp.bfloat16, jnp.int32
    rows_dev, cols_dev, chans = state.shape
    angles, spots, bins, tile_pix = ray_matrix.shape
    nr = lax.axis_size("row")
    nx = lax.axis_size("x")
    nc = lax.axis_size(COL)
    devices = nr * nc
    row, zh, zl, x = (lax.axis_index(a) for a in ("row",) + COL)
    tile_rows = rows_dev // PIX
    tile_cols = cols_dev // PIX
    tiles = tile_rows * tile_cols
    pairs = tiles * HITS
    blk_dev = ray_weight.shape[0]
    blocks = blk_dev * devices
    blk_ang = blocks // ANGLES
    cap = 2 * max(2, (pairs + devices - 2) // devices + 1)
    cap = min(cap, pairs)
    peers = nr * 2 * nx
    slots = peers * cap
    dense = 2 * blk_dev

    def exchange(value):
        return lax.ppermute(value, "zh", [(0, 1), (1, 0)])

    everyone = hits.reshape(nr, tile_rows, nc, tile_cols, HITS).transpose(0, 2, 1, 3, 4)
    everyone = everyone.reshape(nr, 2, 2, nx, pairs)
    group = lax.dynamic_index_in_dim(everyone, zh, 1, keepdims=False).reshape(peers, pairs)
    storage = jnp.sum(
        jnp.where(group[:, :, None] == jnp.arange(blocks, dtype=i32), block_slot, 0), axis=2
    )
    owner = storage // blk_dev
    local = storage % blk_dev
    owner_z = (owner % nc) // nx
    owner_zh = owner_z // 2
    owner_zl = owner_z % 2
    peer = ((owner // nc) * 2 + owner_zl) * nx + owner % nx
    place = owner_zh * blk_dev + local
    earlier = jnp.arange(pairs)[None, :] < jnp.arange(pairs)[:, None]
    ranking = jnp.sum(
        ((peer[:, :, None] == peer[:, None, :]) & earlier[None]).astype(i32), axis=2
    )
    me = (row * 2 + zl) * nx + x
    my_hits = lax.dynamic_index_in_dim(group, me, 0, keepdims=False)
    send_slot = lax.dynamic_index_in_dim(peer * cap + ranking, me, 0, keepdims=False)
    matched = (peer[:, None, :] == me) & (
        ranking[:, None, :] == jnp.arange(cap, dtype=i32)[None, :, None]
    )
    table = dense + jnp.sum(jnp.where(matched, place[:, None, :] - dense, 0), axis=2)
    table = table.reshape(slots)
    mat_idx = (my_hits // blk_ang) * spots + offsets.reshape(pairs)
    routes = jnp.concatenate([mat_idx, send_slot])

    dense_z = jnp.arange(dense, dtype=i32) // blk_dev * 2 + zl
    dense_place = (row * nc + dense_z * nx + x) * blk_dev + jnp.arange(dense, dtype=i32) % blk_dev
    number = jnp.arange(blocks, dtype=i32)
    active = (
        (number % blk_ang).reshape(ANGLES, blk_ang) < angle_count[:, None]
    ).reshape(1, blocks)
    used = jnp.any((block_slot[None, :] == dense_place[:, None]) & active, axis=1).astype(i32)
    used = jnp.concatenate([used, jnp.full((1,), zh * blk_dev, i32)])

    rays = ray_matrix.reshape(angles * spots, bins, tile_pix)

    block = (bins, chans)
    shape = jax.ShapeDtypeStruct
    slot_out = shape((slots,) + block, bf16)
    edges = (
        shape(state.shape, bf16),
        shape((cols_dev, chans), bf16),
        shape((cols_dev, chans), bf16),
        shape((rows_dev, chans), f32),
        shape((rows_dev, chans), f32),
    )

    def limit(mib):
        return pltpu.CompilerParams(vmem_limit_bytes=mib << 20)

    start = pl.pallas_call(
        start_kernel,
        out_shape=edges,
        in_specs=[ANY] * 2,
        out_specs=(VMEM,) * 5,
        scratch_shapes=[
            pltpu.VMEM(state.shape, bf16),
            pltpu.VMEM(state.shape, bf16),
            pltpu.VMEM(state.shape, f32),
            pltpu.SemaphoreType.DMA((2, 4)),
        ],
        compiler_params=limit(8),
        name="start",
    )
    sides = pl.pallas_call(
        sides_kernel,
        out_shape=[shape((rows_dev + 16, chans), f32)] * 2,
        in_specs=[VMEM] * 4,
        out_specs=[VMEM] * 2,
        compiler_params=limit(4),
        cost_estimate=pl.CostEstimate(
            flops=4 * rays.size * 512, bytes_accessed=rays.size * 2, transcendentals=0
        ),
        name="sides",
    )
    pulled_out = shape((tiles, PIX // 2, 2, PIX, chans), f32)
    cols3_out = shape(((rows_dev + 2) // 2, 2, cols_dev, 3 * chans), bf16)
    macs = tiles * tile_pix * chans * (9 * chans + HITS * bins)

    def cost(share):
        return pl.CostEstimate(
            flops=2 * macs * share // tiles, bytes_accessed=rays.size * 2, transcendentals=0
        )

    taps_out = shape((4 * 3 * chans, 2 * chans), bf16)

    inner = pl.pallas_call(
        functools.partial(inner_kernel, tile_cols=tile_cols),
        out_shape=(pulled_out, slot_out, cols3_out, taps_out),
        in_specs=[SMEM] + [VMEM] * 5,
        out_specs=(VMEM,) * 4,
        scratch_shapes=[pltpu.VMEM((rows_dev + 2, cols_dev + 16, chans), f32)],
        compiler_params=limit(16),
        cost_estimate=cost(len(tiles_at(tiles, tile_cols, True))),
        name="inner",
    )
    outer = pl.pallas_call(
        functools.partial(outer_kernel, tile_cols=tile_cols),
        out_shape=(pulled_out, slot_out, cols3_out),
        in_specs=[SMEM] + [VMEM] * 7,
        out_specs=(VMEM,) * 3,
        input_output_aliases={5: 0, 6: 1, 7: 2},
        compiler_params=limit(16),
        cost_estimate=cost(len(tiles_at(tiles, tile_cols, False))),
        name="outer",
    )
    combine = pl.pallas_call(
        combine_kernel,
        out_shape=(shape((dense,) + block, f32), shape((dense,) + block, bf16)),
        in_specs=[SMEM, VMEM],
        out_specs=(VMEM, VMEM),
        scratch_shapes=[pltpu.VMEM((dense + 1,) + block, f32)] * 2,
        compiler_params=limit(8),
        name="combine",
    )
    reply = pl.pallas_call(
        reply_kernel,
        out_shape=slot_out,
        in_specs=[SMEM] * 2 + [VMEM] * 4,
        out_specs=VMEM,
        scratch_shapes=[pltpu.VMEM((dense + 1,) + block, bf16)],
        compiler_params=limit(8),
        name="reply",
    )

    def finish(last):
        return pl.pallas_call(
            functools.partial(finish_kernel, tile_cols=tile_cols, last=last),
            out_shape=(shape(state.shape, f32),) if last else edges,
            in_specs=[SMEM] + [VMEM] * 5,
            out_specs=(pl.BlockSpec(memory_space=pl.ANY),) if last else (VMEM,) * 5,
            scratch_shapes=[
                pltpu.VMEM(state.shape, f32),
                pltpu.SemaphoreType.DMA((tiles,)),
            ],
            compiler_params=limit(20),
            name="finish",
        )

    def across(value):
        value = value.reshape((peers, cap) + block)
        value = lax.all_to_all(value, GROUP, split_axis=0, concat_axis=0, tiled=True)
        return value.reshape((slots,) + block)

    def swaps(value_a, value_b, axis):
        count = lax.axis_size(axis)
        even = [(i, i ^ 1) for i in range(count)]
        uneven = [(i, ((i + 1) ^ 1) - 1) for i in range(1, count - 1)]
        return lax.ppermute(value_a, axis, even), lax.ppermute(value_b, axis, uneven)

    def apart(value):
        return pltpu.with_memory_space_constraint(value, pltpu.HBM)

    def forward(early, scaled, row_a, row_b, col_a, col_b):
        above = swaps(row_a, row_b, "row")
        side_a, side_b = sides(*above, col_a, col_b)
        other_weight = None
        if early:
            side_b, weight = lax.optimization_barrier((side_b, ray_weight.astype(bf16)))
            other_weight = exchange(weight)
        beside = swaps(side_a, side_b, COL)
        *parts, taps = inner(routes, scaled, *above, kernel, rays)
        pulled, outgoing, _ = outer(routes, *beside, taps, rays, *parts)
        return pulled, outgoing, other_weight

    scaled, *rim = start(apart(state), apart(grad))
    for turn in range(ITERS):
        pulled, outgoing, swapped = forward(turn == 0, scaled, *rim)
        if not turn:
            other_weight = swapped
            outgoing, table, used, other_weight = lax.optimization_barrier(
                (outgoing, table, used, other_weight)
            )
        total, mine = combine(table, across(outgoing))
        replies = reply(table, used, total, exchange(mine), ray_weight, other_weight)
        last = turn == ITERS - 1
        scaled, *rim = finish(last)(
            routes, across(replies), pulled, grad, state, rays
        )
    return scaled


def solution(mesh):
    nr, nc = mesh.devices.shape
    fine = Mesh(mesh.devices.reshape(nr, 2, RING // 2, nc // RING), ("row",) + COL)
    image = P("row", COL, None)
    placed = (
        image,
        image,
        P(),
        P(),
        P(("row",) + COL, None, None),
        P(),
        image,
        P(),
        P(),
    )
    return jax.shard_map(
        on_device, mesh=fine, in_specs=placed, out_specs=image, check_vma=False
    )
```

```python
import functools

import jax
import jax.numpy as jnp
from jax import lax
from jax.experimental import pallas as pl
from jax.experimental.pallas import tpu as pltpu
from jax.sharding import Mesh, PartitionSpec as P

PIX = 32
ANGLES = 8
HITS = 16
ITERS = 2
RING = 4

relax_rate = 0.25

COL = ("zh", "zl", "x")
GROUP = ("row", "zl", "x")

VMEM = pl.BlockSpec(memory_space=pltpu.VMEM)
SMEM = pl.BlockSpec(memory_space=pltpu.SMEM)
ANY = pl.BlockSpec(memory_space=pl.ANY)


def start_kernel(state, grad, scaled, row_a, row_b, col_a, col_b, states, grads, whole, mark):
    parts = mark.shape[1]
    rows = states.shape[0] // parts

    def load(a, p):
        source, held = ((state, states), (grad, grads))[a]
        where = pl.ds(p * rows, rows)
        return pltpu.make_async_copy(source.at[where], held.at[where], mark.at[a, p])

    for p in range(parts):
        for a in range(2):
            load(a, p).start()
    for p in range(parts):
        for a in range(2):
            load(a, p).wait()
        where = slice(p * rows, (p + 1) * rows)
        value = states[where].astype(jnp.float32)
        whole[where] = (1.0 - value * value) * grads[where].astype(jnp.float32)
    emit_edges(whole[...], scaled, row_a, row_b, col_a, col_b)


def bring(source, held, mark):
    copy = pltpu.make_async_copy(source, held, mark)
    copy.start()
    return copy


def parity(dim):
    if dim == 0:
        return lax.axis_index("row") % 2
    return (lax.axis_index("zl") * lax.axis_size("x") + lax.axis_index("x")) % 2


def pick(dim, yes, no):
    return jnp.where(parity(dim) == 1, yes, no)


def emit_edges(value, scaled, row_a, row_b, col_a, col_b):
    rows, cols = value.shape[:2]
    scaled[...] = value.astype(jnp.bfloat16)
    row_a[...] = pick(0, value[0], value[rows - 1]).astype(jnp.bfloat16)
    row_b[...] = pick(0, value[rows - 1], value[0]).astype(jnp.bfloat16)
    left, right = value[:, 0, :], value[:, cols - 1, :]
    col_a[...] = pick(1, left, right)
    col_b[...] = pick(1, right, left)


def sides_kernel(near_a, near_b, col_a, col_b, out_a, out_b):
    rows = col_a.shape[0]
    cols = near_a.shape[0]
    f32 = jnp.float32

    def ends(ref):
        low = ref[0:16, :].astype(f32)[0:1, :]
        high = ref[cols - 16 : cols, :].astype(f32)[15:16, :]
        return low, high

    a, b = ends(near_a), ends(near_b)
    above = [pick(0, a[i], b[i]) for i in range(2)]
    below = [pick(0, b[i], a[i]) for i in range(2)]
    for out, edge, order in ((out_a, col_a, (0, 1)), (out_b, col_b, (1, 0))):
        yes, no = order
        out[8 : 8 + rows, :] = edge[...]
        out[7:8, :] = pick(1, above[yes], above[no])
        out[8 + rows : 9 + rows, :] = pick(1, below[yes], below[no])


def matrices_of(routes, rays, t):
    return jnp.concatenate([rays[routes[t * HITS + k]] for k in range(HITS)], axis=0)


def forward_tile(routes, taps, rays, pulled, out, cols3, t, tile_cols):
    chans = pulled.shape[-1]
    bins = rays.shape[1]
    slot = pulled.shape[0] * HITS
    half = PIX // 2
    r0, c0 = t // tile_cols * half, t % tile_cols * PIX
    window = jnp.concatenate(
        [
            cols3[r0 + dr // 2 : r0 + dr // 2 + half, dr % 2, c0 : c0 + PIX, :].reshape(
                half * PIX, 3 * chans
            )
            for dr in range(4)
        ],
        axis=1,
    )
    acc = jnp.dot(window, taps[...], preferred_element_type=jnp.float32)
    for odd in range(2):
        value = acc[:, odd * chans : (odd + 1) * chans].reshape(half, PIX, chans)
        pulled[t, :, odd] = value
    low = pulled[t].reshape(PIX * PIX, chans).astype(jnp.bfloat16)
    value = jnp.dot(
        matrices_of(routes, rays, t), low, preferred_element_type=jnp.float32
    ).astype(jnp.bfloat16)
    for k in range(HITS):
        out[routes[slot + t * HITS + k]] = value[k * bins : (k + 1) * bins, :]


def tiles_at(tiles, tile_cols, inner):
    return [t for t in range(tiles) if (0 < t % tile_cols < tile_cols - 1) == inner]


def inner_kernel(
    source, scaled, near_a, near_b, kernel, rays,
    pulled, out, cols3, taps, wide, routes, mark, *, tile_cols,
):
    coming = bring(source, routes, mark)
    rows, cols, chans = scaled.shape
    f32, bf16 = jnp.float32, jnp.bfloat16
    blank = jnp.zeros((3 * chans, chans), bf16)
    for dr in range(4):
        base = dr * 3 * chans
        for side in range(2):
            lanes = slice(side * chans, (side + 1) * chans)
            tap = dr - side
            if not 0 <= tap < 3:
                taps[base : base + 3 * chans, lanes] = blank
                continue
            for dc in range(3):
                taps[base + dc * chans : base + (dc + 1) * chans, lanes] = kernel[2 - tap, 2 - dc].T
    a, b = near_a[...].astype(f32), near_b[...].astype(f32)
    wide[0, 8 : 8 + cols, :] = pick(0, a, b)
    wide[rows + 1, 8 : 8 + cols, :] = pick(0, b, a)
    wide[1 : rows + 1, 8 : 8 + cols, :] = scaled[...].astype(f32)
    wide[:, 0:8, :] = jnp.zeros((rows + 2, 8, chans), f32)
    wide[:, 8 + cols :, :] = jnp.zeros((rows + 2, 8, chans), f32)
    for dc in range(3):
        value = wide[:, 7 + dc : 7 + dc + cols, :].astype(bf16)
        cols3[:, :, :, dc * chans : (dc + 1) * chans] = value.reshape(
            (rows + 2) // 2, 2, cols, chans
        )
    out[...] = jnp.zeros_like(out)
    coming.wait()
    for t in tiles_at(pulled.shape[0], tile_cols, True):
        forward_tile(routes, taps, rays, pulled, out, cols3, t, tile_cols)


def outer_kernel(
    source, near_a, near_b, taps, rays, _pulled, _out, _cols3,
    pulled, out, cols3, routes, mark, *, tile_cols,
):
    coming = bring(source, routes, mark)
    cols = cols3.shape[2]
    chans = pulled.shape[-1]
    group = 16
    spot = lax.broadcasted_iota(jnp.int32, (group, chans), 0)
    a, b = near_a[...], near_b[...]
    left, right = pick(1, a, b), pick(1, b, a)
    for edge, dc, first, at in ((left, 0, 0, 0), (right, 2, cols - group, group - 1)):
        lanes = slice(dc * chans, (dc + 1) * chans)
        for r in range(2 * cols3.shape[0]):
            there = (r // 2, r % 2, slice(first, first + group), lanes)
            value = jnp.where(spot == at, edge[7 + r : 8 + r, :], cols3[there].astype(jnp.float32))
            cols3[there] = value.astype(jnp.bfloat16)
    coming.wait()
    for t in tiles_at(pulled.shape[0], tile_cols, False):
        forward_tile(routes, taps, rays, pulled, out, cols3, t, tile_cols)


def combine_kernel(source, recv, total, low, acc_a, acc_b, table, mark):
    coming = bring(source, table, mark)
    acc_a[...] = jnp.zeros_like(acc_a)
    acc_b[...] = jnp.zeros_like(acc_b)
    coming.wait()

    def body(j, carry):
        acc_a[table[2 * j]] += recv[2 * j].astype(jnp.float32)
        acc_b[table[2 * j + 1]] += recv[2 * j + 1].astype(jnp.float32)
        return carry

    lax.fori_loop(0, recv.shape[0] // 2, body, 0, unroll=4)
    n = total.shape[0]
    value = acc_a[:n] + acc_b[:n]
    total[...] = value
    low[...] = value.astype(jnp.bfloat16)


def reply_kernel(
    source, flags, total, other, own_weight, other_weight, out, held, table, used, mark
):
    coming = [bring(source, table, mark.at[0]), bring(flags, used, mark.at[1])]
    n = total.shape[0]
    own = own_weight.shape[0]
    place = lax.axis_index("zh") * own
    for half, weight in enumerate((own_weight, other_weight)):
        first = place if half == 0 else n - own - place
        for b in range(own):
            d = first + b
            value = total[d] + other[d].astype(jnp.float32)
            held[d] = (weight[b].astype(jnp.float32) * value).astype(jnp.bfloat16)
    held[n] = jnp.zeros(held.shape[1:], jnp.bfloat16)
    for copy in coming:
        copy.wait()

    def body(j, carry):
        d = table[j]
        out[j] = held[jnp.where(used[d] == 1, d, n)]
        return carry

    lax.fori_loop(0, out.shape[0], body, 0, unroll=8)


def finish_kernel(
    routes, returned, pulled, grad, state, rays, *refs, tile_cols, last,
):
    outs, (whole, mark) = refs[:-2], refs[-2:]
    tiles = pulled.shape[0]
    slot = tiles * HITS
    chans = grad.shape[2]
    f32 = jnp.float32

    def place(t):
        r0, c0 = t // tile_cols * PIX, t % tile_cols * PIX
        return slice(r0, r0 + PIX), slice(c0, c0 + PIX)

    def leave(t):
        where = place(t)
        return pltpu.make_async_copy(whole.at[where], outs[0].at[where], mark.at[t])

    for t in range(tiles):
        picked = jnp.concatenate([returned[routes[slot + t * HITS + k]] for k in range(HITS)], axis=0)
        backed = lax.dot_general(
            picked,
            matrices_of(routes, rays, t),
            (((0,), (0,)), ((), ())),
            preferred_element_type=f32,
        ).T
        change = pulled[t].reshape(backed.shape) - relax_rate * backed
        where = place(t)
        adjoint = grad[where].astype(f32) + change.reshape(PIX, PIX, chans)
        if last:
            whole[where] = adjoint
            leave(t).start()
        else:
            value = state[where].astype(f32)
            whole[where] = (1.0 - value * value) * adjoint
    if last:
        for t in range(tiles):
            leave(t).wait()
    else:
        emit_edges(whole[...], *outs)


def on_device(state, grad, kernel, ray_matrix, ray_weight, hits, offsets, block_slot, angle_count):
    f32, bf16, i32 = jnp.float32, jnp.bfloat16, jnp.int32
    rows_dev, cols_dev, chans = state.shape
    angles, spots, bins, tile_pix = ray_matrix.shape
    nr = lax.axis_size("row")
    nx = lax.axis_size("x")
    nc = lax.axis_size(COL)
    devices = nr * nc
    row, zh, zl, x = (lax.axis_index(a) for a in ("row",) + COL)
    tile_rows = rows_dev // PIX
    tile_cols = cols_dev // PIX
    tiles = tile_rows * tile_cols
    pairs = tiles * HITS
    blk_dev = ray_weight.shape[0]
    blocks = blk_dev * devices
    blk_ang = blocks // ANGLES
    cap = 2 * max(2, (pairs + devices - 2) // devices + 1)
    cap = min(cap, pairs)
    peers = nr * 2 * nx
    slots = peers * cap
    dense = 2 * blk_dev

    def exchange(value):
        return lax.ppermute(value, "zh", [(0, 1), (1, 0)])

    everyone = hits.reshape(nr, tile_rows, nc, tile_cols, HITS).transpose(0, 2, 1, 3, 4)
    everyone = everyone.reshape(nr, 2, 2, nx, pairs)
    group = lax.dynamic_index_in_dim(everyone, zh, 1, keepdims=False).reshape(peers, pairs)
    storage = jnp.sum(
        jnp.where(group[:, :, None] == jnp.arange(blocks, dtype=i32), block_slot, 0), axis=2
    )
    owner = storage // blk_dev
    local = storage % blk_dev
    owner_z = (owner % nc) // nx
    owner_zh = owner_z // 2
    owner_zl = owner_z % 2
    peer = ((owner // nc) * 2 + owner_zl) * nx + owner % nx
    place = owner_zh * blk_dev + local
    earlier = jnp.arange(pairs)[None, :] < jnp.arange(pairs)[:, None]
    ranking = jnp.sum(
        ((peer[:, :, None] == peer[:, None, :]) & earlier[None]).astype(i32), axis=2
    )
    me = (row * 2 + zl) * nx + x
    my_hits = lax.dynamic_index_in_dim(group, me, 0, keepdims=False)
    send_slot = lax.dynamic_index_in_dim(peer * cap + ranking, me, 0, keepdims=False)
    matched = (peer[:, None, :] == me) & (
        ranking[:, None, :] == jnp.arange(cap, dtype=i32)[None, :, None]
    )
    table = dense + jnp.sum(jnp.where(matched, place[:, None, :] - dense, 0), axis=2)
    table = table.reshape(slots)
    mat_idx = (my_hits // blk_ang) * spots + offsets.reshape(pairs)
    routes = jnp.concatenate([mat_idx, send_slot])

    dense_z = jnp.arange(dense, dtype=i32) // blk_dev * 2 + zl
    dense_place = (row * nc + dense_z * nx + x) * blk_dev + jnp.arange(dense, dtype=i32) % blk_dev
    number = jnp.arange(blocks, dtype=i32)
    active = (
        (number % blk_ang).reshape(ANGLES, blk_ang) < angle_count[:, None]
    ).reshape(1, blocks)
    used = jnp.any((block_slot[None, :] == dense_place[:, None]) & active, axis=1).astype(i32)
    used = jnp.concatenate([used, jnp.zeros((1,), i32)])

    rays = ray_matrix.reshape(angles * spots, bins, tile_pix)

    block = (bins, chans)
    shape = jax.ShapeDtypeStruct
    slot_out = shape((slots,) + block, bf16)
    edges = (
        shape(state.shape, bf16),
        shape((cols_dev, chans), bf16),
        shape((cols_dev, chans), bf16),
        shape((rows_dev, chans), f32),
        shape((rows_dev, chans), f32),
    )

    def scalars(count):
        return [pltpu.SMEM((count,), i32), pltpu.SemaphoreType.DMA]

    def limit(mib):
        return pltpu.CompilerParams(vmem_limit_bytes=mib << 20)

    start = pl.pallas_call(
        start_kernel,
        out_shape=edges,
        in_specs=[ANY] * 2,
        out_specs=(VMEM,) * 5,
        scratch_shapes=[
            pltpu.VMEM(state.shape, bf16),
            pltpu.VMEM(state.shape, bf16),
            pltpu.VMEM(state.shape, f32),
            pltpu.SemaphoreType.DMA((2, 4)),
        ],
        compiler_params=limit(8),
        name="start",
    )
    sides = pl.pallas_call(
        sides_kernel,
        out_shape=[shape((rows_dev + 16, chans), f32)] * 2,
        in_specs=[VMEM] * 4,
        out_specs=[VMEM] * 2,
        compiler_params=limit(4),
        cost_estimate=pl.CostEstimate(
            flops=4 * rays.size * 512, bytes_accessed=rays.size * 2, transcendentals=0
        ),
        name="sides",
    )
    pulled_out = shape((tiles, PIX // 2, 2, PIX, chans), f32)
    cols3_out = shape(((rows_dev + 2) // 2, 2, cols_dev, 3 * chans), bf16)
    macs = tiles * tile_pix * chans * (9 * chans + HITS * bins)

    def cost(share):
        return pl.CostEstimate(
            flops=2 * macs * share // tiles, bytes_accessed=rays.size * 2, transcendentals=0
        )

    taps_out = shape((4 * 3 * chans, 2 * chans), bf16)

    inner = pl.pallas_call(
        functools.partial(inner_kernel, tile_cols=tile_cols),
        out_shape=(pulled_out, slot_out, cols3_out, taps_out),
        in_specs=[ANY] + [VMEM] * 5,
        out_specs=(VMEM,) * 4,
        scratch_shapes=[pltpu.VMEM((rows_dev + 2, cols_dev + 16, chans), f32)] + scalars(2 * pairs),
        compiler_params=limit(16),
        cost_estimate=cost(len(tiles_at(tiles, tile_cols, True))),
        name="inner",
    )
    outer = pl.pallas_call(
        functools.partial(outer_kernel, tile_cols=tile_cols),
        out_shape=(pulled_out, slot_out, cols3_out),
        in_specs=[ANY] + [VMEM] * 7,
        out_specs=(VMEM,) * 3,
        scratch_shapes=scalars(2 * pairs),
        input_output_aliases={5: 0, 6: 1, 7: 2},
        compiler_params=limit(16),
        cost_estimate=cost(len(tiles_at(tiles, tile_cols, False))),
        name="outer",
    )
    combine = pl.pallas_call(
        combine_kernel,
        out_shape=(shape((dense,) + block, f32), shape((dense,) + block, bf16)),
        in_specs=[ANY, VMEM],
        out_specs=(VMEM, VMEM),
        scratch_shapes=[pltpu.VMEM((dense + 1,) + block, f32)] * 2 + scalars(slots),
        compiler_params=limit(8),
        name="combine",
    )
    reply = pl.pallas_call(
        reply_kernel,
        out_shape=slot_out,
        in_specs=[ANY] * 2 + [VMEM] * 4,
        out_specs=VMEM,
        scratch_shapes=[
            pltpu.VMEM((dense + 1,) + block, bf16),
            pltpu.SMEM((slots,), i32),
            pltpu.SMEM((dense + 1,), i32),
            pltpu.SemaphoreType.DMA((2,)),
        ],
        compiler_params=limit(8),
        name="reply",
    )

    def finish(last):
        return pl.pallas_call(
            functools.partial(finish_kernel, tile_cols=tile_cols, last=last),
            out_shape=(shape(state.shape, f32),) if last else edges,
            in_specs=[SMEM] + [VMEM] * 5,
            out_specs=(pl.BlockSpec(memory_space=pl.ANY),) if last else (VMEM,) * 5,
            scratch_shapes=[
                pltpu.VMEM(state.shape, f32),
                pltpu.SemaphoreType.DMA((tiles,)),
            ],
            compiler_params=limit(20),
            name="finish",
        )

    def across(value):
        value = value.reshape((peers, cap) + block)
        value = lax.all_to_all(value, GROUP, split_axis=0, concat_axis=0, tiled=True)
        return value.reshape((slots,) + block)

    def swaps(value_a, value_b, axis):
        count = lax.axis_size(axis)
        even = [(i, i ^ 1) for i in range(count)]
        uneven = [(i, ((i + 1) ^ 1) - 1) for i in range(1, count - 1)]
        return lax.ppermute(value_a, axis, even), lax.ppermute(value_b, axis, uneven)

    def apart(value):
        return pltpu.with_memory_space_constraint(value, pltpu.HBM)

    def forward(early, scaled, row_a, row_b, col_a, col_b):
        above = swaps(row_a, row_b, "row")
        side_a, side_b = sides(*above, col_a, col_b)
        other_weight = None
        if early:
            side_b, weight = lax.optimization_barrier((side_b, ray_weight.astype(bf16)))
            other_weight = exchange(weight)
        beside = swaps(side_a, side_b, COL)
        *parts, taps = inner(routes, scaled, *above, kernel, rays)
        pulled, outgoing, _ = outer(routes, *beside, taps, rays, *parts)
        return pulled, outgoing, other_weight

    scaled, *rim = start(apart(state), apart(grad))
    for turn in range(ITERS):
        pulled, outgoing, swapped = forward(turn == 0, scaled, *rim)
        if not turn:
            other_weight = swapped
            outgoing, table, used, other_weight = lax.optimization_barrier(
                (outgoing, table, used, other_weight)
            )
        total, mine = combine(table, across(outgoing))
        replies = reply(table, used, total, exchange(mine), ray_weight, other_weight)
        last = turn == ITERS - 1
        scaled, *rim = finish(last)(
            routes, across(replies), pulled, grad, state, rays
        )
    return scaled


def solution(mesh):
    nr, nc = mesh.devices.shape
    fine = Mesh(mesh.devices.reshape(nr, 2, RING // 2, nc // RING), ("row",) + COL)
    image = P("row", COL, None)
    placed = (
        image,
        image,
        P(),
        P(),
        P(("row",) + COL, None, None),
        P(),
        image,
        P(),
        P(),
    )
    return jax.shard_map(
        on_device, mesh=fine, in_specs=placed, out_specs=image, check_vma=False
    )
```

```python
import functools

import jax
import jax.numpy as jnp
from jax import lax
from jax.experimental import pallas as pl
from jax.experimental.pallas import tpu as pltpu
from jax.sharding import Mesh, PartitionSpec as P

PIX = 32
ANGLES = 8
HITS = 16
ITERS = 2
RING = 4

relax_rate = 0.25

COL = ("zh", "zl", "x")
GROUP = ("row", "zl", "x")

VMEM = pl.BlockSpec(memory_space=pltpu.VMEM)
SMEM = pl.BlockSpec(memory_space=pltpu.SMEM)
ANY = pl.BlockSpec(memory_space=pl.ANY)


def start_kernel(state, grad, scaled, row_a, row_b, col_a, col_b, states, grads, whole, mark):
    parts = mark.shape[1]
    rows = states.shape[0] // parts

    def load(a, p):
        source, held = ((state, states), (grad, grads))[a]
        where = pl.ds(p * rows, rows)
        return pltpu.make_async_copy(source.at[where], held.at[where], mark.at[a, p])

    for p in range(parts):
        for a in range(2):
            load(a, p).start()
    for p in range(parts):
        for a in range(2):
            load(a, p).wait()
        where = slice(p * rows, (p + 1) * rows)
        value = states[where].astype(jnp.float32)
        whole[where] = (1.0 - value * value) * grads[where].astype(jnp.float32)
    emit_edges(whole[...], scaled, row_a, row_b, col_a, col_b)


def bring(source, held, mark):
    copy = pltpu.make_async_copy(source, held, mark)
    copy.start()
    return copy


def parity(dim):
    if dim == 0:
        return lax.axis_index("row") % 2
    return (lax.axis_index("zl") * lax.axis_size("x") + lax.axis_index("x")) % 2


def pick(dim, yes, no):
    return jnp.where(parity(dim) == 1, yes, no)


def emit_edges(value, scaled, row_a, row_b, col_a, col_b):
    rows, cols = value.shape[:2]
    scaled[...] = value.astype(jnp.bfloat16)
    row_a[...] = pick(0, value[0], value[rows - 1]).astype(jnp.bfloat16)
    row_b[...] = pick(0, value[rows - 1], value[0]).astype(jnp.bfloat16)
    left, right = value[:, 0, :], value[:, cols - 1, :]
    col_a[...] = pick(1, left, right)
    col_b[...] = pick(1, right, left)


def sides_kernel(near_a, near_b, col_a, col_b, out_a, out_b):
    rows = col_a.shape[0]
    cols = near_a.shape[0]
    f32 = jnp.float32

    def ends(ref):
        low = ref[0:16, :].astype(f32)[0:1, :]
        high = ref[cols - 16 : cols, :].astype(f32)[15:16, :]
        return low, high

    a, b = ends(near_a), ends(near_b)
    above = [pick(0, a[i], b[i]) for i in range(2)]
    below = [pick(0, b[i], a[i]) for i in range(2)]
    for out, edge, order in ((out_a, col_a, (0, 1)), (out_b, col_b, (1, 0))):
        yes, no = order
        out[8 : 8 + rows, :] = edge[...]
        out[7:8, :] = pick(1, above[yes], above[no])
        out[8 + rows : 9 + rows, :] = pick(1, below[yes], below[no])


def matrices_of(routes, rays, t):
    return jnp.concatenate([rays[routes[t * HITS + k]] for k in range(HITS)], axis=0)


def forward_tile(routes, taps, rays, pulled, out, cols3, t, tile_cols):
    chans = pulled.shape[-1]
    bins = rays.shape[1]
    slot = pulled.shape[0] * HITS
    half = PIX // 2
    r0, c0 = t // tile_cols * half, t % tile_cols * PIX
    window = jnp.concatenate(
        [
            cols3[r0 + dr // 2 : r0 + dr // 2 + half, dr % 2, c0 : c0 + PIX, :].reshape(
                half * PIX, 3 * chans
            )
            for dr in range(4)
        ],
        axis=1,
    )
    acc = jnp.dot(window, taps[...], preferred_element_type=jnp.float32)
    for odd in range(2):
        value = acc[:, odd * chans : (odd + 1) * chans].reshape(half, PIX, chans)
        pulled[t, :, odd] = value
    low = pulled[t].reshape(PIX * PIX, chans).astype(jnp.bfloat16)
    value = jnp.dot(
        matrices_of(routes, rays, t), low, preferred_element_type=jnp.float32
    ).astype(jnp.bfloat16)
    for k in range(HITS):
        out[routes[slot + t * HITS + k]] = value[k * bins : (k + 1) * bins, :]


def tiles_at(tiles, tile_cols, inner):
    return [t for t in range(tiles) if (0 < t % tile_cols < tile_cols - 1) == inner]


def spread(rows, wide, cols3, first):
    count, cols, chans = rows.shape
    f32, bf16 = jnp.float32, jnp.bfloat16
    blank = jnp.zeros((count, 8, chans), f32)
    wide[:, 0:8, :] = blank
    wide[:, 8 + cols : 16 + cols, :] = blank
    wide[:, 8 : 8 + cols, :] = rows.astype(f32)
    for dc in range(3):
        lanes = slice(dc * chans, (dc + 1) * chans)
        value = wide[:, 7 + dc : 7 + dc + cols, :].astype(bf16)
        for r in range(count):
            cols3[(first + r) // 2, (first + r) % 2, :, lanes] = value[r]


def centre_kernel(scaled, kernel, out, cols3, taps, wide):
    chans = scaled.shape[2]
    blank = jnp.zeros((3 * chans, chans), jnp.bfloat16)
    for dr in range(4):
        base = dr * 3 * chans
        for side in range(2):
            lanes = slice(side * chans, (side + 1) * chans)
            tap = dr - side
            if not 0 <= tap < 3:
                taps[base : base + 3 * chans, lanes] = blank
                continue
            for dc in range(3):
                taps[base + dc * chans : base + (dc + 1) * chans, lanes] = kernel[2 - tap, 2 - dc].T
    spread(scaled[...], wide, cols3, 1)
    out[...] = jnp.zeros_like(out)


def inner_kernel(
    source, near_a, near_b, taps, rays, _out, _cols3,
    pulled, out, cols3, wide, routes, mark, *, tile_cols,
):
    coming = bring(source, routes, mark)
    a, b = near_a[...], near_b[...]
    spread(pick(0, a, b)[None], wide, cols3, 0)
    spread(pick(0, b, a)[None], wide, cols3, 2 * cols3.shape[0] - 1)
    coming.wait()
    for t in tiles_at(pulled.shape[0], tile_cols, True):
        forward_tile(routes, taps, rays, pulled, out, cols3, t, tile_cols)


def both_kernel(
    source, scaled, near_a, near_b, kernel, rays,
    pulled, out, cols3, taps, wide, line, routes, mark, *, tile_cols,
):
    centre_kernel(scaled, kernel, out, cols3, taps, wide)
    inner_kernel(
        source, near_a, near_b, taps, rays, None, None,
        pulled, out, cols3, line, routes, mark, tile_cols=tile_cols,
    )


def outer_kernel(
    source, near_a, near_b, taps, rays, _pulled, _out, _cols3,
    pulled, out, cols3, routes, mark, *, tile_cols,
):
    coming = bring(source, routes, mark)
    cols = cols3.shape[2]
    chans = pulled.shape[-1]
    group = 16
    spot = lax.broadcasted_iota(jnp.int32, (group, chans), 0)
    a, b = near_a[...], near_b[...]
    left, right = pick(1, a, b), pick(1, b, a)
    for edge, dc, first, at in ((left, 0, 0, 0), (right, 2, cols - group, group - 1)):
        lanes = slice(dc * chans, (dc + 1) * chans)
        for r in range(2 * cols3.shape[0]):
            there = (r // 2, r % 2, slice(first, first + group), lanes)
            value = jnp.where(spot == at, edge[7 + r : 8 + r, :], cols3[there].astype(jnp.float32))
            cols3[there] = value.astype(jnp.bfloat16)
    coming.wait()
    for t in tiles_at(pulled.shape[0], tile_cols, False):
        forward_tile(routes, taps, rays, pulled, out, cols3, t, tile_cols)


def combine_kernel(source, recv, total, low, acc_a, acc_b, table, mark):
    coming = bring(source, table, mark)
    acc_a[...] = jnp.zeros_like(acc_a)
    acc_b[...] = jnp.zeros_like(acc_b)
    coming.wait()

    def body(j, carry):
        acc_a[table[2 * j]] += recv[2 * j].astype(jnp.float32)
        acc_b[table[2 * j + 1]] += recv[2 * j + 1].astype(jnp.float32)
        return carry

    lax.fori_loop(0, recv.shape[0] // 2, body, 0, unroll=4)
    n = total.shape[0]
    value = acc_a[:n] + acc_b[:n]
    total[...] = value
    low[...] = value.astype(jnp.bfloat16)


def reply_kernel(
    source, flags, total, other, own_weight, other_weight, out, held, table, used, mark
):
    coming = [bring(source, table, mark.at[0]), bring(flags, used, mark.at[1])]
    n = total.shape[0]
    own = own_weight.shape[0]
    place = lax.axis_index("zh") * own
    for half, weight in enumerate((own_weight, other_weight)):
        first = place if half == 0 else n - own - place
        for b in range(own):
            d = first + b
            value = total[d] + other[d].astype(jnp.float32)
            held[d] = (weight[b].astype(jnp.float32) * value).astype(jnp.bfloat16)
    held[n] = jnp.zeros(held.shape[1:], jnp.bfloat16)
    for copy in coming:
        copy.wait()

    def body(j, carry):
        d = table[j]
        out[j] = held[jnp.where(used[d] == 1, d, n)]
        return carry

    lax.fori_loop(0, out.shape[0], body, 0, unroll=8)


def finish_kernel(
    routes, returned, pulled, grad, state, rays, *refs, tile_cols, last,
):
    outs, (whole, mark) = refs[:-2], refs[-2:]
    tiles = pulled.shape[0]
    slot = tiles * HITS
    chans = grad.shape[2]
    f32 = jnp.float32

    def place(t):
        r0, c0 = t // tile_cols * PIX, t % tile_cols * PIX
        return slice(r0, r0 + PIX), slice(c0, c0 + PIX)

    def leave(t):
        where = place(t)
        return pltpu.make_async_copy(whole.at[where], outs[0].at[where], mark.at[t])

    for t in range(tiles):
        picked = jnp.concatenate([returned[routes[slot + t * HITS + k]] for k in range(HITS)], axis=0)
        backed = lax.dot_general(
            picked,
            matrices_of(routes, rays, t),
            (((0,), (0,)), ((), ())),
            preferred_element_type=f32,
        ).T
        change = pulled[t].reshape(backed.shape) - relax_rate * backed
        where = place(t)
        adjoint = grad[where].astype(f32) + change.reshape(PIX, PIX, chans)
        if last:
            whole[where] = adjoint
            leave(t).start()
        else:
            value = state[where].astype(f32)
            whole[where] = (1.0 - value * value) * adjoint
    if last:
        for t in range(tiles):
            leave(t).wait()
    else:
        emit_edges(whole[...], *outs)


def on_device(state, grad, kernel, ray_matrix, ray_weight, hits, offsets, block_slot, angle_count):
    f32, bf16, i32 = jnp.float32, jnp.bfloat16, jnp.int32
    rows_dev, cols_dev, chans = state.shape
    angles, spots, bins, tile_pix = ray_matrix.shape
    nr = lax.axis_size("row")
    nx = lax.axis_size("x")
    nc = lax.axis_size(COL)
    devices = nr * nc
    row, zh, zl, x = (lax.axis_index(a) for a in ("row",) + COL)
    tile_rows = rows_dev // PIX
    tile_cols = cols_dev // PIX
    tiles = tile_rows * tile_cols
    pairs = tiles * HITS
    blk_dev = ray_weight.shape[0]
    blocks = blk_dev * devices
    blk_ang = blocks // ANGLES
    cap = 2 * max(2, (pairs + devices - 2) // devices + 1)
    cap = min(cap, pairs)
    peers = nr * 2 * nx
    slots = peers * cap
    dense = 2 * blk_dev

    def exchange(value):
        return lax.ppermute(value, "zh", [(0, 1), (1, 0)])

    everyone = hits.reshape(nr, tile_rows, nc, tile_cols, HITS).transpose(0, 2, 1, 3, 4)
    everyone = everyone.reshape(nr, 2, 2, nx, pairs)
    group = lax.dynamic_index_in_dim(everyone, zh, 1, keepdims=False).reshape(peers, pairs)
    storage = jnp.sum(
        jnp.where(group[:, :, None] == jnp.arange(blocks, dtype=i32), block_slot, 0), axis=2
    )
    owner = storage // blk_dev
    local = storage % blk_dev
    owner_z = (owner % nc) // nx
    owner_zh = owner_z // 2
    owner_zl = owner_z % 2
    peer = ((owner // nc) * 2 + owner_zl) * nx + owner % nx
    place = owner_zh * blk_dev + local
    earlier = jnp.arange(pairs)[None, :] < jnp.arange(pairs)[:, None]
    ranking = jnp.sum(
        ((peer[:, :, None] == peer[:, None, :]) & earlier[None]).astype(i32), axis=2
    )
    me = (row * 2 + zl) * nx + x
    my_hits = lax.dynamic_index_in_dim(group, me, 0, keepdims=False)
    send_slot = lax.dynamic_index_in_dim(peer * cap + ranking, me, 0, keepdims=False)
    matched = (peer[:, None, :] == me) & (
        ranking[:, None, :] == jnp.arange(cap, dtype=i32)[None, :, None]
    )
    table = dense + jnp.sum(jnp.where(matched, place[:, None, :] - dense, 0), axis=2)
    table = table.reshape(slots)
    mat_idx = (my_hits // blk_ang) * spots + offsets.reshape(pairs)
    routes = jnp.concatenate([mat_idx, send_slot])

    dense_z = jnp.arange(dense, dtype=i32) // blk_dev * 2 + zl
    dense_place = (row * nc + dense_z * nx + x) * blk_dev + jnp.arange(dense, dtype=i32) % blk_dev
    number = jnp.arange(blocks, dtype=i32)
    active = (
        (number % blk_ang).reshape(ANGLES, blk_ang) < angle_count[:, None]
    ).reshape(1, blocks)
    used = jnp.any((block_slot[None, :] == dense_place[:, None]) & active, axis=1).astype(i32)
    used = jnp.concatenate([used, jnp.zeros((1,), i32)])

    rays = ray_matrix.reshape(angles * spots, bins, tile_pix)

    block = (bins, chans)
    shape = jax.ShapeDtypeStruct
    slot_out = shape((slots,) + block, bf16)
    edges = (
        shape(state.shape, bf16),
        shape((cols_dev, chans), bf16),
        shape((cols_dev, chans), bf16),
        shape((rows_dev, chans), f32),
        shape((rows_dev, chans), f32),
    )

    def scalars(count):
        return [pltpu.SMEM((count,), i32), pltpu.SemaphoreType.DMA]

    def limit(mib):
        return pltpu.CompilerParams(vmem_limit_bytes=mib << 20)

    start = pl.pallas_call(
        start_kernel,
        out_shape=edges,
        in_specs=[ANY] * 2,
        out_specs=(VMEM,) * 5,
        scratch_shapes=[
            pltpu.VMEM(state.shape, bf16),
            pltpu.VMEM(state.shape, bf16),
            pltpu.VMEM(state.shape, f32),
            pltpu.SemaphoreType.DMA((2, 4)),
        ],
        compiler_params=limit(8),
        name="start",
    )
    sides = pl.pallas_call(
        sides_kernel,
        out_shape=[shape((rows_dev + 16, chans), f32)] * 2,
        in_specs=[VMEM] * 4,
        out_specs=[VMEM] * 2,
        compiler_params=limit(4),
        cost_estimate=pl.CostEstimate(
            flops=4 * rays.size * 512, bytes_accessed=rays.size * 2, transcendentals=0
        ),
        name="sides",
    )
    pulled_out = shape((tiles, PIX // 2, 2, PIX, chans), f32)
    cols3_out = shape(((rows_dev + 2) // 2, 2, cols_dev, 3 * chans), bf16)
    macs = tiles * tile_pix * chans * (9 * chans + HITS * bins)

    def cost(share):
        return pl.CostEstimate(
            flops=2 * macs * share // tiles, bytes_accessed=rays.size * 2, transcendentals=0
        )

    taps_out = shape((4 * 3 * chans, 2 * chans), bf16)

    wide = pltpu.VMEM((rows_dev, cols_dev + 16, chans), f32)
    line = pltpu.VMEM((1, cols_dev + 16, chans), f32)
    both = pl.pallas_call(
        functools.partial(both_kernel, tile_cols=tile_cols),
        out_shape=(pulled_out, slot_out, cols3_out, taps_out),
        in_specs=[ANY] + [VMEM] * 5,
        out_specs=(VMEM,) * 4,
        scratch_shapes=[wide, line] + scalars(2 * pairs),
        compiler_params=limit(16),
        cost_estimate=cost(len(tiles_at(tiles, tile_cols, True))),
        name="both",
    )
    centre = pl.pallas_call(
        centre_kernel,
        out_shape=(slot_out, cols3_out, taps_out),
        in_specs=[VMEM] * 2,
        out_specs=(VMEM,) * 3,
        scratch_shapes=[wide],
        compiler_params=limit(12),
        cost_estimate=cost(1),
        name="centre",
    )
    inner = pl.pallas_call(
        functools.partial(inner_kernel, tile_cols=tile_cols),
        out_shape=(pulled_out, slot_out, cols3_out),
        in_specs=[ANY] + [VMEM] * 6,
        out_specs=(VMEM,) * 3,
        scratch_shapes=[line] + scalars(2 * pairs),
        input_output_aliases={5: 1, 6: 2},
        compiler_params=limit(12),
        cost_estimate=cost(len(tiles_at(tiles, tile_cols, True))),
        name="inner",
    )
    outer = pl.pallas_call(
        functools.partial(outer_kernel, tile_cols=tile_cols),
        out_shape=(pulled_out, slot_out, cols3_out),
        in_specs=[ANY] + [VMEM] * 7,
        out_specs=(VMEM,) * 3,
        scratch_shapes=scalars(2 * pairs),
        input_output_aliases={5: 0, 6: 1, 7: 2},
        compiler_params=limit(16),
        cost_estimate=cost(len(tiles_at(tiles, tile_cols, False))),
        name="outer",
    )
    combine = pl.pallas_call(
        combine_kernel,
        out_shape=(shape((dense,) + block, f32), shape((dense,) + block, bf16)),
        in_specs=[ANY, VMEM],
        out_specs=(VMEM, VMEM),
        scratch_shapes=[pltpu.VMEM((dense + 1,) + block, f32)] * 2 + scalars(slots),
        compiler_params=limit(8),
        name="combine",
    )
    reply = pl.pallas_call(
        reply_kernel,
        out_shape=slot_out,
        in_specs=[ANY] * 2 + [VMEM] * 4,
        out_specs=VMEM,
        scratch_shapes=[
            pltpu.VMEM((dense + 1,) + block, bf16),
            pltpu.SMEM((slots,), i32),
            pltpu.SMEM((dense + 1,), i32),
            pltpu.SemaphoreType.DMA((2,)),
        ],
        compiler_params=limit(8),
        name="reply",
    )

    def finish(last):
        return pl.pallas_call(
            functools.partial(finish_kernel, tile_cols=tile_cols, last=last),
            out_shape=(shape(state.shape, f32),) if last else edges,
            in_specs=[SMEM] + [VMEM] * 5,
            out_specs=(pl.BlockSpec(memory_space=pl.ANY),) if last else (VMEM,) * 5,
            scratch_shapes=[
                pltpu.VMEM(state.shape, f32),
                pltpu.SemaphoreType.DMA((tiles,)),
            ],
            compiler_params=limit(20),
            name="finish",
        )

    def across(value):
        value = value.reshape((peers, cap) + block)
        value = lax.all_to_all(value, GROUP, split_axis=0, concat_axis=0, tiled=True)
        return value.reshape((slots,) + block)

    def swaps(value_a, value_b, axis):
        count = lax.axis_size(axis)
        even = [(i, i ^ 1) for i in range(count)]
        uneven = [(i, ((i + 1) ^ 1) - 1) for i in range(1, count - 1)]
        return lax.ppermute(value_a, axis, even), lax.ppermute(value_b, axis, uneven)

    def apart(value):
        return pltpu.with_memory_space_constraint(value, pltpu.HBM)

    def forward(early, scaled, row_a, row_b, col_a, col_b):
        above = swaps(row_a, row_b, "row")
        side_a, side_b = sides(*above, col_a, col_b)
        other_weight = None
        if early:
            side_b, weight = lax.optimization_barrier((side_b, ray_weight.astype(bf16)))
            other_weight = exchange(weight)
        beside = swaps(side_a, side_b, COL)
        if early:
            *parts, taps = both(routes, scaled, *above, kernel, rays)
        else:
            outgoing, cols3, taps = centre(scaled, kernel)
            parts = inner(routes, *above, taps, rays, outgoing, cols3)
        pulled, outgoing, _ = outer(routes, *beside, taps, rays, *parts)
        return pulled, outgoing, other_weight

    scaled, *rim = start(apart(state), apart(grad))
    for turn in range(ITERS):
        pulled, outgoing, swapped = forward(turn == 0, scaled, *rim)
        if not turn:
            other_weight = swapped
            outgoing, table, used, other_weight = lax.optimization_barrier(
                (outgoing, table, used, other_weight)
            )
        total, mine = combine(table, across(outgoing))
        replies = reply(table, used, total, exchange(mine), ray_weight, other_weight)
        last = turn == ITERS - 1
        scaled, *rim = finish(last)(
            routes, across(replies), pulled, grad, state, rays
        )
    return scaled


def solution(mesh):
    nr, nc = mesh.devices.shape
    fine = Mesh(mesh.devices.reshape(nr, 2, RING // 2, nc // RING), ("row",) + COL)
    image = P("row", COL, None)
    placed = (
        image,
        image,
        P(),
        P(),
        P(("row",) + COL, None, None),
        P(),
        image,
        P(),
        P(),
    )
    return jax.shard_map(
        on_device, mesh=fine, in_specs=placed, out_specs=image, check_vma=False
    )
```

```python
import functools

import jax
import jax.numpy as jnp
from jax import lax
from jax.experimental import pallas as pl
from jax.experimental.pallas import tpu as pltpu
from jax.sharding import Mesh, PartitionSpec as P

PIX = 32
ANGLES = 8
HITS = 16
ITERS = 2
RING = 4

relax_rate = 0.25

COL = ("zh", "zl", "x")
GROUP = ("row", "zl", "x")

VMEM = pl.BlockSpec(memory_space=pltpu.VMEM)
SMEM = pl.BlockSpec(memory_space=pltpu.SMEM)
ANY = pl.BlockSpec(memory_space=pl.ANY)


def start_kernel(state, grad, scaled, row_a, row_b, col_a, col_b, states, grads, whole, mark):
    parts = mark.shape[1]
    rows = states.shape[0] // parts

    def load(a, p):
        source, held = ((state, states), (grad, grads))[a]
        where = pl.ds(p * rows, rows)
        return pltpu.make_async_copy(source.at[where], held.at[where], mark.at[a, p])

    for p in range(parts):
        for a in range(2):
            load(a, p).start()
    for p in range(parts):
        for a in range(2):
            load(a, p).wait()
        where = slice(p * rows, (p + 1) * rows)
        value = states[where].astype(jnp.float32)
        whole[where] = (1.0 - value * value) * grads[where].astype(jnp.float32)
    emit_edges(whole[...], scaled, row_a, row_b, col_a, col_b)


def bring(source, held, mark):
    copy = pltpu.make_async_copy(source, held, mark)
    copy.start()
    return copy


def parity(dim):
    if dim == 0:
        return lax.axis_index("row") % 2
    return (lax.axis_index("zl") * lax.axis_size("x") + lax.axis_index("x")) % 2


def pick(dim, yes, no):
    return jnp.where(parity(dim) == 1, yes, no)


def emit_edges(value, scaled, row_a, row_b, col_a, col_b):
    rows, cols = value.shape[:2]
    scaled[...] = value.astype(jnp.bfloat16)
    row_a[...] = pick(0, value[0], value[rows - 1]).astype(jnp.bfloat16)
    row_b[...] = pick(0, value[rows - 1], value[0]).astype(jnp.bfloat16)
    left, right = value[:, 0, :], value[:, cols - 1, :]
    col_a[...] = pick(1, left, right)
    col_b[...] = pick(1, right, left)


def sides_kernel(near_a, near_b, col_a, col_b, out_a, out_b):
    rows = col_a.shape[0]
    cols = near_a.shape[0]
    f32 = jnp.float32

    def ends(ref):
        low = ref[0:16, :].astype(f32)[0:1, :]
        high = ref[cols - 16 : cols, :].astype(f32)[15:16, :]
        return low, high

    a, b = ends(near_a), ends(near_b)
    above = [pick(0, a[i], b[i]) for i in range(2)]
    below = [pick(0, b[i], a[i]) for i in range(2)]
    for out, edge, order in ((out_a, col_a, (0, 1)), (out_b, col_b, (1, 0))):
        yes, no = order
        out[8 : 8 + rows, :] = edge[...]
        out[7:8, :] = pick(1, above[yes], above[no])
        out[8 + rows : 9 + rows, :] = pick(1, below[yes], below[no])


def matrices_of(routes, rays, t):
    return jnp.concatenate([rays[routes[t * HITS + k]] for k in range(HITS)], axis=0)


def forward_tile(routes, taps, rays, pulled, out, cols3, t, tile_cols):
    chans = pulled.shape[-1]
    bins = rays.shape[1]
    slot = pulled.shape[0] * HITS
    half = PIX // 2
    r0, c0 = t // tile_cols * half, t % tile_cols * PIX
    window = jnp.concatenate(
        [
            cols3[r0 + dr // 2 : r0 + dr // 2 + half, dr % 2, c0 : c0 + PIX, :].reshape(
                half * PIX, 3 * chans
            )
            for dr in range(4)
        ],
        axis=1,
    )
    acc = jnp.dot(window, taps[...], preferred_element_type=jnp.float32)
    for odd in range(2):
        value = acc[:, odd * chans : (odd + 1) * chans].reshape(half, PIX, chans)
        pulled[t, :, odd] = value
    low = pulled[t].reshape(PIX * PIX, chans).astype(jnp.bfloat16)
    value = jnp.dot(
        matrices_of(routes, rays, t), low, preferred_element_type=jnp.float32
    ).astype(jnp.bfloat16)
    for k in range(HITS):
        out[routes[slot + t * HITS + k]] = value[k * bins : (k + 1) * bins, :]


def tiles_at(tiles, tile_cols, inner):
    return [t for t in range(tiles) if (0 < t % tile_cols < tile_cols - 1) == inner]


def inner_kernel(
    source, scaled, near_a, near_b, kernel, rays,
    pulled, out, cols3, taps, wide, routes, mark, *, tile_cols,
):
    coming = bring(source, routes, mark)
    rows, cols, chans = scaled.shape
    f32, bf16 = jnp.float32, jnp.bfloat16
    blank = jnp.zeros((3 * chans, chans), bf16)
    for dr in range(4):
        base = dr * 3 * chans
        for side in range(2):
            lanes = slice(side * chans, (side + 1) * chans)
            tap = dr - side
            if not 0 <= tap < 3:
                taps[base : base + 3 * chans, lanes] = blank
                continue
            for dc in range(3):
                taps[base + dc * chans : base + (dc + 1) * chans, lanes] = kernel[2 - tap, 2 - dc].T
    a, b = near_a[...].astype(f32), near_b[...].astype(f32)
    wide[0, 8 : 8 + cols, :] = pick(0, a, b)
    wide[rows + 1, 8 : 8 + cols, :] = pick(0, b, a)
    wide[1 : rows + 1, 8 : 8 + cols, :] = scaled[...].astype(f32)
    wide[:, 0:8, :] = jnp.zeros((rows + 2, 8, chans), f32)
    wide[:, 8 + cols :, :] = jnp.zeros((rows + 2, 8, chans), f32)
    for dc in (0, 2):
        value = wide[:, 7 + dc : 7 + dc + cols, :].astype(bf16)
        cols3[:, :, :, dc * chans : (dc + 1) * chans] = value.reshape(
            (rows + 2) // 2, 2, cols, chans
        )
    middle = slice(chans, 2 * chans)
    cols3[0, 0, :, middle] = pick(0, a, b).astype(bf16)
    cols3[(rows + 1) // 2, (rows + 1) % 2, :, middle] = pick(0, b, a).astype(bf16)
    for r in range(1, rows + 1):
        cols3[r // 2, r % 2, :, middle] = scaled[r - 1]
    coming.wait()
    for t in tiles_at(pulled.shape[0], tile_cols, True):
        forward_tile(routes, taps, rays, pulled, out, cols3, t, tile_cols)


def outer_kernel(
    source, near_a, near_b, taps, rays, _pulled, _out, _cols3,
    pulled, out, cols3, routes, mark, *, tile_cols,
):
    coming = bring(source, routes, mark)
    cols = cols3.shape[2]
    chans = pulled.shape[-1]
    group = 16
    spot = lax.broadcasted_iota(jnp.int32, (group, chans), 0)
    a, b = near_a[...], near_b[...]
    left, right = pick(1, a, b), pick(1, b, a)
    for edge, dc, first, at in ((left, 0, 0, 0), (right, 2, cols - group, group - 1)):
        lanes = slice(dc * chans, (dc + 1) * chans)
        for r in range(2 * cols3.shape[0]):
            there = (r // 2, r % 2, slice(first, first + group), lanes)
            value = jnp.where(spot == at, edge[7 + r : 8 + r, :], cols3[there].astype(jnp.float32))
            cols3[there] = value.astype(jnp.bfloat16)
    coming.wait()
    for t in tiles_at(pulled.shape[0], tile_cols, False):
        forward_tile(routes, taps, rays, pulled, out, cols3, t, tile_cols)


def combine_kernel(source, recv, total, low, acc_a, acc_b, table, mark):
    coming = bring(source, table, mark)
    acc_a[...] = jnp.zeros_like(acc_a)
    acc_b[...] = jnp.zeros_like(acc_b)
    coming.wait()

    def body(j, carry):
        acc_a[table[2 * j]] += recv[2 * j].astype(jnp.float32)
        acc_b[table[2 * j + 1]] += recv[2 * j + 1].astype(jnp.float32)
        return carry

    lax.fori_loop(0, recv.shape[0] // 2, body, 0, unroll=4)
    n = total.shape[0]
    value = acc_a[:n] + acc_b[:n]
    total[...] = value
    low[...] = value.astype(jnp.bfloat16)


def reply_kernel(
    source, flags, total, other, own_weight, other_weight, out, held, table, used, mark
):
    coming = [bring(source, table, mark.at[0]), bring(flags, used, mark.at[1])]
    n = total.shape[0]
    own = own_weight.shape[0]
    place = lax.axis_index("zh") * own
    for half, weight in enumerate((own_weight, other_weight)):
        first = place if half == 0 else n - own - place
        for b in range(own):
            d = first + b
            value = total[d] + other[d].astype(jnp.float32)
            held[d] = (weight[b].astype(jnp.float32) * value).astype(jnp.bfloat16)
    held[n] = jnp.zeros(held.shape[1:], jnp.bfloat16)
    for copy in coming:
        copy.wait()

    def body(j, carry):
        d = table[j]
        out[j] = held[jnp.where(used[d] == 1, d, n)]
        return carry

    lax.fori_loop(0, out.shape[0], body, 0, unroll=8)


def finish_kernel(
    routes, returned, pulled, grad, state, rays, *refs, tile_cols, last,
):
    outs, (whole, mark) = refs[:-2], refs[-2:]
    tiles = pulled.shape[0]
    slot = tiles * HITS
    chans = grad.shape[2]
    f32 = jnp.float32

    def place(t):
        r0, c0 = t // tile_cols * PIX, t % tile_cols * PIX
        return slice(r0, r0 + PIX), slice(c0, c0 + PIX)

    def leave(t):
        where = place(t)
        return pltpu.make_async_copy(whole.at[where], outs[0].at[where], mark.at[t])

    for t in range(tiles):
        picked = jnp.concatenate([returned[routes[slot + t * HITS + k]] for k in range(HITS)], axis=0)
        backed = lax.dot_general(
            picked,
            matrices_of(routes, rays, t),
            (((0,), (0,)), ((), ())),
            preferred_element_type=f32,
        ).T
        change = pulled[t].reshape(backed.shape) - relax_rate * backed
        where = place(t)
        adjoint = grad[where].astype(f32) + change.reshape(PIX, PIX, chans)
        if last:
            whole[where] = adjoint
            leave(t).start()
        else:
            value = state[where].astype(f32)
            whole[where] = (1.0 - value * value) * adjoint
    if last:
        for t in range(tiles):
            leave(t).wait()
    else:
        emit_edges(whole[...], *outs)


def on_device(state, grad, kernel, ray_matrix, ray_weight, hits, offsets, block_slot, angle_count):
    f32, bf16, i32 = jnp.float32, jnp.bfloat16, jnp.int32
    rows_dev, cols_dev, chans = state.shape
    angles, spots, bins, tile_pix = ray_matrix.shape
    nr = lax.axis_size("row")
    nx = lax.axis_size("x")
    nc = lax.axis_size(COL)
    devices = nr * nc
    row, zh, zl, x = (lax.axis_index(a) for a in ("row",) + COL)
    tile_rows = rows_dev // PIX
    tile_cols = cols_dev // PIX
    tiles = tile_rows * tile_cols
    pairs = tiles * HITS
    blk_dev = ray_weight.shape[0]
    blocks = blk_dev * devices
    blk_ang = blocks // ANGLES
    cap = 2 * max(2, (pairs + devices - 2) // devices + 1)
    cap = min(cap, pairs)
    peers = nr * 2 * nx
    slots = peers * cap
    dense = 2 * blk_dev

    def exchange(value):
        return lax.ppermute(value, "zh", [(0, 1), (1, 0)])

    everyone = hits.reshape(nr, tile_rows, nc, tile_cols, HITS).transpose(0, 2, 1, 3, 4)
    everyone = everyone.reshape(nr, 2, 2, nx, pairs)
    group = lax.dynamic_index_in_dim(everyone, zh, 1, keepdims=False).reshape(peers, pairs)
    storage = jnp.sum(
        jnp.where(group[:, :, None] == jnp.arange(blocks, dtype=i32), block_slot, 0), axis=2
    )
    owner = storage // blk_dev
    local = storage % blk_dev
    owner_z = (owner % nc) // nx
    owner_zh = owner_z // 2
    owner_zl = owner_z % 2
    peer = ((owner // nc) * 2 + owner_zl) * nx + owner % nx
    place = owner_zh * blk_dev + local
    earlier = jnp.arange(pairs)[None, :] < jnp.arange(pairs)[:, None]
    ranking = jnp.sum(
        ((peer[:, :, None] == peer[:, None, :]) & earlier[None]).astype(i32), axis=2
    )
    me = (row * 2 + zl) * nx + x
    my_hits = lax.dynamic_index_in_dim(group, me, 0, keepdims=False)
    send_slot = lax.dynamic_index_in_dim(peer * cap + ranking, me, 0, keepdims=False)
    matched = (peer[:, None, :] == me) & (
        ranking[:, None, :] == jnp.arange(cap, dtype=i32)[None, :, None]
    )
    table = dense + jnp.sum(jnp.where(matched, place[:, None, :] - dense, 0), axis=2)
    table = table.reshape(slots)
    mat_idx = (my_hits // blk_ang) * spots + offsets.reshape(pairs)
    routes = jnp.concatenate([mat_idx, send_slot])

    dense_z = jnp.arange(dense, dtype=i32) // blk_dev * 2 + zl
    dense_place = (row * nc + dense_z * nx + x) * blk_dev + jnp.arange(dense, dtype=i32) % blk_dev
    number = jnp.arange(blocks, dtype=i32)
    active = (
        (number % blk_ang).reshape(ANGLES, blk_ang) < angle_count[:, None]
    ).reshape(1, blocks)
    used = jnp.any((block_slot[None, :] == dense_place[:, None]) & active, axis=1).astype(i32)
    used = jnp.concatenate([used, jnp.zeros((1,), i32)])

    rays = ray_matrix.reshape(angles * spots, bins, tile_pix)

    block = (bins, chans)
    shape = jax.ShapeDtypeStruct
    slot_out = shape((slots,) + block, bf16)
    edges = (
        shape(state.shape, bf16),
        shape((cols_dev, chans), bf16),
        shape((cols_dev, chans), bf16),
        shape((rows_dev, chans), f32),
        shape((rows_dev, chans), f32),
    )

    def scalars(count):
        return [pltpu.SMEM((count,), i32), pltpu.SemaphoreType.DMA]

    def limit(mib):
        return pltpu.CompilerParams(vmem_limit_bytes=mib << 20)

    start = pl.pallas_call(
        start_kernel,
        out_shape=edges,
        in_specs=[ANY] * 2,
        out_specs=(VMEM,) * 5,
        scratch_shapes=[
            pltpu.VMEM(state.shape, bf16),
            pltpu.VMEM(state.shape, bf16),
            pltpu.VMEM(state.shape, f32),
            pltpu.SemaphoreType.DMA((2, 4)),
        ],
        compiler_params=limit(8),
        name="start",
    )
    sides = pl.pallas_call(
        sides_kernel,
        out_shape=[shape((rows_dev + 16, chans), f32)] * 2,
        in_specs=[VMEM] * 4,
        out_specs=[VMEM] * 2,
        compiler_params=limit(4),
        cost_estimate=pl.CostEstimate(
            flops=4 * rays.size * 512, bytes_accessed=rays.size * 2, transcendentals=0
        ),
        name="sides",
    )
    pulled_out = shape((tiles, PIX // 2, 2, PIX, chans), f32)
    cols3_out = shape(((rows_dev + 2) // 2, 2, cols_dev, 3 * chans), bf16)
    macs = tiles * tile_pix * chans * (9 * chans + HITS * bins)

    def cost(share):
        return pl.CostEstimate(
            flops=2 * macs * share // tiles, bytes_accessed=rays.size * 2, transcendentals=0
        )

    taps_out = shape((4 * 3 * chans, 2 * chans), bf16)

    inner = pl.pallas_call(
        functools.partial(inner_kernel, tile_cols=tile_cols),
        out_shape=(pulled_out, slot_out, cols3_out, taps_out),
        in_specs=[ANY] + [VMEM] * 5,
        out_specs=(VMEM,) * 4,
        scratch_shapes=[pltpu.VMEM((rows_dev + 2, cols_dev + 16, chans), f32)] + scalars(2 * pairs),
        compiler_params=limit(16),
        cost_estimate=cost(len(tiles_at(tiles, tile_cols, True))),
        name="inner",
    )
    outer = pl.pallas_call(
        functools.partial(outer_kernel, tile_cols=tile_cols),
        out_shape=(pulled_out, slot_out, cols3_out),
        in_specs=[ANY] + [VMEM] * 7,
        out_specs=(VMEM,) * 3,
        scratch_shapes=scalars(2 * pairs),
        input_output_aliases={5: 0, 6: 1, 7: 2},
        compiler_params=limit(16),
        cost_estimate=cost(len(tiles_at(tiles, tile_cols, False))),
        name="outer",
    )
    combine = pl.pallas_call(
        combine_kernel,
        out_shape=(shape((dense,) + block, f32), shape((dense,) + block, bf16)),
        in_specs=[ANY, VMEM],
        out_specs=(VMEM, VMEM),
        scratch_shapes=[pltpu.VMEM((dense + 1,) + block, f32)] * 2 + scalars(slots),
        compiler_params=limit(8),
        name="combine",
    )
    reply = pl.pallas_call(
        reply_kernel,
        out_shape=slot_out,
        in_specs=[ANY] * 2 + [VMEM] * 4,
        out_specs=VMEM,
        scratch_shapes=[
            pltpu.VMEM((dense + 1,) + block, bf16),
            pltpu.SMEM((slots,), i32),
            pltpu.SMEM((dense + 1,), i32),
            pltpu.SemaphoreType.DMA((2,)),
        ],
        compiler_params=limit(8),
        name="reply",
    )

    def finish(last):
        return pl.pallas_call(
            functools.partial(finish_kernel, tile_cols=tile_cols, last=last),
            out_shape=(shape(state.shape, f32),) if last else edges,
            in_specs=[SMEM] + [VMEM] * 5,
            out_specs=(pl.BlockSpec(memory_space=pl.ANY),) if last else (VMEM,) * 5,
            scratch_shapes=[
                pltpu.VMEM(state.shape, f32),
                pltpu.SemaphoreType.DMA((tiles,)),
            ],
            compiler_params=limit(20),
            name="finish",
        )

    def across(value):
        value = value.reshape((peers, cap) + block)
        value = lax.all_to_all(value, GROUP, split_axis=0, concat_axis=0, tiled=True)
        return value.reshape((slots,) + block)

    def swaps(value_a, value_b, axis):
        count = lax.axis_size(axis)
        even = [(i, i ^ 1) for i in range(count)]
        uneven = [(i, ((i + 1) ^ 1) - 1) for i in range(1, count - 1)]
        return lax.ppermute(value_a, axis, even), lax.ppermute(value_b, axis, uneven)

    def apart(value):
        return pltpu.with_memory_space_constraint(value, pltpu.HBM)

    def forward(early, scaled, row_a, row_b, col_a, col_b):
        above = swaps(row_a, row_b, "row")
        side_a, side_b = sides(*above, col_a, col_b)
        other_weight = None
        if early:
            side_b, weight = lax.optimization_barrier((side_b, ray_weight.astype(bf16)))
            other_weight = exchange(weight)
        beside = swaps(side_a, side_b, COL)
        *parts, taps = inner(routes, scaled, *above, kernel, rays)
        pulled, outgoing, _ = outer(routes, *beside, taps, rays, *parts)
        return pulled, outgoing, other_weight

    scaled, *rim = start(apart(state), apart(grad))
    for turn in range(ITERS):
        pulled, outgoing, swapped = forward(turn == 0, scaled, *rim)
        if not turn:
            other_weight = swapped
            outgoing, table, used, other_weight = lax.optimization_barrier(
                (outgoing, table, used, other_weight)
            )
        total, mine = combine(table, across(outgoing))
        replies = reply(table, used, total, exchange(mine), ray_weight, other_weight)
        last = turn == ITERS - 1
        scaled, *rim = finish(last)(
            routes, across(replies), pulled, grad, state, rays
        )
    return scaled


def solution(mesh):
    nr, nc = mesh.devices.shape
    fine = Mesh(mesh.devices.reshape(nr, 2, RING // 2, nc // RING), ("row",) + COL)
    image = P("row", COL, None)
    placed = (
        image,
        image,
        P(),
        P(),
        P(("row",) + COL, None, None),
        P(),
        image,
        P(),
        P(),
    )
    return jax.shard_map(
        on_device, mesh=fine, in_specs=placed, out_specs=image, check_vma=False
    )
```

```python
import functools

import jax
import jax.numpy as jnp
from jax import lax
from jax.experimental import pallas as pl
from jax.experimental.pallas import tpu as pltpu
from jax.sharding import Mesh, PartitionSpec as P

PIX = 32
ANGLES = 8
HITS = 16
ITERS = 2
RING = 4

relax_rate = 0.25

COL = ("zh", "zl", "x")
GROUP = ("row", "zl", "x")

VMEM = pl.BlockSpec(memory_space=pltpu.VMEM)
SMEM = pl.BlockSpec(memory_space=pltpu.SMEM)
ANY = pl.BlockSpec(memory_space=pl.ANY)


def start_kernel(state, grad, scaled, row_a, row_b, col_a, col_b, states, grads, whole, mark):
    parts = mark.shape[1]
    rows = states.shape[0] // parts

    def load(a, p):
        source, held = ((state, states), (grad, grads))[a]
        where = pl.ds(p * rows, rows)
        return pltpu.make_async_copy(source.at[where], held.at[where], mark.at[a, p])

    for p in range(parts):
        for a in range(2):
            load(a, p).start()
    for p in range(parts):
        for a in range(2):
            load(a, p).wait()
        where = slice(p * rows, (p + 1) * rows)
        value = states[where].astype(jnp.float32)
        value = (1.0 - value * value) * grads[where].astype(jnp.float32)
        whole[where] = value
        scaled[where] = value.astype(jnp.bfloat16)
    emit_edges(whole, row_a, row_b, col_a, col_b)


def bring(source, held, mark):
    copy = pltpu.make_async_copy(source, held, mark)
    copy.start()
    return copy


def parity(dim):
    if dim == 0:
        return lax.axis_index("row") % 2
    return (lax.axis_index("zl") * lax.axis_size("x") + lax.axis_index("x")) % 2


def pick(dim, yes, no):
    return jnp.where(parity(dim) == 1, yes, no)


def emit_edges(value, row_a, row_b, col_a, col_b):
    rows, cols = value.shape[:2]
    row_a[...] = pick(0, value[0], value[rows - 1]).astype(jnp.bfloat16)
    row_b[...] = pick(0, value[rows - 1], value[0]).astype(jnp.bfloat16)
    left, right = value[:, 0, :], value[:, cols - 1, :]
    col_a[...] = pick(1, left, right)
    col_b[...] = pick(1, right, left)


def sides_kernel(near_a, near_b, col_a, col_b, out_a, out_b):
    rows = col_a.shape[0]
    cols = near_a.shape[0]
    f32 = jnp.float32

    def ends(ref):
        low = ref[0:16, :].astype(f32)[0:1, :]
        high = ref[cols - 16 : cols, :].astype(f32)[15:16, :]
        return low, high

    a, b = ends(near_a), ends(near_b)
    above = [pick(0, a[i], b[i]) for i in range(2)]
    below = [pick(0, b[i], a[i]) for i in range(2)]
    for out, edge, order in ((out_a, col_a, (0, 1)), (out_b, col_b, (1, 0))):
        yes, no = order
        out[8 : 8 + rows, :] = edge[...]
        out[7:8, :] = pick(1, above[yes], above[no])
        out[8 + rows : 9 + rows, :] = pick(1, below[yes], below[no])


def matrices_of(routes, rays, t):
    return jnp.concatenate([rays[routes[t * HITS + k]] for k in range(HITS)], axis=0)


def forward_tile(routes, taps, rays, pulled, out, cols3, t, tile_cols):
    chans = pulled.shape[-1]
    bins = rays.shape[1]
    slot = pulled.shape[0] * HITS
    half = PIX // 2
    r0, c0 = t // tile_cols * half, t % tile_cols * PIX
    window = jnp.concatenate(
        [
            cols3[r0 + dr // 2 : r0 + dr // 2 + half, dr % 2, c0 : c0 + PIX, :].reshape(
                half * PIX, 3 * chans
            )
            for dr in range(4)
        ],
        axis=1,
    )
    acc = jnp.dot(window, taps[...], preferred_element_type=jnp.float32)
    for odd in range(2):
        value = acc[:, odd * chans : (odd + 1) * chans].reshape(half, PIX, chans)
        pulled[t, :, odd] = value
    low = pulled[t].reshape(PIX * PIX, chans).astype(jnp.bfloat16)
    value = jnp.dot(
        matrices_of(routes, rays, t), low, preferred_element_type=jnp.float32
    ).astype(jnp.bfloat16)
    for k in range(HITS):
        out[routes[slot + t * HITS + k]] = value[k * bins : (k + 1) * bins, :]


def tiles_at(tiles, tile_cols, inner):
    return [t for t in range(tiles) if (0 < t % tile_cols < tile_cols - 1) == inner]


def inner_kernel(
    source, scaled, near_a, near_b, kernel, rays,
    pulled, out, cols3, taps, wide, routes, mark, *, tile_cols,
):
    coming = bring(source, routes, mark)
    rows, cols, chans = scaled.shape
    f32, bf16 = jnp.float32, jnp.bfloat16
    blank = jnp.zeros((3 * chans, chans), bf16)
    for dr in range(4):
        base = dr * 3 * chans
        for side in range(2):
            lanes = slice(side * chans, (side + 1) * chans)
            tap = dr - side
            if not 0 <= tap < 3:
                taps[base : base + 3 * chans, lanes] = blank
                continue
            for dc in range(3):
                taps[base + dc * chans : base + (dc + 1) * chans, lanes] = kernel[2 - tap, 2 - dc].T
    a, b = near_a[...].astype(f32), near_b[...].astype(f32)
    wide[0, 8 : 8 + cols, :] = pick(0, a, b)
    wide[rows + 1, 8 : 8 + cols, :] = pick(0, b, a)
    wide[1 : rows + 1, 8 : 8 + cols, :] = scaled[...].astype(f32)
    wide[:, 0:8, :] = jnp.zeros((rows + 2, 8, chans), f32)
    wide[:, 8 + cols :, :] = jnp.zeros((rows + 2, 8, chans), f32)
    for dc in (0, 2):
        value = wide[:, 7 + dc : 7 + dc + cols, :].astype(bf16)
        cols3[:, :, :, dc * chans : (dc + 1) * chans] = value.reshape(
            (rows + 2) // 2, 2, cols, chans
        )
    middle = slice(chans, 2 * chans)
    cols3[0, 0, :, middle] = pick(0, a, b).astype(bf16)
    cols3[(rows + 1) // 2, (rows + 1) % 2, :, middle] = pick(0, b, a).astype(bf16)
    for r in range(1, rows + 1):
        cols3[r // 2, r % 2, :, middle] = scaled[r - 1]
    coming.wait()
    for t in tiles_at(pulled.shape[0], tile_cols, True):
        forward_tile(routes, taps, rays, pulled, out, cols3, t, tile_cols)


def outer_kernel(
    source, near_a, near_b, taps, rays, _pulled, _out, _cols3,
    pulled, out, cols3, routes, mark, *, tile_cols,
):
    coming = bring(source, routes, mark)
    cols = cols3.shape[2]
    chans = pulled.shape[-1]
    group = 16
    spot = lax.broadcasted_iota(jnp.int32, (group, chans), 0)
    a, b = near_a[...], near_b[...]
    left, right = pick(1, a, b), pick(1, b, a)
    for edge, dc, first, at in ((left, 0, 0, 0), (right, 2, cols - group, group - 1)):
        lanes = slice(dc * chans, (dc + 1) * chans)
        for r in range(2 * cols3.shape[0]):
            there = (r // 2, r % 2, slice(first, first + group), lanes)
            value = jnp.where(spot == at, edge[7 + r : 8 + r, :], cols3[there].astype(jnp.float32))
            cols3[there] = value.astype(jnp.bfloat16)
    coming.wait()
    for t in tiles_at(pulled.shape[0], tile_cols, False):
        forward_tile(routes, taps, rays, pulled, out, cols3, t, tile_cols)


def combine_kernel(source, recv, total, low, acc_a, acc_b, table, mark):
    coming = bring(source, table, mark)
    acc_a[...] = jnp.zeros_like(acc_a)
    acc_b[...] = jnp.zeros_like(acc_b)
    coming.wait()

    def body(j, carry):
        acc_a[table[2 * j]] += recv[2 * j].astype(jnp.float32)
        acc_b[table[2 * j + 1]] += recv[2 * j + 1].astype(jnp.float32)
        return carry

    lax.fori_loop(0, recv.shape[0] // 2, body, 0, unroll=4)
    n = total.shape[0]
    value = acc_a[:n] + acc_b[:n]
    total[...] = value
    low[...] = value.astype(jnp.bfloat16)


def reply_kernel(
    source, flags, total, other, own_weight, other_weight, out, held, table, used, mark
):
    coming = [bring(source, table, mark.at[0]), bring(flags, used, mark.at[1])]
    n = total.shape[0]
    own = own_weight.shape[0]
    place = lax.axis_index("zh") * own
    for half, weight in enumerate((own_weight, other_weight)):
        first = place if half == 0 else n - own - place
        for b in range(own):
            d = first + b
            value = total[d] + other[d].astype(jnp.float32)
            held[d] = (weight[b].astype(jnp.float32) * value).astype(jnp.bfloat16)
    held[n] = jnp.zeros(held.shape[1:], jnp.bfloat16)
    for copy in coming:
        copy.wait()

    def body(j, carry):
        d = table[j]
        out[j] = held[jnp.where(used[d] == 1, d, n)]
        return carry

    lax.fori_loop(0, out.shape[0], body, 0, unroll=8)


def finish_kernel(
    routes, returned, pulled, grad, state, rays, *refs, tile_cols, last,
):
    outs, (whole, mark) = refs[:-2], refs[-2:]
    tiles = pulled.shape[0]
    slot = tiles * HITS
    chans = grad.shape[2]
    f32 = jnp.float32

    def place(t):
        r0, c0 = t // tile_cols * PIX, t % tile_cols * PIX
        return slice(r0, r0 + PIX), slice(c0, c0 + PIX)

    def leave(t):
        where = place(t)
        return pltpu.make_async_copy(whole.at[where], outs[0].at[where], mark.at[t])

    for t in range(tiles):
        picked = jnp.concatenate([returned[routes[slot + t * HITS + k]] for k in range(HITS)], axis=0)
        backed = lax.dot_general(
            picked,
            matrices_of(routes, rays, t),
            (((0,), (0,)), ((), ())),
            preferred_element_type=f32,
        ).T
        change = pulled[t].reshape(backed.shape) - relax_rate * backed
        where = place(t)
        adjoint = grad[where].astype(f32) + change.reshape(PIX, PIX, chans)
        if last:
            whole[where] = adjoint
            leave(t).start()
        else:
            value = state[where].astype(f32)
            value = (1.0 - value * value) * adjoint
            whole[where] = value
            outs[0][where] = value.astype(jnp.bfloat16)
    if last:
        for t in range(tiles):
            leave(t).wait()
    else:
        emit_edges(whole, *outs[1:])


def on_device(state, grad, kernel, ray_matrix, ray_weight, hits, offsets, block_slot, angle_count):
    f32, bf16, i32 = jnp.float32, jnp.bfloat16, jnp.int32
    rows_dev, cols_dev, chans = state.shape
    angles, spots, bins, tile_pix = ray_matrix.shape
    nr = lax.axis_size("row")
    nx = lax.axis_size("x")
    nc = lax.axis_size(COL)
    devices = nr * nc
    row, zh, zl, x = (lax.axis_index(a) for a in ("row",) + COL)
    tile_rows = rows_dev // PIX
    tile_cols = cols_dev // PIX
    tiles = tile_rows * tile_cols
    pairs = tiles * HITS
    blk_dev = ray_weight.shape[0]
    blocks = blk_dev * devices
    blk_ang = blocks // ANGLES
    cap = 2 * max(2, (pairs + devices - 2) // devices + 1)
    cap = min(cap, pairs)
    peers = nr * 2 * nx
    slots = peers * cap
    dense = 2 * blk_dev

    def exchange(value):
        return lax.ppermute(value, "zh", [(0, 1), (1, 0)])

    everyone = hits.reshape(nr, tile_rows, nc, tile_cols, HITS).transpose(0, 2, 1, 3, 4)
    everyone = everyone.reshape(nr, 2, 2, nx, pairs)
    group = lax.dynamic_index_in_dim(everyone, zh, 1, keepdims=False).reshape(peers, pairs)
    storage = jnp.sum(
        jnp.where(group[:, :, None] == jnp.arange(blocks, dtype=i32), block_slot, 0), axis=2
    )
    owner = storage // blk_dev
    local = storage % blk_dev
    owner_z = (owner % nc) // nx
    owner_zh = owner_z // 2
    owner_zl = owner_z % 2
    peer = ((owner // nc) * 2 + owner_zl) * nx + owner % nx
    place = owner_zh * blk_dev + local
    earlier = jnp.arange(pairs)[None, :] < jnp.arange(pairs)[:, None]
    ranking = jnp.sum(
        ((peer[:, :, None] == peer[:, None, :]) & earlier[None]).astype(i32), axis=2
    )
    me = (row * 2 + zl) * nx + x
    my_hits = lax.dynamic_index_in_dim(group, me, 0, keepdims=False)
    send_slot = lax.dynamic_index_in_dim(peer * cap + ranking, me, 0, keepdims=False)
    matched = (peer[:, None, :] == me) & (
        ranking[:, None, :] == jnp.arange(cap, dtype=i32)[None, :, None]
    )
    table = dense + jnp.sum(jnp.where(matched, place[:, None, :] - dense, 0), axis=2)
    table = table.reshape(slots)
    mat_idx = (my_hits // blk_ang) * spots + offsets.reshape(pairs)
    routes = jnp.concatenate([mat_idx, send_slot])

    dense_z = jnp.arange(dense, dtype=i32) // blk_dev * 2 + zl
    dense_place = (row * nc + dense_z * nx + x) * blk_dev + jnp.arange(dense, dtype=i32) % blk_dev
    number = jnp.arange(blocks, dtype=i32)
    active = (
        (number % blk_ang).reshape(ANGLES, blk_ang) < angle_count[:, None]
    ).reshape(1, blocks)
    used = jnp.any((block_slot[None, :] == dense_place[:, None]) & active, axis=1).astype(i32)
    used = jnp.concatenate([used, jnp.zeros((1,), i32)])

    rays = ray_matrix.reshape(angles * spots, bins, tile_pix)

    block = (bins, chans)
    shape = jax.ShapeDtypeStruct
    slot_out = shape((slots,) + block, bf16)
    edges = (
        shape(state.shape, bf16),
        shape((cols_dev, chans), bf16),
        shape((cols_dev, chans), bf16),
        shape((rows_dev, chans), f32),
        shape((rows_dev, chans), f32),
    )

    def scalars(count):
        return [pltpu.SMEM((count,), i32), pltpu.SemaphoreType.DMA]

    def limit(mib):
        return pltpu.CompilerParams(vmem_limit_bytes=mib << 20)

    start = pl.pallas_call(
        start_kernel,
        out_shape=edges,
        in_specs=[ANY] * 2,
        out_specs=(VMEM,) * 5,
        scratch_shapes=[
            pltpu.VMEM(state.shape, bf16),
            pltpu.VMEM(state.shape, bf16),
            pltpu.VMEM(state.shape, f32),
            pltpu.SemaphoreType.DMA((2, 4)),
        ],
        compiler_params=limit(8),
        name="start",
    )
    sides = pl.pallas_call(
        sides_kernel,
        out_shape=[shape((rows_dev + 16, chans), f32)] * 2,
        in_specs=[VMEM] * 4,
        out_specs=[VMEM] * 2,
        compiler_params=limit(4),
        cost_estimate=pl.CostEstimate(
            flops=4 * rays.size * 512, bytes_accessed=rays.size * 2, transcendentals=0
        ),
        name="sides",
    )
    pulled_out = shape((tiles, PIX // 2, 2, PIX, chans), f32)
    cols3_out = shape(((rows_dev + 2) // 2, 2, cols_dev, 3 * chans), bf16)
    macs = tiles * tile_pix * chans * (9 * chans + HITS * bins)

    def cost(share):
        return pl.CostEstimate(
            flops=2 * macs * share // tiles, bytes_accessed=rays.size * 2, transcendentals=0
        )

    taps_out = shape((4 * 3 * chans, 2 * chans), bf16)

    inner = pl.pallas_call(
        functools.partial(inner_kernel, tile_cols=tile_cols),
        out_shape=(pulled_out, slot_out, cols3_out, taps_out),
        in_specs=[ANY] + [VMEM] * 5,
        out_specs=(VMEM,) * 4,
        scratch_shapes=[pltpu.VMEM((rows_dev + 2, cols_dev + 16, chans), f32)] + scalars(2 * pairs),
        compiler_params=limit(16),
        cost_estimate=cost(len(tiles_at(tiles, tile_cols, True))),
        name="inner",
    )
    outer = pl.pallas_call(
        functools.partial(outer_kernel, tile_cols=tile_cols),
        out_shape=(pulled_out, slot_out, cols3_out),
        in_specs=[ANY] + [VMEM] * 7,
        out_specs=(VMEM,) * 3,
        scratch_shapes=scalars(2 * pairs),
        input_output_aliases={5: 0, 6: 1, 7: 2},
        compiler_params=limit(16),
        cost_estimate=cost(len(tiles_at(tiles, tile_cols, False))),
        name="outer",
    )
    combine = pl.pallas_call(
        combine_kernel,
        out_shape=(shape((dense,) + block, f32), shape((dense,) + block, bf16)),
        in_specs=[ANY, VMEM],
        out_specs=(VMEM, VMEM),
        scratch_shapes=[pltpu.VMEM((dense + 1,) + block, f32)] * 2 + scalars(slots),
        compiler_params=limit(8),
        name="combine",
    )
    reply = pl.pallas_call(
        reply_kernel,
        out_shape=slot_out,
        in_specs=[ANY] * 2 + [VMEM] * 4,
        out_specs=VMEM,
        scratch_shapes=[
            pltpu.VMEM((dense + 1,) + block, bf16),
            pltpu.SMEM((slots,), i32),
            pltpu.SMEM((dense + 1,), i32),
            pltpu.SemaphoreType.DMA((2,)),
        ],
        compiler_params=limit(8),
        name="reply",
    )

    def finish(last):
        return pl.pallas_call(
            functools.partial(finish_kernel, tile_cols=tile_cols, last=last),
            out_shape=(shape(state.shape, f32),) if last else edges,
            in_specs=[SMEM] + [VMEM] * 5,
            out_specs=(pl.BlockSpec(memory_space=pl.ANY),) if last else (VMEM,) * 5,
            scratch_shapes=[
                pltpu.VMEM(state.shape, f32),
                pltpu.SemaphoreType.DMA((tiles,)),
            ],
            compiler_params=limit(20),
            name="finish",
        )

    def across(value):
        value = value.reshape((peers, cap) + block)
        value = lax.all_to_all(value, GROUP, split_axis=0, concat_axis=0, tiled=True)
        return value.reshape((slots,) + block)

    def swaps(value_a, value_b, axis):
        count = lax.axis_size(axis)
        even = [(i, i ^ 1) for i in range(count)]
        uneven = [(i, ((i + 1) ^ 1) - 1) for i in range(1, count - 1)]
        return lax.ppermute(value_a, axis, even), lax.ppermute(value_b, axis, uneven)

    def apart(value):
        return pltpu.with_memory_space_constraint(value, pltpu.HBM)

    def forward(early, scaled, row_a, row_b, col_a, col_b):
        above = swaps(row_a, row_b, "row")
        side_a, side_b = sides(*above, col_a, col_b)
        other_weight = None
        if early:
            side_b, weight = lax.optimization_barrier((side_b, ray_weight.astype(bf16)))
            other_weight = exchange(weight)
        beside = swaps(side_a, side_b, COL)
        *parts, taps = inner(routes, scaled, *above, kernel, rays)
        pulled, outgoing, _ = outer(routes, *beside, taps, rays, *parts)
        return pulled, outgoing, other_weight

    scaled, *rim = start(apart(state), apart(grad))
    for turn in range(ITERS):
        pulled, outgoing, swapped = forward(turn == 0, scaled, *rim)
        if not turn:
            other_weight = swapped
            outgoing, table, used, other_weight = lax.optimization_barrier(
                (outgoing, table, used, other_weight)
            )
        total, mine = combine(table, across(outgoing))
        replies = reply(table, used, total, exchange(mine), ray_weight, other_weight)
        last = turn == ITERS - 1
        scaled, *rim = finish(last)(
            routes, across(replies), pulled, grad, state, rays
        )
    return scaled


def solution(mesh):
    nr, nc = mesh.devices.shape
    fine = Mesh(mesh.devices.reshape(nr, 2, RING // 2, nc // RING), ("row",) + COL)
    image = P("row", COL, None)
    placed = (
        image,
        image,
        P(),
        P(),
        P(("row",) + COL, None, None),
        P(),
        image,
        P(),
        P(),
    )
    return jax.shard_map(
        on_device, mesh=fine, in_specs=placed, out_specs=image, check_vma=False
    )
```
